32 devices in a mesh: batch: 8 (over z, y), seq: 4 (over x, core).
Axes of the slice: x: 2, y: 2, z: 4, core: 2. Of those that a mesh axis runs over, the one named last changes fastest.
Arguments:
- encoder_layer_input: bfloat16 [8, 1024, 768], P('batch', 'seq'), may hold values from -6 to 6
- decoder_layer_input: bfloat16 [8, 512, 768], P('batch', 'seq'), may hold values from -6 to 6
- cotangent: bfloat16 [8, 512, 768], P('batch', 'seq'), may hold values from -6 to 6
- encoder_used_lengths: int32 [8], P('batch'), may hold values from 512 to 1024, as said below
- decoder_used_lengths: int32 [8], P('batch'), may hold values from 128 to 512, as said below
- attn_master: float32 [9216, 768], P(('batch', 'seq'))
- inner_master: float32 [3072, 2048], P(('batch', 'seq')), may hold values from -0.21875 to 0.21875
- outer_master: float32 [4096, 768], P(('batch', 'seq')), may hold values from -0.125 to 0.125
- gain_master: float32 [4608], P(('batch', 'seq')), may hold values from 0.5 to 1.5
- attn_first: float32 [9216, 768], P(('batch', 'seq')), may hold values from -512 to 512
- inner_first: float32 [3072, 2048], P(('batch', 'seq')), may hold values from -512 to 512
- outer_first: float32 [4096, 768], P(('batch', 'seq')), may hold values from -512 to 512
- gain_first: float32 [4608], P(('batch', 'seq')), may hold values from -512 to 512
- attn_second: float32 [9216, 768], P(('batch', 'seq')), may hold values from 8192 to 32768
- inner_second: float32 [3072, 2048], P(('batch', 'seq')), may hold values from 8192 to 32768
- outer_second: float32 [4096, 768], P(('batch', 'seq')), may hold values from 8192 to 32768
- gain_second: float32 [4608], P(('batch', 'seq')), may hold values from 8192 to 32768
Outputs:
- decoder_layer_output: bfloat16 [8, 512, 768], P('batch', 'seq')
- encoder_input_gradient: float32 [8, 1024, 768], P('batch', 'seq')
- decoder_input_gradient: float32 [8, 512, 768], P('batch', 'seq')
- attn_grad: float32 [9216, 768], P(('batch', 'seq'))
- inner_grad: float32 [3072, 2048], P(('batch', 'seq'))
- outer_grad: float32 [4096, 768], P(('batch', 'seq'))
- gain_grad: float32 [4608], P(('batch', 'seq'))
- attn_first_new: float32 [9216, 768], P(('batch', 'seq'))
- inner_first_new: float32 [3072, 2048], P(('batch', 'seq'))
- outer_first_new: float32 [4096, 768], P(('batch', 'seq'))
- gain_first_new: float32 [4608], P(('batch', 'seq'))
- attn_second_new: float32 [9216, 768], P(('batch', 'seq'))
- inner_second_new: float32 [3072, 2048], P(('batch', 'seq'))
- outer_second_new: float32 [4096, 768], P(('batch', 'seq'))
- gain_second_new: float32 [4608], P(('batch', 'seq'))
- attn_new: float32 [9216, 768], P(('batch', 'seq'))
- inner_new: float32 [3072, 2048], P(('batch', 'seq'))
- outer_new: float32 [4096, 768], P(('batch', 'seq'))
- gain_new: float32 [4608], P(('batch', 'seq'))
- attn_copy: bfloat16 [9216, 768], P(('batch', 'seq'))
- inner_copy: bfloat16 [3072, 2048], P(('batch', 'seq'))
- outer_copy: bfloat16 [4096, 768], P(('batch', 'seq'))
- gain_copy: bfloat16 [4608], P(('batch', 'seq'))
- weight_norms: float32 [24], replicated
- update_norms: float32 [24], replicated
The draws below stay inside these ranges and needn't reach their ends.
Inputs may be any that keep to these rules, and one draw needn't show every extreme that they name: `encoder_used_lengths`: some sequence uses all 1024 encoder positions. `decoder_used_lengths`: some sequence uses all 512 decoder positions.
All inputs are finite; a program needn't handle non-finite values.
Results may differ from the reference program's by a relative error of at most 0.019.
Values may be sent and summed in bfloat16 or wider, within the bound.
No kernel may reach another device: no remote copies, remote signals or barrier semaphores. Data moves between devices by JAX's collectives and lax.ppermute only.
A program may use at most 384 MiB of HBM per device.

```python
import math
import jax
import jax.numpy as jnp
from jax import lax

D = 768
HEADS = 12
HEAD = 64
FF = 2048
STEP = 5
SEQS = 8
ENC_LEN = 1024
DEC_LEN = 512
TOKENS = 8192


def draw_attn_master(key, part):
    normal_draw = jnp.clip(jax.random.normal(key, (12 * D, D), jnp.float32), -5.0, 5.0)
    matrix_kind = jnp.arange(12 * D, dtype=jnp.int32) // D % 4
    factor = jnp.where(matrix_kind == 3, 8.0, 1.0) * D ** (-0.5)
    return normal_draw * factor[:, None]


def draw_lengths(key, lowest, highest):
    first_key, second_key = jax.random.split(key)
    drawn = jax.random.randint(first_key, (SEQS,), lowest, highest + 1)
    place = jax.random.randint(second_key, (), 0, SEQS)
    return jnp.where(jnp.arange(SEQS, dtype=jnp.int32) == place, highest, drawn).astype(jnp.int32)


def draw_encoder_used_lengths(key, part):
    return draw_lengths(jax.random.fold_in(key, 11), ENC_LEN // 2, ENC_LEN)


def draw_decoder_used_lengths(key, part):
    return draw_lengths(jax.random.fold_in(key, 23), DEC_LEN // 4, DEC_LEN)


def level_of(own_key, extent, cuts, low, top_value):
    loudness, own = 1.0, jax.random.fold_in(own_key, 6)
    for axis_at, shards_of in cuts:
        heights = jnp.exp(jax.random.uniform(jax.random.fold_in(own, axis_at), (shards_of,), jnp.float32, low / len(cuts), top_value / len(cuts)))
        loudness = loudness * jnp.repeat(heights, extent[axis_at] // shards_of).reshape([-1 if axis == axis_at else 1 for axis in range(len(extent))])
    return loudness


def scatter_about(stream_key, shape, spread, bound, pieces=(), kind=jnp.bfloat16):
    values = spread * jax.random.normal(stream_key, shape, jnp.float32)
    if pieces:
        values = values * level_of(stream_key, shape, pieces, -0.22, 0.18)
    return jnp.clip(values, -bound, bound).astype(kind)


def setup_inputs(seed: int = 0) -> dict:
    key_of = jax.random.split(jax.random.key(seed), 18)
    return {
        "encoder_layer_input": scatter_about(key_of[0], (SEQS, ENC_LEN, D), 1.0, 6.0, ((0, 8), (1, 4))),
        "decoder_layer_input": scatter_about(key_of[1], (SEQS, DEC_LEN, D), 1.0, 6.0, ((0, 8), (1, 4))),
        "cotangent": scatter_about(key_of[2], (SEQS, DEC_LEN, D), 1.0, 6.0, ((0, 8), (1, 4))),
        "encoder_used_lengths": draw_encoder_used_lengths(jax.random.fold_in(key_of[17], 71), 0),
        "decoder_used_lengths": draw_decoder_used_lengths(jax.random.fold_in(key_of[17], 71), 0),
        "attn_master": draw_attn_master(jax.random.fold_in(key_of[17], 71), 0),
        "inner_master": scatter_about(key_of[6], (4 * D, FF), D ** -0.5, 0.21875, ((0, 32),), jnp.float32),
        "outer_master": scatter_about(key_of[7], (2 * FF, D), FF ** -0.5, 0.125, ((0, 32),), jnp.float32),
        "gain_master": jnp.clip(1.0 + 0.1 * jax.random.normal(key_of[8], (6 * D,), jnp.float32), 0.5, 1.5),
        "attn_first": scatter_about(key_of[9], (12 * D, D), (TOKENS ** 0.5), 512.0, ((0, 32),), jnp.float32),
        "inner_first": scatter_about(key_of[10], (4 * D, FF), (TOKENS ** 0.5), 512.0, ((0, 32),), jnp.float32),
        "outer_first": scatter_about(key_of[11], (2 * FF, D), (TOKENS ** 0.5), 512.0, ((0, 32),), jnp.float32),
        "gain_first": scatter_about(key_of[12], (6 * D,), (TOKENS ** 0.5), 512.0, ((0, 32),), jnp.float32),
        "attn_second": jnp.clip(jnp.exp(math.log(32768.0) - 1.3862944 * jax.random.uniform(key_of[13], (12 * D, D), jnp.float32) ** level_of(key_of[13], (12 * D, D), ((0, 32),), -0.2, 0.2)), 8192.0, 32768.0),
        "inner_second": jnp.clip(jnp.exp(math.log(32768.0) - 1.3862944 * jax.random.uniform(key_of[14], (4 * D, FF), jnp.float32) ** level_of(key_of[14], (4 * D, FF), ((0, 32),), -0.2, 0.2)), 8192.0, 32768.0),
        "outer_second": jnp.clip(jnp.exp(math.log(32768.0) - 1.3862944 * jax.random.uniform(key_of[15], (2 * FF, D), jnp.float32) ** level_of(key_of[15], (2 * FF, D), ((0, 32),), -0.2, 0.2)), 8192.0, 32768.0),
        "gain_second": jnp.clip(jnp.exp(math.log(32768.0) - 1.3862944 * jax.random.uniform(key_of[16], (6 * D,), jnp.float32) ** level_of(key_of[16], (6 * D,), ((0, 32),), -0.2, 0.2)), 8192.0, 32768.0),
    }


eps_norm = 1e-06
adam_eps = 1e-06
lamb_rate = 0.5
decay_weight = 0.01

@jax.custom_vjp
def low(v):
    return lax.optimization_barrier(v.astype(jnp.bfloat16)).astype(jnp.float32)

@jax.custom_vjp
def low_back(v):
    return v

def low_keep(v):
    return (low(v), None)

def low_pass(kept, grad):
    return (grad,)

def back_keep(v):
    return (v, None)

def back_low(kept, grad):
    return (low(grad),)
low.defvjp(low_keep, low_pass)
low_back.defvjp(back_keep, back_low)

def both_round(value):
    return low_back(low(value))

def matmul(left_operand, right_operand):
    return jnp.dot(left_operand, right_operand, precision=lax.Precision.HIGHEST)

def rms_scale(values, gain_row):
    inverse = lax.rsqrt(lax.optimization_barrier(jnp.mean(values * values, axis=-1, keepdims=True)) + eps_norm)
    return values * inverse * gain_row

def attend(query_in, source_in, attn_stack, base, allowed):
    length_q = query_in.shape[0]
    length_k = source_in.shape[0]
    queries = both_round(matmul(query_in, attn_stack[base])).reshape(length_q, HEADS, HEAD)
    keys_all = both_round(matmul(source_in, attn_stack[base + 1])).reshape(length_k, HEADS, HEAD)
    values_all = both_round(matmul(source_in, attn_stack[base + 2])).reshape(length_k, HEADS, HEAD)
    scores = low_back(jnp.einsum('qhd,khd->hqk', queries, keys_all, precision=lax.Precision.HIGHEST) * 0.125)
    scores = jnp.where(allowed[None], scores, -1000000000.0)
    probs = jax.nn.softmax(scores, axis=-1)
    mixed = jnp.einsum('hqk,khd->qhd', low(probs), values_all, precision=lax.Precision.HIGHEST)
    mixed = both_round(mixed.reshape(length_q, D))
    return low_back(matmul(mixed, attn_stack[base + 3]))

def feed_forward(normed, gate_w, up_w, down_w):
    gate = low_back(matmul(normed, gate_w))
    upper = low_back(matmul(normed, up_w))
    hidden = low(jax.nn.gelu(gate, approximate=True) * upper)
    return low_back(matmul(hidden, down_w))

def sequence_forward(weight_set, enc_state, dec_state, enc_length, dec_length):
    attn_stack, inner_stack, outer_stack, gain_stack = weight_set
    enc_pos = jnp.arange(ENC_LEN, dtype=jnp.int32)
    dec_pos = jnp.arange(DEC_LEN, dtype=jnp.int32)
    enc_allowed = jnp.broadcast_to((enc_pos < enc_length)[None, :], (ENC_LEN, ENC_LEN))
    self_allowed = (dec_pos[None, :] <= dec_pos[:, None]) & (dec_pos[None, :] < dec_length)
    cross_allowed = jnp.broadcast_to((enc_pos < enc_length)[None, :], (DEC_LEN, ENC_LEN))
    normed = low(rms_scale(enc_state, gain_stack[0]))
    hidden = enc_state + attend(normed, normed, attn_stack, 0, enc_allowed)
    normed = low(rms_scale(hidden, gain_stack[1]))
    hidden = hidden + feed_forward(normed, inner_stack[0], inner_stack[1], outer_stack[0])
    encoded = low(rms_scale(hidden, gain_stack[2]))
    normed = low(rms_scale(dec_state, gain_stack[3]))
    state = dec_state + attend(normed, normed, attn_stack, 4, self_allowed)
    normed = low(rms_scale(state, gain_stack[4]))
    state = state + attend(normed, encoded, attn_stack, 8, cross_allowed)
    normed = low(rms_scale(state, gain_stack[5]))
    return state + feed_forward(normed, inner_stack[2], inner_stack[3], outer_stack[1])

def reference(encoder_layer_input, decoder_layer_input, cotangent, encoder_used_lengths, decoder_used_lengths, attn_master, inner_master, outer_master, gain_master, attn_first, inner_first, outer_first, gain_first, attn_second, inner_second, outer_second, gain_second):
    parameter_tree = (attn_master.reshape(12, D, D), inner_master.reshape(4, D, FF), outer_master.reshape(2, FF, D), gain_master.reshape(6, D))

    def each_sequence_values(totals, inputs_row):
        enc_row, dec_row, cot_row, enc_length, dec_length = inputs_row

        def forward(weight_set, enc_state, dec_state):
            lowered = tuple((low(group_member) for group_member in weight_set))
            return sequence_forward(lowered, enc_state, dec_state, enc_length, dec_length)
        dec_state, pullback = jax.vjp(forward, parameter_tree, enc_row.astype(jnp.float32), dec_row.astype(jnp.float32))
        alive_rows = (jnp.arange(DEC_LEN, dtype=jnp.int32) < dec_length).astype(jnp.float32)[:, None]
        par_grads, encoder_input_gradient, decoder_input_gradient = pullback(cot_row.astype(jnp.float32) * alive_rows)
        totals = tuple((total_in + group_member for total_in, group_member in zip(totals, par_grads)))
        return (totals, (dec_state.astype(jnp.bfloat16), encoder_input_gradient, decoder_input_gradient))
    empty_entries = tuple((jnp.zeros(group_member.shape, jnp.float32) for group_member in parameter_tree))
    gradient_totals, (decoder_layer_output, encoder_input_gradient, decoder_input_gradient) = lax.scan(each_sequence_values, empty_entries, (encoder_layer_input, decoder_layer_input, cotangent, encoder_used_lengths, decoder_used_lengths))
    grads = (gradient_totals[0].reshape(12 * D, D), gradient_totals[1].reshape(4 * D, FF), gradient_totals[2].reshape(2 * FF, D), gradient_totals[3].reshape(6 * D))
    masters = (attn_master, inner_master, outer_master, gain_master)
    firsts = (attn_first, inner_first, outer_first, gain_first)
    seconds = (attn_second, inner_second, outer_second, gain_second)
    group_counts = (12, 4, 2, 6)
    decays = (decay_weight, decay_weight, decay_weight, 0.0)
    correction = 1.0 - 0.5 ** STEP
    first_list, second_list, master_list, copy_list, weight_list, update_list = ([], [], [], [], [], [])
    for master, first_old, second_old, gradient, groups_in, decay_rate in zip(masters, firsts, seconds, grads, group_counts, decays):
        first_new = 0.5 * first_old + 0.5 * gradient
        second_new = 0.5 * second_old + 0.5 * gradient * gradient
        update = first_new / correction / (jnp.sqrt(second_new / correction) + adam_eps) + decay_rate * master
        weight_sq = lax.optimization_barrier(jnp.sum((master * master).reshape(groups_in, -1), axis=1))
        update_sq = lax.optimization_barrier(jnp.sum((update * update).reshape(groups_in, -1), axis=1))
        trust_ratio = jnp.sqrt(weight_sq) / (jnp.sqrt(update_sq) + 1e-06)
        master_new = master - lamb_rate * (trust_ratio[:, None] * update.reshape(groups_in, -1)).reshape(master.shape)
        first_list.append(first_new)
        second_list.append(second_new)
        master_list.append(master_new)
        copy_list.append(master_new.astype(jnp.bfloat16))
        weight_list.append(jnp.sqrt(weight_sq))
        update_list.append(jnp.sqrt(update_sq))
    weight_norms = jnp.concatenate(weight_list)
    update_norms = jnp.concatenate(update_list)
    return (decoder_layer_output, encoder_input_gradient, decoder_input_gradient, grads[0], grads[1], grads[2], grads[3], first_list[0], first_list[1], first_list[2], first_list[3], second_list[0], second_list[1], second_list[2], second_list[3], master_list[0], master_list[1], master_list[2], master_list[3], copy_list[0], copy_list[1], copy_list[2], copy_list[3], weight_norms, update_norms)
```

```python
import jax
import jax.numpy as jnp
from jax import lax
from jax.sharding import PartitionSpec as P

D = 768
HEADS = 12
HEAD = 64
FF = 2048
STEP = 5

eps_norm = 1e-06
adam_eps = 1e-06
lamb_rate = 0.5
decay_weight = 0.01
masked_score = -1000000000.0

F32 = jnp.float32
BF16 = jnp.bfloat16


def seq_swap(x, k):
    n = lax.axis_size("seq")
    return lax.ppermute(x, "seq", [(i, i ^ k) for i in range(n)])


def batch_swap(x, k):
    n = lax.axis_size("batch")
    return lax.ppermute(x, "batch", [(i, i ^ k) for i in range(n)])


def batch_shift(x, k):
    n = lax.axis_size("batch")
    return lax.ppermute(x, "batch", [(i, (i + k) % n) for i in range(n)])


def seq_bits():
    bits, k = [], 1
    while k < lax.axis_size("seq"):
        bits.append(k)
        k *= 2
    return bits


def row_order():
    order = [0]
    for k in reversed(seq_bits()):
        order = order + [o ^ k for o in order]
    return order


def gather_rows(x):
    for k in reversed(seq_bits()):
        x = jnp.concatenate([x, seq_swap(x, k)], axis=0)
    return x


def scatter_rows(partial):
    for k in seq_bits():
        half = partial.shape[0] // 2
        partial = partial[:half] + seq_swap(partial[half:].astype(BF16), k).astype(F32)
    return partial


def xor_blocks(x, s):
    n = x.shape[0]
    for k in seq_bits():
        swapped = jnp.stack([x[j ^ k] for j in range(n)])
        x = jnp.where((s & k) != 0, swapped, x)
    return x


def seq_exchange(blocks, s):
    n = blocks.shape[0]
    mine = xor_blocks(blocks, s)
    got = jnp.stack([mine[0]] + [seq_swap(mine[j], j) for j in range(1, n)])
    return xor_blocks(got, s)


def batch_gather(block):
    nb = lax.axis_size("batch")
    ring = nb // 2
    b = lax.axis_index("batch")
    z, y = b // 2, b % 2
    out = jnp.zeros((ring, 2) + block.shape, block.dtype)
    zeros = (0,) * block.ndim
    current = block
    for k in range(ring):
        if k:
            current = batch_shift(current, 2)
        other = batch_swap(current, 1)
        at = (z + ring - k) % ring
        out = lax.dynamic_update_slice(out, current[None, None], (at, y) + zeros)
        out = lax.dynamic_update_slice(out, other[None, None], (at, 1 - y) + zeros)
    return out.reshape((nb,) + block.shape)


def batch_reduce(blocks):
    nb = lax.axis_size("batch")
    ring = nb // 2
    b = lax.axis_index("batch")
    z, y = b // 2, b % 2
    pairs = blocks.reshape((ring, 2) + blocks.shape[1:])
    mine = jnp.where(y == 0, pairs[:, 0], pairs[:, 1])
    other = jnp.where(y == 0, pairs[:, 1], pairs[:, 0])
    sums = mine.astype(F32) + batch_swap(other, 1).astype(F32)

    def part(dest):
        return lax.dynamic_index_in_dim(sums, dest % ring, 0, keepdims=False)

    running = part(z + ring - 1)
    for k in range(1, ring):
        running = batch_shift(running.astype(BF16), 2).astype(F32) + part(z + 2 * ring - k - 1)
    return running


def sum_all(x):
    for k in seq_bits():
        x = x + seq_swap(x, k)
    nb = lax.axis_size("batch")
    k = 1
    while k < nb:
        x = x + batch_swap(x, k)
        k *= 2
    return x


def gather_all(x):
    ns, nb = lax.axis_size("seq"), lax.axis_size("batch")
    s, b = lax.axis_index("seq"), lax.axis_index("batch")
    x = x[None]
    k = 1
    while k < ns * nb:
        got = seq_swap(x, k) if k < ns else batch_swap(x, k // ns)
        low = ((s if k < ns else b * ns) & k) == 0
        x = jnp.where(low, jnp.concatenate([x, got]), jnp.concatenate([got, x]))
        k *= 2
    return x


def inverse_rms(values):
    return lax.rsqrt(jnp.mean(values * values, axis=-1, keepdims=True) + eps_norm)


def rms_scale(values, gain_row):
    return values * inverse_rms(values) * gain_row


def norm_back(values, gain_row, upstream):
    inverse = inverse_rms(values)
    unit = values * inverse
    scaled = upstream * gain_row
    grad = inverse * (scaled - unit * jnp.mean(scaled * unit, axis=-1, keepdims=True))
    return grad, jnp.sum(upstream * unit, axis=0)


def product(left, right):
    return jnp.dot(left, right, preferred_element_type=F32)


def product_back(left, right):
    return lax.dot_general(left, right, (((1,), (1,)), ((), ())), preferred_element_type=F32)


def weight_grad(left, right):
    return lax.dot_general(left, right, (((0,), (0,)), ((), ())), preferred_element_type=F32)


def split_heads(x):
    return x.reshape(x.shape[0], x.shape[1] // HEAD, HEAD)


def attend_forward(query_rows, source_rows, w, out_w, allowed):
    q = product(query_rows, w[0]).astype(BF16)
    k = product(source_rows, w[1]).astype(BF16)
    v = product(source_rows, w[2]).astype(BF16)
    scores = (
        jnp.einsum("qhd,khd->hqk", split_heads(q), split_heads(k), preferred_element_type=F32)
        * 0.125
    )
    scores = jnp.where(allowed[None], scores, masked_score)
    peak = jnp.max(scores, axis=-1, keepdims=True)
    expo = jnp.exp(scores - peak)
    total = jnp.sum(expo, axis=-1, keepdims=True)
    probs = (expo / total).astype(BF16)
    mixed = jnp.einsum("hqk,khd->qhd", probs, split_heads(v), preferred_element_type=F32)
    mixed = mixed.reshape(q.shape).astype(BF16)
    return product(mixed, out_w), (q, k, v, peak + jnp.log(total), mixed)


def attend_back(dz, query_rows, source_rows, w, out_w, allowed, saved):
    q, k, v, log_total, mixed = saved
    grad_out_w = weight_grad(mixed, dz)
    grad_mixed = product_back(dz, out_w).astype(BF16)
    gh, qh, kh, vh = (split_heads(x) for x in (grad_mixed, q, k, v))
    scores = jnp.einsum("qhd,khd->hqk", qh, kh, preferred_element_type=F32) * 0.125
    scores = jnp.where(allowed[None], scores, masked_score)
    probs = jnp.exp(scores - log_total)
    grad_probs = jnp.einsum("qhd,khd->hqk", gh, vh, preferred_element_type=F32)
    center = jnp.sum(grad_probs * probs, axis=-1, keepdims=True)
    grad_scores = (probs * (grad_probs - center)).astype(BF16)
    dq = jnp.einsum("hqk,khd->qhd", grad_scores, kh, preferred_element_type=F32) * 0.125
    dk = jnp.einsum("hqk,qhd->khd", grad_scores, qh, preferred_element_type=F32) * 0.125
    dv = jnp.einsum("hqk,qhd->khd", probs.astype(BF16), gh, preferred_element_type=F32)
    dq = dq.reshape(q.shape).astype(BF16)
    dk = dk.reshape(k.shape).astype(BF16)
    dv = dv.reshape(v.shape).astype(BF16)
    grads = (weight_grad(query_rows, dq), weight_grad(source_rows, dk), weight_grad(source_rows, dv))
    grad_query = product_back(dq, w[0])
    grad_source = product_back(dk, w[1]) + product_back(dv, w[2])
    return grads, grad_out_w, grad_query, grad_source


def activate(gate, upper):
    return jax.nn.gelu(gate, approximate=True) * upper


def feed_forward(rows, gate_w, up_w, down_w):
    gate = product(rows, gate_w)
    upper = product(rows, up_w)
    hidden = activate(gate, upper).astype(BF16)
    return product(hidden, down_w), (gate, upper, hidden)


def feed_back(dz, rows, gate_w, up_w, down_w, saved):
    gate, upper, hidden = saved
    grad_down = weight_grad(hidden, dz)
    grad_hidden = product_back(dz, down_w)
    _, pullback = jax.vjp(activate, gate, upper)
    grad_gate, grad_upper = pullback(grad_hidden)
    grad_gate = grad_gate.astype(BF16)
    grad_upper = grad_upper.astype(BF16)
    grad_rows = product_back(grad_gate, gate_w) + product_back(grad_upper, up_w)
    return weight_grad(rows, grad_gate), weight_grad(rows, grad_upper), grad_down, grad_rows


def group_ids(rows, per_group, offset):
    start = lax.axis_index(("batch", "seq")) * rows
    return offset + (start + jnp.arange(rows, dtype=jnp.int32)) // per_group


def one_hot(row_ids):
    labels = jnp.arange(24, dtype=jnp.int32)
    return (row_ids[:, None] == labels[None, :]).astype(F32)


def group_sums(arrays, id_list):
    running = jnp.zeros((24,), F32)
    for group_member, row_ids in zip(arrays, id_list):
        squares = group_member * group_member
        if group_member.ndim == 2:
            squares = jnp.sum(squares, axis=1)
        running = running + jnp.sum(one_hot(row_ids) * squares[:, None], axis=0)
    return running


def per_device(
    encoder_layer_input,
    decoder_layer_input,
    cotangent,
    encoder_used_lengths,
    decoder_used_lengths,
    attn_master,
    inner_master,
    outer_master,
    gain_master,
    attn_first,
    inner_first,
    outer_first,
    gain_first,
    attn_second,
    inner_second,
    outer_second,
    gain_second,
):
    ns, nb = lax.axis_size("seq"), lax.axis_size("batch")
    s = lax.axis_index("seq")
    masters = (attn_master, inner_master, outer_master, gain_master)
    id_list = (
        group_ids(attn_master.shape[0], D, 0),
        group_ids(inner_master.shape[0], D, 12),
        group_ids(outer_master.shape[0], FF, 16),
        group_ids(gain_master.shape[0], D, 18),
    )
    ar, ir, orow = attn_master.shape[0], inner_master.shape[0], outer_master.shape[0]
    dc, fc = D // ns, FF // ns
    cuts = FF // (ns * orow)

    gains = gather_all(gain_master.astype(BF16)).reshape(6, D).astype(F32)
    attn_low = attn_master.astype(BF16).reshape(ar, ns, dc).swapaxes(0, 1)
    attn_cols = batch_gather(seq_exchange(attn_low, s).reshape(ns * ar, dc)).reshape(12, D, dc)
    inner_low = inner_master.astype(BF16).reshape(ir, cuts, ns, orow).transpose(2, 0, 1, 3)
    inner_cols = batch_gather(
        seq_exchange(inner_low.reshape(ns, ir, fc), s).reshape(ns * ir, fc)
    ).reshape(4, D, fc)
    outer_rows = batch_gather(outer_master.astype(BF16)).reshape(2, fc, D)
    out_blocks = jnp.stack([attn_cols[3], attn_cols[7], attn_cols[11]])
    out_blocks = out_blocks.reshape(3, ns, dc, dc).swapaxes(0, 1)
    out_w = seq_exchange(out_blocks, s).transpose(1, 2, 0, 3).reshape(3, dc, D)

    enc_state = encoder_layer_input[0].astype(F32)
    dec_state = decoder_layer_input[0].astype(F32)
    enc_rows, dec_rows = enc_state.shape[0], dec_state.shape[0]
    owners = [s ^ o for o in row_order()]
    enc_pos = jnp.concatenate([o * enc_rows + jnp.arange(enc_rows, dtype=jnp.int32) for o in owners])
    dec_pos = jnp.concatenate([o * dec_rows + jnp.arange(dec_rows, dtype=jnp.int32) for o in owners])
    enc_valid = (enc_pos < encoder_used_lengths[0])[None, :]
    dec_valid = (dec_pos < decoder_used_lengths[0])[None, :]
    enc_allowed = jnp.broadcast_to(enc_valid, (ns * enc_rows, ns * enc_rows))
    cross_allowed = jnp.broadcast_to(enc_valid, (ns * dec_rows, ns * enc_rows))
    self_allowed = (dec_pos[None, :] <= dec_pos[:, None]) & dec_valid
    alive = (s * dec_rows + jnp.arange(dec_rows, dtype=jnp.int32)) < decoder_used_lengths[0]
    seed = cotangent[0].astype(F32) * alive.astype(F32)[:, None]
    seed_all = gather_rows(seed.astype(BF16))

    rows_a = gather_rows(rms_scale(enc_state, gains[0]).astype(BF16))
    rows_c = gather_rows(rms_scale(dec_state, gains[3]).astype(BF16))
    branch, saved_enc = attend_forward(rows_a, rows_a, attn_cols[0:3], out_w[0], enc_allowed)
    enc_mid = enc_state + scatter_rows(branch)
    rows_b = gather_rows(rms_scale(enc_mid, gains[1]).astype(BF16))
    branch, saved_enc_ff = feed_forward(rows_b, inner_cols[0], inner_cols[1], outer_rows[0])
    enc_out = enc_mid + scatter_rows(branch)
    rows_e = gather_rows(rms_scale(enc_out, gains[2]).astype(BF16))
    branch, saved_self = attend_forward(rows_c, rows_c, attn_cols[4:7], out_w[1], self_allowed)
    dec_mid = dec_state + scatter_rows(branch)
    rows_d = gather_rows(rms_scale(dec_mid, gains[4]).astype(BF16))
    branch, saved_cross = attend_forward(rows_d, rows_e, attn_cols[8:11], out_w[2], cross_allowed)
    dec_late = dec_mid + scatter_rows(branch)
    rows_f = gather_rows(rms_scale(dec_late, gains[5]).astype(BF16))
    branch, saved_dec_ff = feed_forward(rows_f, inner_cols[2], inner_cols[3], outer_rows[1])
    decoder_layer_output = (dec_late + scatter_rows(branch)).astype(BF16)

    dec_gate, dec_up, dec_down, grad_rows = feed_back(
        seed_all, rows_f, inner_cols[2], inner_cols[3], outer_rows[1], saved_dec_ff
    )
    grad_x, gain_five = norm_back(dec_late, gains[5], scatter_rows(grad_rows))
    upstream = seed + grad_x
    cross_w, cross_out, grad_query, grad_source = attend_back(
        gather_rows(upstream.astype(BF16)), rows_d, rows_e, attn_cols[8:11], out_w[2], cross_allowed, saved_cross
    )
    grad_encoded = scatter_rows(grad_source)
    grad_x, gain_four = norm_back(dec_mid, gains[4], scatter_rows(grad_query))
    upstream = upstream + grad_x
    self_w, self_out, grad_query, grad_source = attend_back(
        gather_rows(upstream.astype(BF16)), rows_c, rows_c, attn_cols[4:7], out_w[1], self_allowed, saved_self
    )
    grad_x, gain_three = norm_back(dec_state, gains[3], scatter_rows(grad_query + grad_source))
    decoder_input_gradient = upstream + grad_x
    upstream, gain_two = norm_back(enc_out, gains[2], grad_encoded)
    enc_gate, enc_up, enc_down, grad_rows = feed_back(
        gather_rows(upstream.astype(BF16)), rows_b, inner_cols[0], inner_cols[1], outer_rows[0], saved_enc_ff
    )
    grad_x, gain_one = norm_back(enc_mid, gains[1], scatter_rows(grad_rows))
    upstream = upstream + grad_x
    enc_w, enc_out_w, grad_query, grad_source = attend_back(
        gather_rows(upstream.astype(BF16)), rows_a, rows_a, attn_cols[0:3], out_w[0], enc_allowed, saved_enc
    )
    grad_x, gain_zero = norm_back(enc_state, gains[0], scatter_rows(grad_query + grad_source))
    encoder_input_gradient = upstream + grad_x

    outer_grad = batch_reduce(jnp.stack([enc_down, dec_down]).astype(BF16).reshape(nb, orow, D))
    inner_part = batch_reduce(
        jnp.stack([enc_gate, enc_up, dec_gate, dec_up]).astype(BF16).reshape(nb, ns * ir, fc)
    )
    inner_part = seq_exchange(inner_part.astype(BF16).reshape(ns, ir, fc), s)
    inner_grad = inner_part.reshape(ns, ir, cuts, orow).transpose(1, 2, 0, 3).reshape(ir, FF).astype(F32)
    out_blocks = jnp.stack([enc_out_w, self_out, cross_out]).astype(BF16)
    out_blocks = out_blocks.reshape(3, dc, ns, dc).transpose(2, 0, 1, 3)
    out_cols = seq_exchange(out_blocks, s).swapaxes(0, 1).reshape(3, D, dc)
    attn_list = []
    for index, triple in enumerate((enc_w, self_w, cross_w)):
        attn_list += [g.astype(BF16) for g in triple] + [out_cols[index]]
    attn_part = batch_reduce(jnp.stack(attn_list).reshape(nb, ns * ar, dc))
    attn_part = seq_exchange(attn_part.astype(BF16).reshape(ns, ar, dc), s)
    attn_grad = attn_part.swapaxes(0, 1).reshape(ar, D).astype(F32)
    gain_sum = sum_all(
        jnp.concatenate((gain_zero, gain_one, gain_two, gain_three, gain_four, gain_five))
    )
    gr = gain_master.shape[0]
    gain_grad = lax.dynamic_slice_in_dim(gain_sum, lax.axis_index(("batch", "seq")) * gr, gr)

    grads = (attn_grad, inner_grad, outer_grad, gain_grad)
    firsts = (attn_first, inner_first, outer_first, gain_first)
    seconds = (attn_second, inner_second, outer_second, gain_second)
    decays = (decay_weight, decay_weight, decay_weight, 0.0)
    correction = 1.0 - 0.5**STEP
    first_list, second_list, update_list = ([], [], [])
    for master, first_old, second_old, gradient, decay_rate in zip(
        masters, firsts, seconds, grads, decays
    ):
        first_new = 0.5 * first_old + 0.5 * gradient
        second_new = 0.5 * second_old + 0.5 * gradient * gradient
        update = (
            first_new / correction / (jnp.sqrt(second_new / correction) + adam_eps)
            + decay_rate * master
        )
        first_list.append(first_new)
        second_list.append(second_new)
        update_list.append(update)
    weight_squares = sum_all(group_sums(masters, id_list))
    update_squares = sum_all(group_sums(update_list, id_list))
    weight_norms = jnp.sqrt(weight_squares)
    update_norms = jnp.sqrt(update_squares)
    trust_ratio = weight_norms / (update_norms + 1e-06)
    master_list, copy_list = ([], [])
    for master, update, row_ids in zip(masters, update_list, id_list):
        row_scale = jnp.sum(one_hot(row_ids) * trust_ratio[None, :], axis=1)
        if master.ndim == 2:
            row_scale = row_scale[:, None]
        master_new = master - lamb_rate * row_scale * update
        master_list.append(master_new)
        copy_list.append(master_new.astype(BF16))
    return (
        decoder_layer_output[None],
        encoder_input_gradient[None],
        decoder_input_gradient[None],
        *grads,
        *first_list,
        *second_list,
        *master_list,
        *copy_list,
        weight_norms,
        update_norms,
    )


def solution(mesh):
    rows = P("batch", "seq", None)
    matrix = P(("batch", "seq"), None)
    vector = P(("batch", "seq"))
    kinds = (matrix, matrix, matrix, vector)
    return jax.shard_map(
        per_device,
        mesh=mesh,
        in_specs=(rows, rows, rows, P("batch"), P("batch")) + kinds * 3,
        out_specs=(rows, rows, rows) + kinds * 5 + (P(), P()),
        check_vma=False,
    )
```

```python
import functools
import math

import jax
import jax.numpy as jnp
from jax import lax
from jax.experimental import pallas as pl
from jax.experimental.pallas import tpu as pltpu
from jax.sharding import PartitionSpec as P

D = 768
HEADS = 12
HEAD = 64
FF = 2048
STEP = 5

eps_norm = 1e-06
adam_eps = 1e-06
lamb_rate = 0.5
decay_weight = 0.01
masked_score = -1000000000.0

F32 = jnp.float32
BF16 = jnp.bfloat16


def seq_swap(x, k):
    n = lax.axis_size("seq")
    return lax.ppermute(x, "seq", [(i, i ^ k) for i in range(n)])


def batch_swap(x, k):
    n = lax.axis_size("batch")
    return lax.ppermute(x, "batch", [(i, i ^ k) for i in range(n)])


def gather_blocks(x):
    other = seq_swap(x, 2)
    return [x, seq_swap(x, 1), other, seq_swap(other, 1)]


def far_payload(keep_far, send_far):
    return (keep_far + seq_swap(send_far, 1).astype(F32)).astype(BF16)


def xor_blocks(x, s):
    n = x.shape[0]
    for k in (1, 2):
        swapped = jnp.stack([x[j ^ k] for j in range(n)])
        x = jnp.where((s & k) != 0, swapped, x)
    return x


def seq_exchange(blocks, s):
    n = blocks.shape[0]
    mine = xor_blocks(blocks, s)
    got = jnp.stack([mine[0]] + [seq_swap(mine[j], j) for j in range(1, n)])
    return xor_blocks(got, s)


def tie(x, *others):
    return lax.optimization_barrier((x, others))[0]


def ring_gathers(blocks):
    nb = lax.axis_size("batch")
    rounds = nb // 2
    shift = [(i, (i + 2) % nb) for i in range(nb)]
    results, before = [], None
    for group in blocks:
        current = list(group)
        if before is not None:
            current = [tie(x, *before) for x in current]
        got = [[] for _ in group]
        for k in range(rounds):
            if k:
                current = [lax.ppermute(x, "batch", shift) for x in current]
            if k == max(rounds - 2, 0):
                before = current
            for g, x in zip(got, current):
                g += [x, batch_swap(x, 1)]
        results += got
    return results


def assemble_body(by_lanes, moves, count, groups, *refs):
    ins, outs, sem = refs[: count * groups], refs[count * groups : -1], refs[-1]
    b = lax.axis_index("batch")
    z, y = b // 2, b % 2
    ring, copies = count // 2, []
    for n in range(count):
        k, e = n // 2, n % 2
        at = lax.rem(z + ring - k, ring) * 2 + (y + e - 2 * y * e)
        for group, which, (r0, r1), (c0, c1), (to_row, to_lane) in moves:
            ref, out = ins[group * count + n], outs[which]
            rows = pl.ds(to_row, r1 - r0)
            if by_lanes:
                width = out.shape[1] // count
                start = pl.multiple_of(at * width + to_lane, 128)
                target = out.at[rows, pl.ds(start, c1 - c0)]
            else:
                target = out.at[at, rows, pl.ds(to_lane, c1 - c0)]
            copies.append(pltpu.make_async_copy(ref.at[r0:r1, c0:c1], target, sem.at[len(copies)]))
    for copy in copies:
        copy.start()
    for copy in copies:
        copy.wait()


def assemble(groups, moves, shapes, by_lanes, name):
    count = len(groups[0])
    blocks = [x for g in groups for x in g]
    outs = [
        jax.ShapeDtypeStruct((h, count * w) if by_lanes else (count, h, w), BF16) for h, w in shapes
    ]
    return pl.pallas_call(
        functools.partial(assemble_body, by_lanes, moves, count, len(groups)),
        in_specs=[pl.BlockSpec(memory_space=pltpu.VMEM)] * len(blocks),
        out_specs=[pl.BlockSpec(memory_space=pl.ANY)] * len(outs),
        out_shape=outs,
        scratch_shapes=[pltpu.SemaphoreType.DMA((count * len(moves),))],
        cost_estimate=pl.CostEstimate(flops=10**13, bytes_accessed=10**10, transcendentals=0),
        name=name,
    )(*blocks)


def gathered_rows(got, name):
    h, w = got[0].shape
    return assemble([got], [(0, 0, (0, h), (0, w), (0, 0))], [(h, w)], False, name)[0]


def gathered_lanes(got, name):
    h, w = got[0].shape
    if w % 128 == 0:
        return assemble([got], [(0, 0, (0, h), (0, w), (0, 0))], [(h, w)], True, name)[0]
    return gathered_rows(got, name).swapaxes(0, 1).reshape(h, -1)


def gathered_feeds(got, rows, name):
    h, w = got[0].shape
    fc = w - 256
    moves = [(0, 0, (0, h), (0, fc), (0, 0))]
    for g in range(D // 128):
        r, c = g % 3 * rows, fc + g // 3 * 128
        moves.append((0, 1, (r, r + rows), (c, c + 128), (0, 128 * g)))
    return assemble([got], moves, [(h, fc), (rows, D)], False, name)


def pair_blocks(blocks):
    y = lax.axis_index("batch") % 2
    pairs = blocks.reshape((blocks.shape[0] // 2, 2) + blocks.shape[1:])
    return [lax.dynamic_index_in_dim(pairs, i, 1, keepdims=False) for i in (y, 1 - y)]


def own_block(parts, dest):
    per = parts[0][0].shape[0]
    total = None
    for n, (kept, got) in enumerate(parts):
        at = jnp.clip(dest - n * per, 0, per - 1)
        x = lax.dynamic_index_in_dim(kept, at, 0, keepdims=False).astype(F32)
        x = x + lax.dynamic_index_in_dim(got, at, 0, keepdims=False).astype(F32)
        total = x if n == 0 else jnp.where(dest >= n * per, x, total)
    return total


def ring_reduce(parts, first):
    nb = lax.axis_size("batch")
    ring, z = nb // 2, lax.axis_index("batch") // 2
    last = first + len(parts) * parts[0][0].shape[0]
    after = yield None
    moved = None
    for k in range(1, ring + 1):
        dest = (z + 2 * ring - k) % ring
        held = [(tie(kept, after), got) for kept, got in parts]
        total = own_block(held, dest - first)
        if moved is not None:
            total = total + moved.astype(F32)
        if k == ring:
            yield [total]
            return
        active = [i for i in range(nb) if first <= (i // 2 - k) % ring < last]
        sent = total.astype(BF16)
        moved = lax.ppermute(sent, "batch", [(i, (i + 2) % nb) for i in active])
        after = yield sent


def tree_reduce(parts, first):
    nb = lax.axis_size("batch")
    if nb != 8 or first or len(parts) > 1:
        yield from ring_reduce(parts, first)
        return

    def places(pairs_of):
        return [(2 * i + e, 2 * j + e) for i, j in pairs_of for e in range(2)]

    after = yield None
    kept, got = parts[0]
    total = tie(kept, after)[0].astype(F32) + got[0].astype(F32)
    for hop in (((3, 2), (1, 0)), ((2, 0),)):
        sent = total.astype(BF16)
        moved = lax.ppermute(sent, "batch", places(hop))
        after = yield sent
        total = total + tie(moved, after).astype(F32)
    yield [total]


def sum_steps(x):
    nb = lax.axis_size("batch")
    hops = [(seq_swap, 1), (seq_swap, 2)]
    k = 1
    while k < nb:
        hops.append((batch_swap, k))
        k *= 2
    after = None
    for swap, k in hops:
        got = swap(x if after is None else tie(x, after), k)
        after = yield x
        x = x + (got if after is None else tie(got, after))
    yield [x]


def sum_all(x):
    for x in sum_steps(x):
        pass
    return x[0]


class Clock:
    def __init__(self):
        self.last = None

    def now(self, x):
        return x if self.last is None else tie(x, self.last)

    def mark(self, x):
        self.last = x
        return x

    def step(self, work):
        got = work.send(self.last)
        return got if isinstance(got, list) else self.mark(got)

    def finish(self, work):
        got = None
        while not isinstance(got, list):
            got = self.step(work)
        return got


def nt(a, b):
    return lax.dot_general(a, b, (((1,), (1,)), ((), ())), preferred_element_type=F32)


def nn(a, b):
    return lax.dot_general(a, b, (((1,), (0,)), ((), ())), preferred_element_type=F32)


def tn(a, b):
    return lax.dot_general(a, b, (((0,), (0,)), ((), ())), preferred_element_type=F32)


def whole(x):
    shape = x.shape
    return pl.BlockSpec(shape, lambda i: (0,) * len(shape))


def part(shape, *index):
    return pl.BlockSpec(shape, lambda i: index)


def plain(arrays):
    return [(x, whole(x)) for x in arrays]


SCALARS = pl.BlockSpec(memory_space=pltpu.SMEM)


def call(body, ins, outs, flops, scratch=(), name=None):
    arrays = [a for a, _ in ins]
    specs = [whole(a) if s is None else s for a, s in ins]
    shapes = [jax.ShapeDtypeStruct(s, d) for s, d in outs]
    moved = sum(2 * math.prod(s) for s, _ in outs) + sum(2 * min(a.size, 2**20) for a in arrays)
    return pl.pallas_call(
        body,
        grid=(1,),
        in_specs=specs,
        out_specs=[whole(o) for o in shapes],
        out_shape=shapes,
        scratch_shapes=list(scratch),
        cost_estimate=pl.CostEstimate(flops=10**13, bytes_accessed=10**10, transcendentals=0),
        name=name,
    )(*arrays)


def positions(shape, axis, owner, rows):
    at = lax.broadcasted_iota(jnp.int32, shape, axis)
    shift = rows.bit_length() - 1
    return ((owner ^ (at >> shift)) << shift) + (at & (rows - 1))


def score_bias(meta, first_row, tile, q_rows, k_rows, causal):
    keys = positions((1, 4 * k_rows), 1, meta[0], k_rows)
    if not causal:
        return jnp.where(keys < meta[1], 0.0, masked_score)
    at = first_row + lax.broadcasted_iota(jnp.int32, (tile, 1), 0)
    shift = q_rows.bit_length() - 1
    queries = ((meta[0] ^ (at >> shift)) << shift) + (at & (q_rows - 1))
    return jnp.where((keys <= queries) & (keys < meta[1]), 0.0, masked_score)


def head_mask(shape, h):
    lane = lax.broadcasted_iota(jnp.int32, shape, 1)
    return (lane >= h * HEAD) & (lane < (h + 1) * HEAD)


def attend_tile(q, k, v, bias, heads):
    mixed = jnp.zeros(q.shape, F32)
    logs = jnp.zeros((q.shape[0], 128), F32)
    q = (q.astype(F32) * 0.125).astype(BF16)
    lane = lax.broadcasted_iota(jnp.int32, logs.shape, 1)
    for h in range(heads):
        mask = head_mask(q.shape, h)
        scores = nt(jnp.where(mask, q, jnp.zeros_like(q)), k) + bias
        peak = jnp.max(scores, axis=-1, keepdims=True)
        expo = jnp.exp(scores - peak)
        total = jnp.sum(expo, axis=-1, keepdims=True)
        probs = (expo * (1.0 / total)).astype(BF16)
        mixed = jnp.where(mask, nn(probs, v), mixed)
        logs = jnp.where(lane == h, peak + jnp.log(total), logs)
    return mixed, logs


def attend_rows(meta, q_ref, k_ref, v_ref, wo_ref, first, q_rows, k_rows, causal, outs, total_ref):
    logs_ref, mixed_ref = outs[:2]
    heads = q_ref.shape[1] // HEAD

    def step(t, carry):
        at = pl.multiple_of(t * q_rows, q_rows)
        q = q_ref[pl.ds(first + at, q_rows), :]
        bias = score_bias(meta, first + at, q_rows, q_rows, k_rows, causal)
        mixed, logs = attend_tile(q, k_ref[...], v_ref[...], bias, heads)
        low = mixed.astype(BF16)
        logs_ref[pl.ds(at, q_rows), :] = logs
        mixed_ref[pl.ds(at, q_rows), :] = low
        if wo_ref is not None:
            total_ref[pl.ds(at, q_rows), :] = nn(low, wo_ref[...])
        return carry

    lax.fori_loop(0, 2, step, 0)
    if wo_ref is not None:
        outs[2][...] = total_ref[:q_rows, :]
        outs[3][...] = total_ref[q_rows:, :].astype(BF16)


def project_body(rows, mixed_ref, wo_ref, keep_ref, send_ref):
    keep_ref[...] = nn(mixed_ref[:rows, :], wo_ref[...])
    send_ref[...] = nn(mixed_ref[rows:, :], wo_ref[...]).astype(BF16)


def project(mixed, out_w, group, name):
    rows, dc = mixed.shape[0] // 2, mixed.shape[1]
    return call(
        functools.partial(project_body, rows),
        [(mixed, None), out_weights(out_w, group)],
        [((rows, D), F32), ((rows, D), BF16)],
        4 * rows * dc * D,
        name=name,
    )


def attend_far_body(cross, raw, fused, causal, q_rows, k_rows, *refs):
    refs = list(refs)
    meta = refs.pop(0)
    queries, refs = refs[:4], refs[4:]
    sources = queries
    if cross:
        sources, refs = refs[:4], refs[4:]
    if raw:
        gain = refs.pop(0)
    wq, wk, wv = refs[:3]
    refs = refs[3:]
    wo = refs.pop(0) if fused else None
    if raw:
        rows_ref = refs.pop(0)
        for j in range(4):
            h = queries[j][...].astype(F32)
            inverse = lax.rsqrt(jnp.mean(h * h, axis=-1, keepdims=True) + eps_norm)
            rows_ref[j * q_rows : (j + 1) * q_rows, :] = (h * inverse * gain[...]).astype(BF16)
        queries = sources = [rows_ref.at[j * q_rows : (j + 1) * q_rows, :] for j in range(4)]
    q_ref, k_ref, v_ref = refs[:3]
    outs, total_ref = refs[3 : 7 if fused else 5], (refs[7] if fused else None)
    for j in range(4):
        q_ref[j * q_rows : (j + 1) * q_rows, :] = nt(queries[j][...], wq[...]).astype(BF16)
        rows = sources[j][...]
        k_ref[j * k_rows : (j + 1) * k_rows, :] = nt(rows, wk[...]).astype(BF16)
        v_ref[j * k_rows : (j + 1) * k_rows, :] = nt(rows, wv[...]).astype(BF16)
    attend_rows(meta, q_ref, k_ref, v_ref, wo, 2 * q_rows, q_rows, k_rows, causal, outs, total_ref)


def attend_near_body(causal, q_rows, k_rows, meta, q_ref, k_ref, v_ref, wo, *rest):
    attend_rows(meta, q_ref, k_ref, v_ref, wo, 0, q_rows, k_rows, causal, rest[:4], rest[4])


def attn_weights(attn_t, group):
    return [(attn_t, part((D // 4, D), 0, 4 * group + i)) for i in range(3)]


def out_weights(out_w, group):
    dc = out_w.shape[1]
    return (out_w, pl.BlockSpec((None, dc, D), lambda i: (group, 0, 0)))


def half_outs(q_rows, dc):
    return [((2 * q_rows, 128), F32), ((2 * q_rows, dc), BF16), ((q_rows, D), F32), ((q_rows, D), BF16)]


def attend_far(meta, queries, sources, attn_t, out_w, group, causal, gain=None):
    cross, raw, fused = sources is not None, gain is not None, out_w is not None
    q_rows, dc = queries[0][1].block_shape[0], D // 4
    k_rows = sources[0][1].block_shape[0] if cross else q_rows
    flops = 2 * D * dc * (4 * q_rows + 8 * k_rows) + 16 * q_rows * k_rows * D
    return call(
        functools.partial(attend_far_body, cross, raw, fused, causal, q_rows, k_rows),
        [(meta, SCALARS)]
        + list(queries)
        + (list(sources) if cross else [])
        + ([(gain, None)] if raw else [])
        + attn_weights(attn_t, group)
        + ([out_weights(out_w, group)] if fused else []),
        ([((4 * q_rows, D), BF16)] if raw else [])
        + [((4 * q_rows, dc), BF16), ((4 * k_rows, dc), BF16), ((4 * k_rows, dc), BF16)]
        + half_outs(q_rows, dc)[: 4 if fused else 2],
        flops,
        [pltpu.VMEM((2 * q_rows, D), F32)] if fused else [],
        f"attend_far_{group}",
    )


def attend_near(meta, q, k, v, out_w, group, causal):
    q_rows, k_rows, dc = q.shape[0] // 4, k.shape[0] // 4, q.shape[1]
    return call(
        functools.partial(attend_near_body, causal, q_rows, k_rows),
        [(meta, SCALARS), (q, part((2 * q_rows, dc), 0, 0)), (k, None), (v, None), out_weights(out_w, group)],
        half_outs(q_rows, dc),
        16 * q_rows * k_rows * D,
        [pltpu.VMEM((2 * q_rows, D), F32)],
        f"attend_near_{group}",
    )


def close_body(near_ref, core_ref, far_ref, residual_ref, gain_ref, out_ref, normed_ref):
    h = residual_ref[...].astype(F32) + near_ref[...] + core_ref[...].astype(F32) + far_ref[...].astype(F32)
    inverse = lax.rsqrt(jnp.mean(h * h, axis=-1, keepdims=True) + eps_norm)
    out_ref[...] = h
    normed_ref[...] = (h * inverse * gain_ref[...]).astype(BF16)


def close(near, core, far, residual, gain, name):
    shape = near.shape
    return call(
        close_body,
        [(x, None) for x in (near, core, far, residual, gain)],
        [(shape, F32), (shape, BF16)],
        10 * near.size,
        name=name,
    )


def close_back_body(near_ref, core_ref, far_ref, stream_ref, gain_ref, *rest):
    if len(rest) == 4:
        upstream_ref, rest = rest[0], rest[1:]
    else:
        upstream_ref = None
    out_ref, low_ref, dgain_ref = rest
    h = stream_ref[...].astype(F32)
    up = near_ref[...] + core_ref[...].astype(F32) + far_ref[...].astype(F32)
    inverse = lax.rsqrt(jnp.mean(h * h, axis=-1, keepdims=True) + eps_norm)
    unit = h * inverse
    scaled = up * gain_ref[...]
    grad = inverse * (scaled - unit * jnp.mean(scaled * unit, axis=-1, keepdims=True))
    if upstream_ref is not None:
        grad = upstream_ref[...].astype(F32) + grad
    out_ref[...] = grad
    low_ref[...] = grad.astype(BF16)
    dgain_ref[...] = jnp.sum(up * unit, axis=0, keepdims=True)


def close_back(near, core, far, stream, gain, upstream, name):
    shape = near.shape
    ins = [near, core, far, stream, gain] + ([] if upstream is None else [upstream])
    return call(
        close_back_body,
        [(x, None) for x in ins],
        [(shape, F32), (shape, BF16), ((1, shape[1]), F32)],
        20 * near.size,
        name=name,
    )


def attend_back_body(cross, causal, q_rows, k_rows, tile, *refs):
    meta = refs[0]
    dz = refs[1:5]
    q_ref, qt_ref, k_ref, v_ref, logs_near, logs_far, wq, wk, wv, wo = refs[5:15]
    dq_ref, dkt_ref, dvt_ref = refs[15:18]
    outs = refs[18 : 18 + (8 if cross else 4)]
    do_ref, dot_ref, dkt_sum, dvt_sum, logs_ref = refs[18 + len(outs) :]
    heads = q_ref.shape[1] // HEAD
    for j in range(4):
        at = slice(j * q_rows, (j + 1) * q_rows)
        rows = dz[j][...]
        do_ref[at, :] = nt(rows, wo[...]).astype(BF16)
        dot_ref[:, at] = nt(wo[...], rows).astype(BF16)
    logs_ref[: 2 * q_rows, :] = logs_near[...]
    logs_ref[2 * q_rows :, :] = logs_far[...]
    dkt_sum[...] = jnp.zeros_like(dkt_sum)
    dvt_sum[...] = jnp.zeros_like(dvt_sum)

    def step(t, carry):
        at = pl.ds(pl.multiple_of(t * tile, tile), tile)
        q, do = q_ref[at, :], do_ref[at, :]
        q = (q.astype(F32) * 0.125).astype(BF16)
        qt, dot = qt_ref[:, at], dot_ref[:, at]
        logs = logs_ref[at, :]
        bias = score_bias(meta, t * tile, tile, q_rows, k_rows, causal)
        dq = jnp.zeros(q.shape, F32)
        for h in range(heads):
            mask = head_mask(q.shape, h)
            zero = jnp.zeros_like(q)
            probs = jnp.exp(nt(jnp.where(mask, q, zero), k_ref[...]) + bias - logs[:, h : h + 1])
            grad_probs = nt(jnp.where(mask, do, zero), v_ref[...])
            weighted = probs * grad_probs
            center = jnp.sum(weighted, axis=-1, keepdims=True)
            grad_scores = (weighted - probs * center).astype(BF16)
            feats = slice(h * HEAD, (h + 1) * HEAD)
            dvt_sum[feats, :] += nn(dot[feats, :], probs.astype(BF16))
            dkt_sum[feats, :] += nn(qt[feats, :], grad_scores)
            dq = jnp.where(mask, nn(grad_scores, k_ref[...]), dq)
        dq_ref[at, :] = (dq * 0.125).astype(BF16)
        return carry

    lax.fori_loop(0, 4 * q_rows // tile, step, 0)
    dkt_ref[...] = (dkt_sum[...] * 0.125).astype(BF16)
    dvt_ref[...] = dvt_sum[...].astype(BF16)

    def query_part(j):
        return nn(dq_ref[j * q_rows : (j + 1) * q_rows, :], wq[...])

    def source_part(j):
        at = slice(j * k_rows, (j + 1) * k_rows)
        return tn(dkt_ref[:, at], wk[...]) + tn(dvt_ref[:, at], wv[...])

    parts = (query_part, source_part) if cross else ((lambda j: query_part(j) + source_part(j)),)
    for n, make in enumerate(parts):
        for j in range(4):
            outs[4 * n + j][...] = make(j).astype(outs[4 * n + j].dtype)


def attend_back(meta, dz, qt, attn_t, out_w, group, saved, q_rows, k_rows, causal, cross):
    q, k, v, logs_near, logs_far = saved
    dc = q.shape[1]
    tile = min(256, 4 * q_rows)

    def four(rows):
        return [((rows, D), F32), ((rows, D), BF16)] * 2

    outs = call(
        functools.partial(attend_back_body, cross, causal, q_rows, k_rows, tile),
        [(meta, SCALARS)]
        + list(dz)
        + [(q, None), (qt, None), (k, None), (v, None), (logs_near, None), (logs_far, None)]
        + attn_weights(attn_t, group)
        + [out_weights(out_w, group)],
        [((4 * q_rows, dc), BF16), ((dc, 4 * k_rows), BF16), ((dc, 4 * k_rows), BF16)]
        + (four(q_rows) + four(k_rows) if cross else four(q_rows)),
        80 * q_rows * k_rows * D + 4 * D * dc * (4 * q_rows + 4 * k_rows),
        [
            pltpu.VMEM((4 * q_rows, dc), BF16),
            pltpu.VMEM((dc, 4 * q_rows), BF16),
            pltpu.VMEM((dc, 4 * k_rows), F32),
            pltpu.VMEM((dc, 4 * k_rows), F32),
            pltpu.VMEM((4 * q_rows, 128), F32),
        ],
        f"attend_back_{group}",
    )
    return outs[:3], outs[3:]


def attend_weights_body(cross, q_rows, k_rows, *refs):
    queries = refs[0:4]
    sources = refs[4:8] if cross else queries
    rest = refs[8:] if cross else refs[4:]
    dq, dkt, dvt, dwq, dwk, dwv = rest
    gq = gk = gv = None
    for j in range(4):
        at, ak = slice(j * q_rows, (j + 1) * q_rows), slice(j * k_rows, (j + 1) * k_rows)
        x, y = queries[j][...], sources[j][...]
        a, b, c = tn(dq[at, :], x), nn(dkt[:, ak], y), nn(dvt[:, ak], y)
        gq, gk, gv = (a, b, c) if j == 0 else (gq + a, gk + b, gv + c)
    for ref, g in ((dwq, gq), (dwk, gk), (dwv, gv)):
        ref[...] = g.astype(BF16)


def attend_weights(queries, sources, grads, name):
    cross = sources is not None
    dq, dkt, dvt = grads
    q_rows, k_rows, dc = dq.shape[0] // 4, dkt.shape[1] // 4, dq.shape[1]
    return call(
        functools.partial(attend_weights_body, cross, q_rows, k_rows),
        list(queries)
        + (list(sources) if cross else [])
        + [(dq, None), (dkt, None), (dvt, None)],
        [((dc, D), BF16)] * 3,
        2 * D * dc * (4 * q_rows + 8 * k_rows),
        name=name,
    )


def out_weight_body(q_rows, d0, d1, d2, d3, near, far, out):
    total = None
    for j, ref in enumerate((d0, d1, d2, d3)):
        mixed = (near, far)[j // 2][(j % 2) * q_rows : (j % 2 + 1) * q_rows, :]
        x = tn(ref[...], mixed)
        total = x if j == 0 else total + x
    out[...] = total.astype(BF16)


def out_weight(dz, near, far, name):
    q_rows, dc = near.shape[0] // 2, near.shape[1]
    return call(
        functools.partial(out_weight_body, q_rows),
        list(dz) + [(near, None), (far, None)],
        [((D, dc), BF16)],
        8 * D * dc * q_rows,
        name=name,
    )[0]


GELU_A, GELU_B = math.sqrt(2.0 / math.pi), 0.044715


def feed_forward_body(rows, x0, x1, wg, wu, wd, gate_ref, up_ref, hidden_ref, keep_ref, send_ref):
    for j, x_ref in enumerate((x0, x1)):
        at = slice(j * rows, (j + 1) * rows)
        x = x_ref[...]
        gate, up = nn(x, wg[...]), nn(x, wu[...])
        gate_ref[at, :] = gate
        up_ref[at, :] = up
        inner = jnp.tanh(GELU_A * (gate + GELU_B * (gate * gate * gate)))
        hidden_ref[at, :] = (0.5 * gate * (1.0 + inner) * up).astype(BF16)
        out = (keep_ref, send_ref)[j]
        out[...] = nn(hidden_ref[at, :], wd[...]).astype(out.dtype)


def feed_weights(inner_cols, outer_rows, which):
    fc = inner_cols.shape[1]
    return [
        (inner_cols, part((D, fc), 2 * which, 0)),
        (inner_cols, part((D, fc), 2 * which + 1, 0)),
        (outer_rows, part((fc, D), which, 0)),
    ]


def feed_forward(half, inner_cols, outer_rows, which, name):
    rows, fc = half[0].shape[0], inner_cols.shape[1]
    return call(
        functools.partial(feed_forward_body, rows),
        plain(half) + feed_weights(inner_cols, outer_rows, which),
        [((2 * rows, fc), F32), ((2 * rows, fc), F32), ((2 * rows, fc), BF16), ((rows, D), F32), ((rows, D), BF16)],
        12 * rows * fc * D,
        name=name,
    )


def feed_back_body(rows, d0, d1, gate_ref, up_ref, wg, wu, wd, dgate_ref, dup_ref, keep_ref, send_ref):
    for j, d_ref in enumerate((d0, d1)):
        at = slice(j * rows, (j + 1) * rows)
        dh = nt(d_ref[...], wd[...])
        t, up = gate_ref[at, :], up_ref[at, :]
        square = t * t
        inner = jnp.tanh(GELU_A * t * (1.0 + GELU_B * square))
        slope = 0.5 * (1.0 + inner) + 0.5 * t * (1.0 - inner * inner) * (
            GELU_A * (1.0 + 3.0 * GELU_B * square)
        )
        dgate_ref[at, :] = (dh * up * slope).astype(BF16)
        dup_ref[at, :] = (dh * (0.5 * t * (1.0 + inner))).astype(BF16)
        out = (keep_ref, send_ref)[j]
        out[...] = (nt(dgate_ref[at, :], wg[...]) + nt(dup_ref[at, :], wu[...])).astype(out.dtype)


def feed_back(dz_half, gate, up, inner_cols, outer_rows, which, name):
    rows, fc = gate.shape[0] // 2, inner_cols.shape[1]
    return call(
        functools.partial(feed_back_body, rows),
        list(dz_half) + [(gate, None), (up, None)] + feed_weights(inner_cols, outer_rows, which),
        [((2 * rows, fc), BF16), ((2 * rows, fc), BF16), ((rows, D), F32), ((rows, D), BF16)],
        12 * rows * fc * D,
        name=name,
    )


def feed_weight_body(rows, packed, *refs):
    xs, dzs = refs[0:4], refs[4:8]
    dg, du, hid = refs[8:10], refs[10:12], refs[12:14]
    outs = refs[14:]
    gate = up = down = None
    for j in range(4):
        at = slice((j % 2) * rows, (j % 2 + 1) * rows)
        x = xs[j][...]
        a, b = tn(x, dg[j // 2][at, :]), tn(x, du[j // 2][at, :])
        c = tn(hid[j // 2][at, :], dzs[j][...])
        gate, up, down = (a, b, c) if j == 0 else (gate + a, up + b, down + c)
    fc = gate.shape[1]
    if not packed:
        outs[0][:D, :] = gate.astype(BF16)
        outs[0][D:, :] = up.astype(BF16)
        outs[1][...] = down.astype(BF16)
        return
    out = outs[0]
    height = out.shape[1]
    for n, grad in enumerate((gate, up)):
        for k in range(2):
            out[2 * n + k, :, :fc] = grad[k * height : (k + 1) * height, :].astype(BF16)
    short = fc // 4
    for q in range(4):
        for g in range(D // 128):
            piece = down[q * short : (q + 1) * short, g * 128 : (g + 1) * 128].astype(BF16)
            r, c = g % 3 * short, fc + g // 3 * 128
            out[q, r : r + short, c : c + 128] = piece


def feed_weight(xs, dzs, dgate, dup, hidden, packed, name):
    rows, fc = xs[0].shape[0], dgate[0].shape[1]
    return call(
        functools.partial(feed_weight_body, rows, packed),
        plain(xs) + list(dzs) + plain((*dgate, *dup, *hidden)),
        [((4, D // 2, fc + 256), BF16)] if packed else [((2 * D, fc), BF16), ((fc, D), BF16)],
        24 * rows * fc * D,
        name=name,
    )


def send_blocks(mine):
    return [mine[0]] + [seq_swap(mine[j], j) for j in range(1, 4)]


def place(scratch, refs, s):
    for j, ref in enumerate(refs):
        scratch[s ^ j] = ref[...]


def head_pack_body(ar, gr, lines, attn_ref, gain_ref, inner_ref, *refs):
    outs, scratch = refs[0:4], refs[4]
    s = lax.axis_index("seq")
    ir, width = inner_ref.shape[0], scratch.shape[2]
    dc, room, short = D // 4, width - ar, ir // 3
    turned = attn_ref[...].T
    gains = jnp.concatenate([gain_ref[...], jnp.zeros((1, lines * room - gr), F32)], axis=1)
    for t in range(4):
        at = s ^ t
        scratch[at, :dc, ar:] = jnp.zeros((dc, room), BF16)
        scratch[at, :dc, :ar] = turned[t * dc : (t + 1) * dc, :].astype(BF16)
        for n in range(lines):
            scratch[at, n : n + 1, ar:] = gains[:, n * room : (n + 1) * room].astype(BF16)
        for q in range(4):
            low = (4 * q + t) * 128
            piece = inner_ref[:, low : low + 128].astype(BF16)
            if q < 3:
                scratch[at, dc : dc + ir, q * 128 : (q + 1) * 128] = piece
            else:
                for n in range(3):
                    scratch[at, dc + ir :, n * 128 : (n + 1) * 128] = piece[n * short : (n + 1) * short, :]
    for j in range(4):
        outs[j][...] = scratch[j]


def head_unpack_body(ar, gr, lines, ir, *refs):
    ins, outer_ref = refs[0:4], refs[4]
    attn_ref, feed_ref, scratch = refs[5:8]
    place(scratch, ins, lax.axis_index("seq"))
    dc, room, short, orow = D // 4, scratch.shape[2] - ar, ir // 3, outer_ref.shape[0]
    pieces = []
    for k in range(4):
        attn_ref[:dc, k * ar : (k + 1) * ar] = scratch[k, :dc, :ar]
        rows = slice(k * ir, (k + 1) * ir)
        feed_ref[rows, :384] = scratch[k, dc : dc + ir, :]
        for n in range(3):
            feed_ref[k * ir + n * short : k * ir + (n + 1) * short, 384:512] = scratch[
                k, dc + ir :, n * 128 : (n + 1) * 128
            ]
        pieces += [scratch[k, n : n + 1, ar : ar + min(room, gr - n * room)].astype(F32) for n in range(lines)]
    for g in range(D // 128):
        r, c = g % 3 * orow, 512 + g // 3 * 128
        feed_ref[r : r + orow, c : c + 128] = outer_ref[:, g * 128 : (g + 1) * 128].astype(BF16)
    pieces.append(jnp.zeros((1, attn_ref.shape[1] - 4 * gr), F32))
    line = jnp.concatenate(pieces, axis=1)
    fill = jnp.zeros((attn_ref.shape[0] - dc - 1, line.shape[1]), F32)
    attn_ref[dc:, :] = jnp.concatenate([line, fill], axis=0).astype(BF16)


def head_exchange(attn_master, inner_master, outer_master, gain_master):
    ar, dc, gr = attn_master.shape[0], D // 4, gain_master.shape[0]
    ir = inner_master.shape[0]
    width = (ar // 128 + 1) * 128
    lines = -(-gr // (width - ar))
    tall = dc + ir + ir // 3
    scratch = [pltpu.VMEM((4, tall, width), BF16)]
    outs = call(
        functools.partial(head_pack_body, ar, gr, lines),
        plain([attn_master, gain_master[None], inner_master]),
        [((tall, width), BF16)] * 4,
        0,
        scratch,
        "head_pack",
    )
    return call(
        functools.partial(head_unpack_body, ar, gr, lines, ir),
        plain(send_blocks(outs) + [outer_master]),
        [((dc + 16, 4 * ar), BF16), ((4 * ir, D), BF16)],
        0,
        scratch,
        "head_unpack",
    )


def turn_pack_body(count, *refs):
    ins, outs, scratch = refs[:count], refs[count : count + 4], refs[count + 4]
    s = lax.axis_index("seq")
    dc = scratch.shape[2]
    for t in range(4):
        for g in range(count):
            scratch[s ^ t, g] = ins[g][:, t * dc : (t + 1) * dc].T
    for j in range(4):
        outs[j][...] = scratch[j]


def lanes_unpack_body(*refs):
    ins, out, scratch = refs[:4], refs[4], refs[5]
    place(scratch, ins, lax.axis_index("seq"))
    width = scratch.shape[3]
    for k in range(4):
        for g in range(scratch.shape[1]):
            out[g, :, k * width : (k + 1) * width] = scratch[k, g]


def rows_pack_body(count, *refs):
    ins, outs, scratch = refs[:count], refs[count : count + 4], refs[count + 4]
    s = lax.axis_index("seq")
    dc = scratch.shape[2]
    for t in range(4):
        for g in range(count):
            scratch[s ^ t, g] = ins[g][t * dc : (t + 1) * dc, :]
    for j in range(4):
        outs[j][...] = scratch[j]


def square_pack(body, ins, name):
    count, dc = len(ins), D // 4
    return call(
        functools.partial(body, count),
        ins,
        [((count, dc, dc), BF16)] * 4,
        0,
        [pltpu.VMEM((4, count, dc, dc), BF16)],
        name,
    )


def lanes_unpack(got, name):
    shape = got[0].shape
    return call(
        lanes_unpack_body,
        plain(got),
        [(shape[:2] + (4 * shape[2],), BF16)],
        0,
        [pltpu.VMEM((4,) + shape, BF16)],
        name,
    )[0]


def tail_pack_body(first_ref, rest_ref, *refs):
    outs, scratch = refs[:4], refs[4]
    s, z = lax.axis_index("seq"), lax.axis_index("batch") // (lax.axis_size("batch") // 4)
    total = jnp.where(z == 0, first_ref[...], rest_ref[...])
    width = scratch.shape[2]
    for t in range(4):
        scratch[s ^ t] = total[:, t * width : (t + 1) * width].astype(BF16)
    for j in range(4):
        outs[j][...] = scratch[j]


def tail_unpack_body(*refs):
    ins, out, scratch = refs[:4], refs[4], refs[5]
    place(scratch, ins, lax.axis_index("seq"))
    dc = scratch.shape[1]
    for k in range(4):
        out[:, k * dc : (k + 1) * dc] = scratch[k].astype(F32).T


def tail_exchange(first, rest, s, ar):
    dc = first.shape[0]
    if ar % 16:
        total = jnp.where(lax.axis_index("batch") < lax.axis_size("batch") // 4, first, rest)
        got = seq_exchange(total.astype(BF16).reshape(dc, 4, ar).swapaxes(0, 1), s)
        return got.reshape(4 * dc, ar).T.astype(F32)
    mine = call(
        tail_pack_body, plain([first, rest]), [((dc, ar), BF16)] * 4, 0, [pltpu.VMEM((4, dc, ar), BF16)], "tail_pack"
    )
    return call(
        tail_unpack_body,
        plain(send_blocks(mine)),
        [((ar, 4 * dc), F32)],
        0,
        [pltpu.VMEM((4, dc, ar), BF16)],
        "tail_unpack",
    )[0]


def split_lanes(scratch, pieces):
    width = scratch.shape[2]
    for n, piece in enumerate(pieces):
        for low in range(n * D, (n + 1) * D, D // 2):
            to = low % width
            scratch[low // width, :, to : to + D // 2] = piece[:, low - n * D : low - n * D + D // 2]


def part_pack_body(position, *refs):
    got, others = refs[0:4], refs[4:6]
    kept_ref, sent_ref, squares, scratch = refs[6:10]
    place(squares, got, lax.axis_index("seq"))
    pieces = [x[...] for x in others]
    pieces.insert(position, jnp.concatenate([squares[k, 0] for k in range(4)], axis=1))
    split_lanes(scratch, pieces)
    y = lax.axis_index("batch") % 2
    kept_ref[0] = scratch[y]
    sent_ref[0] = scratch[1 - y]


def attn_part(got, others, position, width, name):
    dc = D // 4
    if width % 128 or lax.axis_size("batch") != 8:
        pieces = list(others)
        if got is not None:
            pieces.insert(position, lanes_unpack(got, name)[0])
        joined = jnp.concatenate(pieces, axis=1)
        return pair_blocks(joined.reshape(dc, 3 * D // width, width).swapaxes(0, 1))
    return call(
        functools.partial(part_pack_body, position),
        plain(list(got) + list(others)),
        [((1, dc, width), BF16)] * 2,
        0,
        [pltpu.VMEM((4, 1, dc, dc), BF16), pltpu.VMEM((2, dc, width), BF16)],
        name,
    )


def self_part_body(rows, *refs):
    x = refs[0:4]
    dq, dkt, dvt, kept_ref, sent_ref, scratch = refs[4:10]
    gq = gk = gv = None
    for j in range(4):
        at = slice(j * rows, (j + 1) * rows)
        y = x[j][...]
        a, b, c = tn(dq[at, :], y), nn(dkt[:, at], y), nn(dvt[:, at], y)
        gq, gk, gv = (a, b, c) if j == 0 else (gq + a, gk + b, gv + c)
    split_lanes(scratch, [g.astype(BF16) for g in (gq, gk, gv)])
    y = lax.axis_index("batch") % 2
    kept_ref[0] = scratch[y]
    sent_ref[0] = scratch[1 - y]


def self_part(rows, grads, width, name):
    dq, dkt, dvt = grads
    per, dc = dq.shape[0] // 4, dq.shape[1]
    if width % 128 or lax.axis_size("batch") != 8:
        return attn_part(None, attend_weights(rows, None, grads, name), 0, width, name)
    return call(
        functools.partial(self_part_body, per),
        list(rows) + plain([dq, dkt, dvt]),
        [((1, dc, width), BF16)] * 2,
        0,
        [pltpu.VMEM((2, dc, width), BF16)],
        name,
    )


def group_ids(rows, per_group, offset):
    start = lax.axis_index(("batch", "seq")) * rows
    return offset + (start + jnp.arange(rows, dtype=jnp.int32)) // per_group


def one_hot(row_ids):
    labels = jnp.arange(24, dtype=jnp.int32)
    return (row_ids[:, None] == labels[None, :]).astype(F32)


def group_sums(arrays, id_list):
    running = jnp.zeros((24,), F32)
    for group_member, row_ids in zip(arrays, id_list):
        squares = group_member * group_member
        if group_member.ndim == 2:
            squares = jnp.sum(squares, axis=1)
        running = running + jnp.sum(one_hot(row_ids) * squares[:, None], axis=0)
    return running


def per_device(
    encoder_layer_input,
    decoder_layer_input,
    cotangent,
    encoder_used_lengths,
    decoder_used_lengths,
    attn_master,
    inner_master,
    outer_master,
    gain_master,
    attn_first,
    inner_first,
    outer_first,
    gain_first,
    attn_second,
    inner_second,
    outer_second,
    gain_second,
):
    ns, nb = lax.axis_size("seq"), lax.axis_size("batch")
    s, b = lax.axis_index("seq"), lax.axis_index("batch")
    masters = (attn_master, inner_master, outer_master, gain_master)
    id_list = (
        group_ids(attn_master.shape[0], D, 0),
        group_ids(inner_master.shape[0], D, 12),
        group_ids(outer_master.shape[0], FF, 16),
        group_ids(gain_master.shape[0], D, 18),
    )
    ar, ir, orow = attn_master.shape[0], inner_master.shape[0], outer_master.shape[0]
    dc, fc = D // ns, FF // ns
    cuts = FF // (ns * orow)

    gr = gain_master.shape[0]
    packed = nb == 8 and ar % 16 == 0 and 3 * orow == ns * ir and cuts == 4
    if packed:
        attn_mine, feed_mine = head_exchange(attn_master, inner_master, outer_master, gain_master)
        attn_got, feed_got = ring_gathers([(attn_mine,), (feed_mine,)])
        inner_cols, outer_rows = gathered_feeds(feed_got, orow, "gather_feeds")
    else:
        width = (ar // 128 + 1) * 128
        lines = -(-gr // (width - ar))
        corner = jnp.pad(gain_master.astype(BF16), (0, lines * (width - ar) - gr)).reshape(lines, width - ar)
        corner = jnp.broadcast_to(jnp.pad(corner, ((0, dc - lines), (0, 0))), (ns, dc, width - ar))
        attn_low = attn_master.astype(BF16).T.reshape(ns, dc, ar)
        got = seq_exchange(jnp.concatenate([attn_low, corner], axis=2), s)
        attn_mine = got[:, :, :ar].swapaxes(0, 1).reshape(dc, ns * ar)
        gains_mine = got[:, :lines, ar:].reshape(ns, -1)[:, :gr].reshape(1, ns * gr)
        attn_mine = jnp.concatenate([attn_mine, jnp.pad(gains_mine, ((0, 15), (0, ns * (ar - gr))))])
        inner_low = inner_master.astype(BF16).reshape(ir, cuts, ns, orow).transpose(2, 0, 1, 3)
        inner_mine = seq_exchange(inner_low.reshape(ns, ir, fc), s).reshape(ns * ir, fc)
        attn_got, inner_got, outer_got = ring_gathers(
            [(attn_mine,), (inner_mine,), (outer_master.astype(BF16),)]
        )
        inner_cols = gathered_rows(inner_got, "gather_inner")
        outer_rows = gathered_rows(outer_got, "gather_outer")
    inner_cols, outer_rows = inner_cols.reshape(4 * D, fc), outer_rows.reshape(2 * fc, D)
    attn_t = gathered_lanes(attn_got, "gather_attn")
    gains = attn_t[dc].reshape(nb, ns * ar)[:, : ns * gr].reshape(6, D).astype(F32)
    gain = [gains[i : i + 1] for i in range(6)]
    out_mine = square_pack(
        turn_pack_body, [(attn_t, part((dc, D), 0, 4 * g + 3)) for g in range(3)], "out_pack"
    )
    out_got = send_blocks(out_mine)

    enc_in, dec_in = encoder_layer_input[0], decoder_layer_input[0]
    er, dr = enc_in.shape[0], dec_in.shape[0]
    enc_meta = jnp.stack([s, encoder_used_lengths[0]]).astype(jnp.int32)
    dec_meta = jnp.stack([s, decoder_used_lengths[0]]).astype(jnp.int32)
    alive = (s * dr + jnp.arange(dr, dtype=jnp.int32)) < decoder_used_lengths[0]
    seed = jnp.where(alive[:, None], cotangent[0], jnp.zeros_like(cotangent[0]))
    blocks = gather_blocks(jnp.concatenate([enc_in, dec_in, seed]))
    enc_blocks = [(x, part((er, D), 0, 0)) for x in blocks]
    dec_blocks = [(x, part((dr, D), er // dr, 0)) for x in blocks]
    seed_blocks = [(x, part((dr, D), er // dr + 1, 0)) for x in blocks]

    def quarters(rows):
        return [(rows, part((rows.shape[0] // 4, D), j, 0)) for j in range(4)]

    clock = Clock()
    now, mark = clock.now, clock.mark

    rows_a, q0, k0, v0, logs_far0, mixed_far0 = attend_far(
        tie(enc_meta, out_mine[1]), enc_blocks, None, attn_t, None, 0, False, gain[0]
    )
    out_w = lanes_unpack([out_got[0]] + [tie(x, mixed_far0) for x in out_got[1:]], "out_unpack")
    far = mark(far_payload(*project(mixed_far0, out_w, 0, "project_far_0")))
    x_enc = seq_swap(far, 2)
    logs_near0, mixed_near0, kn_enc, sn = attend_near(enc_meta, now(q0), k0, v0, out_w, 0, False)
    mark(sn)
    c_enc = seq_swap(sn, 1)
    rows_c, q1, k1, v1, logs_far1, mixed_far1, kf, sf = attend_far(
        now(dec_meta), dec_blocks, None, attn_t, out_w, 1, True, gain[3]
    )
    mark(sf)
    enc_mid, norm_b = close(now(kn_enc), c_enc, x_enc, enc_in, gain[1], "close_enc_attn")
    mark(norm_b)
    rows_b = gather_blocks(norm_b)
    x_self = seq_swap(mark(far_payload(kf, now(sf))), 2)
    logs_near1, mixed_near1, kn, sn = attend_near(dec_meta, now(q1), k1, v1, out_w, 1, True)
    mark(sn)
    c_self = seq_swap(sn, 1)
    eg1, eu1, eh1, kf, sf = feed_forward((now(rows_b[2]), rows_b[3]), inner_cols, outer_rows, 0, "enc_feed_far")
    far = mark(far_payload(kf, sf))
    x_enc = seq_swap(far, 2)
    eg0, eu0, eh0, kn_enc, sn = feed_forward((now(rows_b[0]), rows_b[1]), inner_cols, outer_rows, 0, "enc_feed_near")
    mark(sn)
    c_enc = seq_swap(sn, 1)
    dec_mid, norm_d = close(now(kn), c_self, x_self, dec_in, gain[4], "close_self")
    mark(norm_d)
    enc_out, norm_e = close(now(kn_enc), c_enc, x_enc, enc_mid, gain[2], "close_enc_feed")
    mark(norm_e)
    rows_e = gather_blocks(norm_e)
    rows_d = gather_blocks(now(norm_d))
    q2, k2, v2, logs_far2, mixed_far2, kf, sf = attend_far(
        now(enc_meta), plain(rows_d), plain(rows_e), attn_t, out_w, 2, False
    )
    far = mark(far_payload(kf, sf))
    x_dec = seq_swap(far, 2)
    logs_near2, mixed_near2, kn, sn = attend_near(enc_meta, now(q2), k2, v2, out_w, 2, False)
    mark(sn)
    dec_late, norm_f = close(now(kn), seq_swap(sn, 1), x_dec, dec_mid, gain[5], "close_cross")
    mark(norm_f)
    rows_f = gather_blocks(norm_f)
    dg0, du0, dh0, kn_out, sn_out = feed_forward(
        (now(rows_f[0]), rows_f[1]), inner_cols, outer_rows, 1, "dec_feed_near"
    )
    mark(dh0)
    a0, b0, kn_dec, sn_dec = feed_back(
        seed_blocks[:2], now(dg0), du0, inner_cols, outer_rows, 1, "dec_feed_back_near"
    )
    mark(sn_dec)
    c_dec = seq_swap(sn_dec, 1)
    dg1, du1, dh1, kf_out, sf_out = feed_forward(
        (now(rows_f[2]), rows_f[3]), inner_cols, outer_rows, 1, "dec_feed_far"
    )
    mark(dh1)
    a1, b1, kf, sf = feed_back(seed_blocks[2:], now(dg1), du1, inner_cols, outer_rows, 1, "dec_feed_back_far")

    far = mark(far_payload(kf, sf))
    x_dec = seq_swap(far, 2)
    dec_feed = feed_weight(
        rows_f, seed_blocks, (now(a0), a1), (b0, b1), (dh0, dh1), packed, "dec_feed_weight"
    )
    mark(dec_feed[-1])
    up_five, low, gain_five = close_back(now(kn_dec), c_dec, x_dec, dec_late, gain[5], seed, "back_dec_feed")
    mark(low)
    dz_cross = plain(gather_blocks(low))
    half = nb // 2
    feed_shapes = [(D // 2, fc + 256)] if packed else [(ns * ir, fc), (orow, D)]

    def pair_send(kept, sent):
        return kept, batch_swap(mark(sent), 1)

    def feed_parts(grads):
        blocks = [now(x).reshape((half,) + shape) for x, shape in zip(grads, feed_shapes)]
        return [pair_send(*pair_blocks(x)) for x in blocks]

    dec_parts = feed_parts(dec_feed)

    c_out, x_out = seq_swap(now(sn_out), 1), seq_swap(mark(far_payload(kf_out, now(sf_out))), 2)
    decoder_layer_output = (dec_late + kn_out + c_out.astype(F32) + x_out.astype(F32)).astype(BF16)

    cross_d, outs = attend_back(
        enc_meta, dz_cross, now(q2).T, attn_t, out_w, 2, (q2, k2, v2, logs_near2, logs_far2), dr, er, False, True
    )
    far = mark(far_payload(outs[6], outs[7]))
    x_enc, c_enc = seq_swap(far, 2), seq_swap(now(outs[5]), 1)
    cross_w = attend_weights(plain(rows_d), plain(rows_e), (now(cross_d[0]), *cross_d[1:]), "cross_weights")
    mark(cross_w[0])
    far_dec = mark(far_payload(outs[2], now(outs[3])))
    cross_out = out_weight(dz_cross, now(mixed_near2), mixed_far2, "cross_out_weight")
    mark(cross_out)
    out_sent = square_pack(rows_pack_body, plain([now(cross_out)]), "cross_out_pack")
    mark(out_sent[1])
    up_two, low, gain_two = close_back(now(outs[4]), c_enc, x_enc, enc_out, gain[2], None, "back_encoded")
    mark(low)
    dz = plain(gather_blocks(low))
    out_got = send_blocks([out_sent[0]] + [now(x) for x in out_sent[1:]])
    x_dec, c_dec = seq_swap(now(far_dec), 2), seq_swap(now(outs[1]), 1)
    kn_dec = outs[0]
    a0, b0, kn_enc, sn = feed_back(dz[:2], now(eg0), eu0, inner_cols, outer_rows, 0, "enc_feed_back_near")
    mark(sn)
    c_enc = seq_swap(sn, 1)
    out_got = [out_got[0]] + [now(x) for x in out_got[1:]]
    part_three = pair_send(*attn_part(out_got, cross_w[1:], 2, ns * ar, "part_three"))
    a1, b1, kf, sf = feed_back(dz[2:], now(eg1), eu1, inner_cols, outer_rows, 0, "enc_feed_back_far")
    far = mark(far_payload(kf, sf))
    x_enc = seq_swap(far, 2)
    up_four, low_self, gain_four = close_back(now(kn_dec), c_dec, x_dec, dec_mid, gain[4], up_five, "back_cross")
    mark(low_self)
    dz_self = plain(gather_blocks(low_self))
    enc_feed = feed_weight(
        rows_b, dz, (now(a0), a1), (b0, b1), (eh0, eh1), packed, "enc_feed_weight"
    )
    mark(enc_feed[-1])
    enc_parts = feed_parts(enc_feed)
    up_one, low, gain_one = close_back(now(kn_enc), c_enc, x_enc, enc_mid, gain[1], up_two, "back_enc_feed")
    mark(low)
    dz_enc = plain(gather_blocks(low))
    self_d, outs = attend_back(
        dec_meta, dz_self, now(q1).T, attn_t, out_w, 1, (q1, k1, v1, logs_near1, logs_far1), dr, dr, True, False
    )
    mark(outs[3])
    self_out = out_weight(dz_self, now(mixed_near1), mixed_far1, "self_out_weight")
    mark(self_out)
    out_sent = square_pack(rows_pack_body, plain([now(self_out)]), "self_out_pack")
    mark(out_sent[1])
    out_got = send_blocks(out_sent)
    self_w = attend_weights(quarters(rows_c), None, (now(self_d[0]), *self_d[1:]), "self_weights")
    mark(self_w[0])
    kn_self, c_self = outs[0], seq_swap(now(outs[1]), 1)
    x_self = seq_swap(mark(far_payload(outs[2], now(outs[3]))), 2)
    feeds = [ring_reduce([e, d], 0) for e, d in zip(enc_parts, dec_parts)]
    for x in feeds:
        next(x)
        clock.step(x)
    out_got = [out_got[0]] + [now(x) for x in out_got[1:]]
    part_two = pair_send(*attn_part(out_got, (self_w[2], cross_w[0]), 1, ns * ar, "part_two"))
    enc_out_w = out_weight(dz_enc, now(mixed_near0), mixed_far0, "enc_out_weight")
    mark(enc_out_w)
    out_sent = square_pack(rows_pack_body, plain([now(enc_out_w)]), "enc_out_pack")
    mark(out_sent[1])
    out_got = send_blocks(out_sent)
    for x in feeds:
        clock.step(x)
    enc_d, outs = attend_back(
        enc_meta, dz_enc, now(q0).T, attn_t, out_w, 0, (q0, k0, v0, logs_near0, logs_far0), er, er, False, False
    )
    far = mark(far_payload(outs[2], outs[3]))
    x_enc, c_enc = seq_swap(far, 2), seq_swap(now(outs[1]), 1)
    part_zero = pair_send(
        *self_part(quarters(rows_a), (now(enc_d[0]), *enc_d[1:]), ns * ar, "part_zero")
    )
    for x in feeds:
        clock.step(x)
    out_got = [out_got[0]] + [now(x) for x in out_got[1:]]
    part_one = pair_send(*attn_part(out_got, self_w[:2], 0, ns * ar, "part_one"))
    decoder_input_gradient, _, gain_three = close_back(
        now(kn_self), c_self, x_self, dec_in, gain[3], up_four, "back_self"
    )
    mark(gain_three)
    encoder_input_gradient, _, gain_zero = close_back(
        now(outs[0]), c_enc, x_enc, enc_in, gain[0], up_one, "back_enc_attn"
    )
    mark(gain_zero)

    gain_parts = [x[0] for x in (now(gain_zero), gain_one, gain_two, gain_three, gain_four, gain_five)]
    totals = sum_steps(jnp.concatenate(gain_parts + [group_sums(masters, id_list)]))
    mark(next(totals))
    place_zero = tree_reduce([part_zero], 0)
    next(place_zero)
    clock.step(place_zero)
    clock.step(totals)
    rest = ring_reduce([part_one, part_two, part_three], nb // 8)
    next(rest)
    clock.step(rest)
    clock.step(totals)
    clock.step(totals)
    clock.step(place_zero)
    clock.step(rest)
    clock.step(totals)
    feed_sums = [mark(clock.finish(x)[0]) for x in feeds]
    if packed:
        inner_part = feed_sums[0][:, :fc]
        outer_grad = jnp.concatenate(
            [feed_sums[0][g % 3 * orow :, fc + g // 3 * 128 :][:orow, :128] for g in range(D // 128)], axis=1
        )
    else:
        inner_part, outer_grad = feed_sums
    inner_part = seq_exchange(inner_part.astype(BF16).reshape(ns, ir, fc), s)
    inner_grad = inner_part.reshape(ns, ir, cuts, orow).transpose(1, 2, 0, 3).reshape(ir, FF).astype(F32)
    clock.step(rest)
    (all_sums,) = clock.finish(totals)
    (sum_rest,), (sum_zero,) = clock.finish(rest), clock.finish(place_zero)
    attn_grad = tail_exchange(sum_zero, sum_rest, s, ar)
    gain_sum, weight_squares = all_sums[: 6 * D], all_sums[6 * D :]
    gain_grad = lax.dynamic_slice_in_dim(gain_sum, lax.axis_index(("batch", "seq")) * gr, gr)

    grads = (attn_grad, inner_grad, outer_grad, gain_grad)
    firsts = (attn_first, inner_first, outer_first, gain_first)
    seconds = (attn_second, inner_second, outer_second, gain_second)
    decays = (decay_weight, decay_weight, decay_weight, 0.0)
    correction = 1.0 - 0.5**STEP
    first_list, second_list, update_list = ([], [], [])
    for master, first_old, second_old, gradient, decay_rate in zip(
        masters, firsts, seconds, grads, decays
    ):
        first_new = 0.5 * first_old + 0.5 * gradient
        second_new = 0.5 * second_old + 0.5 * gradient * gradient
        update = (
            first_new / correction / (jnp.sqrt(second_new / correction) + adam_eps)
            + decay_rate * master
        )
        first_list.append(first_new)
        second_list.append(second_new)
        update_list.append(update)
    update_squares = sum_all(group_sums(update_list, id_list))
    weight_norms = jnp.sqrt(weight_squares)
    update_norms = jnp.sqrt(update_squares)
    trust_ratio = weight_norms / (update_norms + 1e-06)
    master_list, copy_list = ([], [])
    for master, update, row_ids in zip(masters, update_list, id_list):
        row_scale = jnp.sum(one_hot(row_ids) * trust_ratio[None, :], axis=1)
        if master.ndim == 2:
            row_scale = row_scale[:, None]
        master_new = master - lamb_rate * row_scale * update
        master_list.append(master_new)
        copy_list.append(master_new.astype(BF16))
    return (
        decoder_layer_output[None],
        encoder_input_gradient[None],
        decoder_input_gradient[None],
        *grads,
        *first_list,
        *second_list,
        *master_list,
        *copy_list,
        weight_norms,
        update_norms,
    )


def solution(mesh):
    rows = P("batch", "seq", None)
    matrix = P(("batch", "seq"), None)
    vector = P(("batch", "seq"))
    kinds = (matrix, matrix, matrix, vector)
    return jax.shard_map(
        per_device,
        mesh=mesh,
        in_specs=(rows, rows, rows, P("batch"), P("batch")) + kinds * 3,
        out_specs=(rows, rows, rows) + kinds * 5 + (P(), P()),
        check_vma=False,
    )
```

```python
import functools
import math

import jax
import jax.numpy as jnp
from jax import lax
from jax.experimental import pallas as pl
from jax.experimental.pallas import tpu as pltpu
from jax.sharding import PartitionSpec as P

D = 768
HEADS = 12
HEAD = 64
FF = 2048
STEP = 5

eps_norm = 1e-06
adam_eps = 1e-06
lamb_rate = 0.5
decay_weight = 0.01
masked_score = -1000000000.0

F32 = jnp.float32
BF16 = jnp.bfloat16

FLOPS, BYTES = 10**13, 10**10


def seq_swap(x, k):
    n = lax.axis_size("seq")
    return lax.ppermute(x, "seq", [(i, i ^ k) for i in range(n)])


def batch_swap(x, k):
    n = lax.axis_size("batch")
    return lax.ppermute(x, "batch", [(i, i ^ k) for i in range(n)])


def gather_blocks(x):
    other, near = seq_swap(x, 2), seq_swap(x, 1)
    return [x, near, other, seq_swap(tie(other, near), 1)]


def xor_blocks(x, s):
    n = x.shape[0]
    for k in (1, 2):
        swapped = jnp.stack([x[j ^ k] for j in range(n)])
        x = jnp.where((s & k) != 0, swapped, x)
    return x


def seq_exchange(blocks, s):
    n = blocks.shape[0]
    mine = xor_blocks(blocks, s)
    got = jnp.stack([mine[0]] + [seq_swap(mine[j], j) for j in range(1, n)])
    return xor_blocks(got, s)


def tie(x, *others):
    return lax.optimization_barrier((x, others))[0]


def ring_shift(x, active=None):
    nb = lax.axis_size("batch")
    return lax.ppermute(x, "batch", [(i, (i + 2) % nb) for i in (range(nb) if active is None else active)])


def ring_gather(block):
    rounds = lax.axis_size("batch") // 2
    after = yield None
    moving, got, paired = block if after is None else tie(block, after), [], None
    for k in range(rounds):
        following = None
        if k + 1 < rounds:
            payload = moving if paired is None else tie(moving, paired)
            following = ring_shift(payload)
        got.append(moving)
        paired = batch_swap(moving if following is not None or paired is None else tie(moving, paired), 1)
        got.append(paired)
        after = yield moving if following is None else payload
        if following is not None:
            moving = following if after is None else tie(following, after)
            paired = got[-1]
    yield got


def assemble_body(by_lanes, moves, count, low, *refs):
    here = len(refs) - 1 - low[1]
    ins, outs, sem = refs[:here], refs[here:-1], refs[-1]
    b = lax.axis_index("batch")
    z, y = b // 2, b % 2
    ring, copies = count // 2, []
    for i, ref in enumerate(ins):
        k, e = (low[0] + i) // 2, (low[0] + i) % 2
        at = lax.rem(z + ring - k, ring) * 2 + (y + e - 2 * y * e)
        for which, (r0, r1), (c0, c1), (to_row, to_lane) in moves:
            out = outs[which]
            rows = pl.ds(to_row, r1 - r0)
            if by_lanes:
                start = pl.multiple_of(at * (out.shape[1] // count) + to_lane, 128)
                target = out.at[rows, pl.ds(start, c1 - c0)]
            else:
                target = out.at[at, rows, pl.ds(to_lane, c1 - c0)]
            copies.append(pltpu.make_async_copy(ref.at[r0:r1, c0:c1], target, sem.at[len(copies)]))
    for copy in copies:
        copy.start()
    for copy in copies:
        copy.wait()


def assemble(blocks, moves, shapes, by_lanes, name, last=0):
    count = len(blocks)
    outs = [jax.ShapeDtypeStruct((h, count * w) if by_lanes else (count, h, w), BF16) for h, w in shapes]
    any_space = pl.BlockSpec(memory_space=pl.ANY)
    made = []
    for low, high in ((0, count - last), (count - last, count)):
        if low == high:
            continue
        part_of = blocks[low:high]

        def body(*refs, low=low, made=tuple(made), part_of=part_of):
            given = refs[: len(part_of)]
            assemble_body(by_lanes, moves, count, (low, len(outs)), *given, *refs[len(part_of) + len(made) :])

        made = pl.pallas_call(
            body,
            in_specs=[pl.BlockSpec(memory_space=pltpu.VMEM)] * len(part_of) + [any_space] * len(made),
            out_specs=[any_space] * len(outs),
            out_shape=outs,
            input_output_aliases={len(part_of) + i: i for i in range(len(made))},
            scratch_shapes=[pltpu.SemaphoreType.DMA((len(part_of) * len(moves),))],
            cost_estimate=pl.CostEstimate(flops=FLOPS, bytes_accessed=BYTES, transcendentals=0),
            name=f"{name}_{low}",
        )(*part_of, *made)
    return made


def gathered_rows(got, name):
    h, w = got[0].shape
    return assemble(got, [(0, (0, h), (0, w), (0, 0))], [(h, w)], False, name)[0]


def gathered_lanes(got, name):
    h, w = got[0].shape
    if w % 128 == 0:
        return assemble(got, [(0, (0, h), (0, w), (0, 0))], [(h, w)], True, name)[0]
    return gathered_rows(got, name).swapaxes(0, 1).reshape(h, -1)


def gathered_feeds(got, rows, name):
    h, w = got[0].shape
    fc = w - 256
    moves = [(0, (0, h), (0, fc), (0, 0))]
    for g in range(D // 128):
        r, c = g % 3 * rows, fc + g // 3 * 128
        moves.append((1, (r, r + rows), (c, c + 128), (0, 128 * g)))
    return assemble(got, moves, [(h, fc), (rows, D)], False, name, 2)


def pair_blocks(blocks):
    y = lax.axis_index("batch") % 2
    pairs = blocks.reshape((blocks.shape[0] // 2, 2) + blocks.shape[1:])
    return [lax.dynamic_index_in_dim(pairs, i, 1, keepdims=False) for i in (y, 1 - y)]


def hop_body(step, counts, moving, riding, *refs):
    count = len(counts)
    kept, got = refs[:count], refs[count : 2 * count]
    refs = list(refs[2 * count :])
    moved = refs.pop(0) if moving else None
    extra = refs.pop(0) if riding else None
    out, one, two, sem = refs
    ring = lax.axis_size("batch") // 2
    dest = lax.rem(lax.axis_index("batch") // 2 + 2 * ring - step, ring)
    for n in range(count):
        low = sum(counts[:n])

        @pl.when((dest >= low) & (dest < low + counts[n]))
        def _(n=n, low=low):
            mine = pltpu.make_async_copy(kept[n].at[dest - low], one, sem.at[0])
            other = pltpu.make_async_copy(got[n].at[dest - low], two, sem.at[1])
            mine.start()
            other.start()
            mine.wait()
            other.wait()

    total = one[...].astype(F32) + two[...].astype(F32)
    rows = one.shape[0]
    if moving:
        total = total + moved[:rows, :].astype(F32)
    out[:rows, :] = total.astype(out.dtype)
    if riding:
        lines = jnp.concatenate([extra[dest * 2], extra[dest * 2 + 1]], axis=0)
        if moving:
            lines = lines + moved[rows : rows + 2, :].astype(F32)
        out[rows:, :] = jnp.concatenate([lines, jnp.zeros((14, lines.shape[1]), F32)], axis=0).astype(out.dtype)


def hop(parts, step, moved, extra, dtype, name):
    shape = parts[0][0].shape[1:]
    arrays = [k for k, _ in parts] + [g for _, g in parts]
    specs = [pl.BlockSpec(memory_space=pl.ANY)] * len(arrays)
    for x in (moved, extra):
        if x is not None:
            arrays.append(x)
            specs.append(pl.BlockSpec(memory_space=pltpu.VMEM))
    out = shape if extra is None else (shape[0] + 16, shape[1])
    return pl.pallas_call(
        functools.partial(hop_body, step, [k.shape[0] for k, _ in parts], moved is not None, extra is not None),
        in_specs=specs,
        out_specs=pl.BlockSpec(memory_space=pltpu.VMEM),
        out_shape=jax.ShapeDtypeStruct(out, dtype),
        scratch_shapes=[pltpu.VMEM(shape, BF16), pltpu.VMEM(shape, BF16), pltpu.SemaphoreType.DMA((2,))],
        cost_estimate=pl.CostEstimate(flops=FLOPS, bytes_accessed=BYTES, transcendentals=0),
        name=f"{name}_{step}",
    )(*arrays)


def ring_reduce(parts, name, extra=None, flight=None):
    ring = lax.axis_size("batch") // 2
    after = yield None
    moved = None
    for k in range(1, ring + 1):
        if moved is None:
            held = [(kept if after is None else tie(kept, after), got) for kept, got in parts]
        else:
            held, moved = parts, tie(moved, after)
        if k == ring:
            yield [hop(held, k, moved, extra, F32, name)]
            return
        sent = hop(held, k, moved, extra, BF16, name)
        moved = ring_shift(sent)
        if flight is not None:
            flight.append(moved)
        after = yield sent


def sum_seq(x):
    for k in (1, 2):
        x = x + seq_swap(x, k)
    return x


def sum_all(x):
    x = sum_seq(x)
    k = 1
    while k < lax.axis_size("batch"):
        x = x + batch_swap(x, k)
        k *= 2
    return x


class Clock:
    def __init__(self):
        self.last = None

    def now(self, x):
        return x if self.last is None else tie(x, self.last)

    def mark(self, x):
        self.last = x
        return x

    def step(self, work):
        got = work.send(self.last)
        return got if isinstance(got, list) else self.mark(got)

    def finish(self, work):
        got = None
        while not isinstance(got, list):
            got = self.step(work)
        return got


def nt(a, b):
    return lax.dot_general(a, b, (((1,), (1,)), ((), ())), preferred_element_type=F32)


def nn(a, b):
    return lax.dot_general(a, b, (((1,), (0,)), ((), ())), preferred_element_type=F32)


def tn(a, b):
    return lax.dot_general(a, b, (((0,), (0,)), ((), ())), preferred_element_type=F32)


def whole(x):
    shape = x.shape
    return pl.BlockSpec(shape, lambda i: (0,) * len(shape))


def part(shape, *index):
    return pl.BlockSpec(shape, lambda i: index)


def plain(arrays):
    return [(x, whole(x)) for x in arrays]


SCALARS = pl.BlockSpec(memory_space=pltpu.SMEM)


def call(body, ins, outs, flops, scratch=(), name=None):
    arrays = [a for a, _ in ins]
    specs = [whole(a) if s is None else s for a, s in ins]
    shapes = [jax.ShapeDtypeStruct(s, d) for s, d in outs]
    return pl.pallas_call(
        body,
        grid=(1,),
        in_specs=specs,
        out_specs=[whole(o) for o in shapes],
        out_shape=shapes,
        scratch_shapes=list(scratch),
        cost_estimate=pl.CostEstimate(flops=FLOPS, bytes_accessed=BYTES, transcendentals=0),
        name=name,
    )(*arrays)


def positions(shape, axis, owner, rows):
    at = lax.broadcasted_iota(jnp.int32, shape, axis)
    shift = rows.bit_length() - 1
    return ((owner ^ (at >> shift)) << shift) + (at & (rows - 1))


def score_bias(meta, first_row, tile, q_rows, k_rows, causal):
    keys = positions((1, 4 * k_rows), 1, meta[0], k_rows)
    if not causal:
        return jnp.where(keys < meta[1], 0.0, masked_score)
    at = first_row + lax.broadcasted_iota(jnp.int32, (tile, 1), 0)
    shift = q_rows.bit_length() - 1
    queries = ((meta[0] ^ (at >> shift)) << shift) + (at & (q_rows - 1))
    return jnp.where((keys <= queries) & (keys < meta[1]), 0.0, masked_score)


def head_mask(shape, h):
    lane = lax.broadcasted_iota(jnp.int32, shape, 1)
    return (lane >= h * HEAD) & (lane < (h + 1) * HEAD)


def attend_tile(q, k, v, bias, heads):
    mixed = jnp.zeros(q.shape, F32)
    logs = jnp.zeros((q.shape[0], 128), F32)
    q = (q.astype(F32) * 0.125).astype(BF16)
    lane = lax.broadcasted_iota(jnp.int32, logs.shape, 1)
    for h in range(heads):
        mask = head_mask(q.shape, h)
        scores = nt(jnp.where(mask, q, jnp.zeros_like(q)), k) + bias
        peak = jnp.max(scores, axis=-1, keepdims=True)
        expo = jnp.exp(scores - peak)
        total = jnp.sum(expo, axis=-1, keepdims=True)
        probs = (expo * (1.0 / total)).astype(BF16)
        mixed = jnp.where(mask, nn(probs, v), mixed)
        logs = jnp.where(lane == h, peak + jnp.log(total), logs)
    return mixed, logs


def attend_rows(meta, q_ref, k_ref, v_ref, wo_ref, first, q_rows, k_rows, causal, outs, total_ref):
    logs_ref, mixed_ref = outs[:2]
    heads = q_ref.shape[1] // HEAD

    def step(t, carry):
        at = pl.multiple_of(t * q_rows, q_rows)
        q = q_ref[pl.ds(first + at, q_rows), :]
        bias = score_bias(meta, first + at, q_rows, q_rows, k_rows, causal)
        mixed, logs = attend_tile(q, k_ref[...], v_ref[...], bias, heads)
        low = mixed.astype(BF16)
        logs_ref[pl.ds(at, q_rows), :] = logs
        mixed_ref[pl.ds(at, q_rows), :] = low
        if wo_ref is not None:
            total_ref[pl.ds(at, q_rows), :] = nn(low, wo_ref[...])
        return carry

    lax.fori_loop(0, 2, step, 0)
    if wo_ref is not None:
        outs[2][...] = total_ref[:q_rows, :].astype(outs[2].dtype)
        outs[3][...] = total_ref[q_rows:, :].astype(BF16)


def project_body(rows, mixed_ref, wo_ref, keep_ref, send_ref):
    keep_ref[...] = nn(mixed_ref[:rows, :], wo_ref[...]).astype(BF16)
    send_ref[...] = nn(mixed_ref[rows:, :], wo_ref[...]).astype(BF16)


def project(mixed, out_w, name):
    rows, dc = mixed.shape[0] // 2, mixed.shape[1]
    return call(
        functools.partial(project_body, rows),
        [(mixed, None), out_weights(out_w)],
        [((rows, D), BF16), ((rows, D), BF16)],
        4 * rows * dc * D,
        name=name,
    )


def attend_far_body(cross, raw, fused, causal, q_rows, k_rows, *refs):
    refs = list(refs)
    meta = refs.pop(0)
    queries, refs = refs[:4], refs[4:]
    sources = queries
    if cross:
        sources, refs = refs[:4], refs[4:]
    if raw:
        gain = refs.pop(0)
    wq, wk, wv = refs[:3]
    refs = refs[3:]
    wo = refs.pop(0) if fused else None
    if raw:
        rows_ref = refs.pop(0)
        for j in range(4):
            h = queries[j][...].astype(F32)
            inverse = lax.rsqrt(jnp.mean(h * h, axis=-1, keepdims=True) + eps_norm)
            rows_ref[j * q_rows : (j + 1) * q_rows, :] = (h * inverse * gain[...]).astype(BF16)
        queries = sources = [rows_ref.at[j * q_rows : (j + 1) * q_rows, :] for j in range(4)]
    q_ref, k_ref, v_ref = refs[:3]
    outs, total_ref = refs[3 : 7 if fused else 5], (refs[7] if fused else None)
    for j in range(4):
        q_ref[j * q_rows : (j + 1) * q_rows, :] = nt(queries[j][...], wq[...]).astype(BF16)
        rows = sources[j][...]
        k_ref[j * k_rows : (j + 1) * k_rows, :] = nt(rows, wk[...]).astype(BF16)
        v_ref[j * k_rows : (j + 1) * k_rows, :] = nt(rows, wv[...]).astype(BF16)
    attend_rows(meta, q_ref, k_ref, v_ref, wo, 2 * q_rows, q_rows, k_rows, causal, outs, total_ref)


def attend_near_body(causal, q_rows, k_rows, meta, q_ref, k_ref, v_ref, wo, *rest):
    attend_rows(meta, q_ref, k_ref, v_ref, wo, 0, q_rows, k_rows, causal, rest[:4], rest[4])


def attn_weights(attn_t, group):
    return [(attn_t, part((D // 4, D), 0, 4 * group + i)) for i in range(3)]


def out_weights(out_w):
    stack, place = out_w
    return (stack, pl.BlockSpec((None, stack.shape[1], D), lambda i: (place, 0, 0)))


def half_outs(q_rows, dc, keep):
    return [((2 * q_rows, 128), F32), ((2 * q_rows, dc), BF16), ((q_rows, D), keep), ((q_rows, D), BF16)]


def attend_far(meta, queries, sources, attn_t, out_w, group, causal, gain=None):
    cross, raw, fused = sources is not None, gain is not None, out_w is not None
    q_rows, dc = queries[0][1].block_shape[0], D // 4
    k_rows = sources[0][1].block_shape[0] if cross else q_rows
    flops = 2 * D * dc * (4 * q_rows + 8 * k_rows) + 16 * q_rows * k_rows * D
    return call(
        functools.partial(attend_far_body, cross, raw, fused, causal, q_rows, k_rows),
        [(meta, SCALARS)]
        + list(queries)
        + (list(sources) if cross else [])
        + ([(gain, None)] if raw else [])
        + attn_weights(attn_t, group)
        + ([out_weights(out_w)] if fused else []),
        ([((4 * q_rows, D), BF16)] if raw else [])
        + [((4 * q_rows, dc), BF16), ((4 * k_rows, dc), BF16), ((4 * k_rows, dc), BF16)]
        + half_outs(q_rows, dc, BF16)[: 4 if fused else 2],
        flops,
        [pltpu.VMEM((2 * q_rows, D), F32)] if fused else [],
        f"attend_far_{group}",
    )


def attend_near(meta, q, k, v, out_w, group, causal):
    q_rows, k_rows, dc = q.shape[0] // 4, k.shape[0] // 4, q.shape[1]
    return call(
        functools.partial(attend_near_body, causal, q_rows, k_rows),
        [(meta, SCALARS), (q, part((2 * q_rows, dc), 0, 0)), (k, None), (v, None), out_weights(out_w)],
        half_outs(q_rows, dc, F32),
        16 * q_rows * k_rows * D,
        [pltpu.VMEM((2 * q_rows, D), F32)],
        f"attend_near_{group}",
    )


STEPS = 1


def row_call(body, ins, outs, name):
    rows = ins[0].shape[0]

    def spec(shape):
        if shape[0] == 1:
            return pl.BlockSpec(shape, lambda i: (0, 0))
        return pl.BlockSpec((rows // STEPS,) + tuple(shape[1:]), lambda i: (i, 0))

    return pl.pallas_call(
        body,
        grid=(STEPS,),
        in_specs=[spec(x.shape) for x in ins],
        out_specs=[spec(s) for s, _ in outs],
        out_shape=[jax.ShapeDtypeStruct(s, d) for s, d in outs],
        cost_estimate=pl.CostEstimate(flops=FLOPS, bytes_accessed=BYTES, transcendentals=0),
        name=name,
    )(*ins)


def add_low(a, b):
    return (a.astype(F32) + b.astype(F32)).astype(BF16)


def far_payload(keep_far, send_far):
    return add_low(keep_far, seq_swap(send_far, 1))


def close_body(near_ref, core_ref, far_ref, residual_ref, gain_ref, out_ref, normed_ref):
    h = residual_ref[...].astype(F32) + near_ref[...] + core_ref[...].astype(F32) + far_ref[...].astype(F32)
    inverse = lax.rsqrt(jnp.mean(h * h, axis=-1, keepdims=True) + eps_norm)
    out_ref[...] = h
    normed_ref[...] = (h * inverse * gain_ref[...]).astype(BF16)


def close(near, core, far, residual, gain, name):
    return row_call(
        close_body, [near, core, far, residual, gain], [(near.shape, F32), (near.shape, BF16)], name
    )


def close_back_body(near_ref, core_ref, far_ref, stream_ref, gain_ref, *rest):
    if len(rest) == 4:
        upstream_ref, rest = rest[0], rest[1:]
    else:
        upstream_ref = None
    out_ref, low_ref, dgain_ref = rest
    h = stream_ref[...].astype(F32)
    up = near_ref[...] + core_ref[...].astype(F32) + far_ref[...].astype(F32)
    inverse = lax.rsqrt(jnp.mean(h * h, axis=-1, keepdims=True) + eps_norm)
    unit = h * inverse
    scaled = up * gain_ref[...]
    grad = inverse * (scaled - unit * jnp.mean(scaled * unit, axis=-1, keepdims=True))
    if upstream_ref is not None:
        grad = upstream_ref[...].astype(F32) + grad
    out_ref[...] = grad
    low_ref[...] = grad.astype(BF16)

    @pl.when(pl.program_id(0) == 0)
    def _():
        dgain_ref[...] = jnp.zeros_like(dgain_ref)

    dgain_ref[...] += jnp.sum(up * unit, axis=0, keepdims=True)


def close_back(near, core, far, stream, gain, upstream, name):
    shape = near.shape
    ins = [near, core, far, stream, gain] + ([] if upstream is None else [upstream])
    return row_call(close_back_body, ins, [(shape, F32), (shape, BF16), ((1, shape[1]), F32)], name)


def attend_back_body(cross, causal, q_rows, k_rows, tile, *refs):
    meta = refs[0]
    dz = refs[1:5]
    q_ref, qt_ref, k_ref, v_ref, logs_near, logs_far, wq, wk, wv, wo = refs[5:15]
    dq_ref, dkt_ref, dvt_ref = refs[15:18]
    outs = refs[18 : 18 + (8 if cross else 4)]
    do_ref, dot_ref, dkt_sum, dvt_sum, logs_ref = refs[18 + len(outs) :]
    heads = q_ref.shape[1] // HEAD
    for j in range(4):
        at = slice(j * q_rows, (j + 1) * q_rows)
        rows = dz[j][...]
        do_ref[at, :] = nt(rows, wo[...]).astype(BF16)
        dot_ref[:, at] = nt(wo[...], rows).astype(BF16)
    logs_ref[: 2 * q_rows, :] = logs_near[...]
    logs_ref[2 * q_rows :, :] = logs_far[...]
    dkt_sum[...] = jnp.zeros_like(dkt_sum)
    dvt_sum[...] = jnp.zeros_like(dvt_sum)

    def step(t, carry):
        at = pl.ds(pl.multiple_of(t * tile, tile), tile)
        q, do = q_ref[at, :], do_ref[at, :]
        q = (q.astype(F32) * 0.125).astype(BF16)
        qt, dot = qt_ref[:, at], dot_ref[:, at]
        logs = logs_ref[at, :]
        bias = score_bias(meta, t * tile, tile, q_rows, k_rows, causal)
        dq = jnp.zeros(q.shape, F32)
        for h in range(heads):
            mask = head_mask(q.shape, h)
            zero = jnp.zeros_like(q)
            probs = jnp.exp(nt(jnp.where(mask, q, zero), k_ref[...]) + bias - logs[:, h : h + 1])
            grad_probs = nt(jnp.where(mask, do, zero), v_ref[...])
            weighted = probs * grad_probs
            center = jnp.sum(weighted, axis=-1, keepdims=True)
            grad_scores = (weighted - probs * center).astype(BF16)
            feats = slice(h * HEAD, (h + 1) * HEAD)
            dvt_sum[feats, :] += nn(dot[feats, :], probs.astype(BF16))
            dkt_sum[feats, :] += nn(qt[feats, :], grad_scores)
            dq = jnp.where(mask, nn(grad_scores, k_ref[...]), dq)
        dq_ref[at, :] = (dq * 0.125).astype(BF16)
        return carry

    lax.fori_loop(0, 4 * q_rows // tile, step, 0)
    dkt_ref[...] = (dkt_sum[...] * 0.125).astype(BF16)
    dvt_ref[...] = dvt_sum[...].astype(BF16)

    def query_part(j):
        return nn(dq_ref[j * q_rows : (j + 1) * q_rows, :], wq[...])

    def source_part(j):
        at = slice(j * k_rows, (j + 1) * k_rows)
        return tn(dkt_ref[:, at], wk[...]) + tn(dvt_ref[:, at], wv[...])

    parts = (query_part, source_part) if cross else ((lambda j: query_part(j) + source_part(j)),)
    for n, make in enumerate(parts):
        for j in range(4):
            outs[4 * n + j][...] = make(j).astype(outs[4 * n + j].dtype)


def attend_back(meta, dz, qt, attn_t, out_w, group, saved, q_rows, k_rows, causal, cross):
    q, k, v, logs_near, logs_far = saved
    dc = q.shape[1]
    tile = min(256, 4 * q_rows)

    def four(rows):
        return [((rows, D), F32), ((rows, D), BF16), ((rows, D), BF16), ((rows, D), BF16)]

    outs = call(
        functools.partial(attend_back_body, cross, causal, q_rows, k_rows, tile),
        [(meta, SCALARS)]
        + list(dz)
        + [(q, None), (qt, None), (k, None), (v, None), (logs_near, None), (logs_far, None)]
        + attn_weights(attn_t, group)
        + [out_weights(out_w)],
        [((4 * q_rows, dc), BF16), ((dc, 4 * k_rows), BF16), ((dc, 4 * k_rows), BF16)]
        + (four(q_rows) + four(k_rows) if cross else four(q_rows)),
        80 * q_rows * k_rows * D + 4 * D * dc * (4 * q_rows + 4 * k_rows),
        [
            pltpu.VMEM((4 * q_rows, dc), BF16),
            pltpu.VMEM((dc, 4 * q_rows), BF16),
            pltpu.VMEM((dc, 4 * k_rows), F32),
            pltpu.VMEM((dc, 4 * k_rows), F32),
            pltpu.VMEM((4 * q_rows, 128), F32),
        ],
        f"attend_back_{group}",
    )
    return outs[:3], outs[3:]


def attend_weights_body(cross, q_rows, k_rows, *refs):
    queries = refs[0:4]
    sources = refs[4:8] if cross else queries
    dq, dkt, dvt, *outs = refs[8:] if cross else refs[4:]
    gq = gk = gv = None
    for j in range(4):
        at, ak = slice(j * q_rows, (j + 1) * q_rows), slice(j * k_rows, (j + 1) * k_rows)
        x, y = queries[j][...], sources[j][...]
        a, b, c = tn(dq[at, :], x), nn(dkt[:, ak], y), nn(dvt[:, ak], y)
        gq, gk, gv = (a, b, c) if j == 0 else (gq + a, gk + b, gv + c)
    for ref, g in zip(outs, (gq, gk, gv)):
        ref[...] = g.astype(BF16)


def attend_weights(queries, sources, grads, name):
    cross = sources is not None
    dq, dkt, dvt = grads
    q_rows, k_rows, dc = dq.shape[0] // 4, dkt.shape[1] // 4, dq.shape[1]
    return call(
        functools.partial(attend_weights_body, cross, q_rows, k_rows),
        list(queries) + (list(sources) if cross else []) + [(dq, None), (dkt, None), (dvt, None)],
        [((dc, D), BF16)] * 3,
        0,
        name=name,
    )


def out_total(dz, near, far, q_rows):
    total = None
    for j, ref in enumerate(dz):
        mixed = (near, far)[j // 2][(j % 2) * q_rows : (j % 2 + 1) * q_rows, :]
        x = tn(ref[...], mixed)
        total = x if j == 0 else total + x
    return total


def out_weight_body(sizes, *refs):
    outs, scratch = refs[6 * len(sizes) : -1], refs[-1]
    s, rows = lax.axis_index("seq"), scratch.shape[2]
    for n, q_rows in enumerate(sizes):
        total = out_total(refs[6 * n : 6 * n + 4], refs[6 * n + 4], refs[6 * n + 5], q_rows)
        for t in range(4):
            scratch[s ^ t, n] = total[t * rows : (t + 1) * rows, :].astype(BF16)
    hand_out(scratch, outs)


def out_weight(groups, name):
    dc = D // 4
    ins, sizes = [], []
    for dz, near, far in groups:
        ins += list(dz) + [(near, None), (far, None)]
        sizes.append(near.shape[0] // 2)
    return call(
        functools.partial(out_weight_body, sizes),
        ins,
        sent_shapes((len(groups), dc, dc), BF16),
        0,
        [pltpu.VMEM((4, len(groups), dc, dc), BF16)],
        name,
    )


GELU_A, GELU_B = math.sqrt(2.0 / math.pi), 0.044715


def feed_forward_body(rows, x0, x1, wg, wu, wd, gate_ref, up_ref, hidden_ref, keep_ref, send_ref):
    for j, x_ref in enumerate((x0, x1)):
        at = slice(j * rows, (j + 1) * rows)
        x = x_ref[...]
        gate, up = nn(x, wg[...]), nn(x, wu[...])
        gate_ref[at, :] = gate
        up_ref[at, :] = up
        inner = jnp.tanh(GELU_A * (gate + GELU_B * (gate * gate * gate)))
        hidden_ref[at, :] = (0.5 * gate * (1.0 + inner) * up).astype(BF16)
        out = (keep_ref, send_ref)[j]
        out[...] = nn(hidden_ref[at, :], wd[...]).astype(out.dtype)


def feed_weights(inner_cols, outer_rows, which):
    fc = inner_cols.shape[1]
    return [
        (inner_cols, part((D, fc), 2 * which, 0)),
        (inner_cols, part((D, fc), 2 * which + 1, 0)),
        (outer_rows, part((fc, D), which, 0)),
    ]


def feed_forward(half, inner_cols, outer_rows, which, keep, name):
    rows, fc = half[0].shape[0], inner_cols.shape[1]
    return call(
        functools.partial(feed_forward_body, rows),
        plain(half) + feed_weights(inner_cols, outer_rows, which),
        [((2 * rows, fc), F32), ((2 * rows, fc), F32), ((2 * rows, fc), BF16), ((rows, D), keep), ((rows, D), BF16)],
        12 * rows * fc * D,
        name=name,
    )


def feed_back_body(rows, d0, d1, gate_ref, up_ref, wg, wu, wd, dgate_ref, dup_ref, keep_ref, send_ref):
    for j, d_ref in enumerate((d0, d1)):
        at = slice(j * rows, (j + 1) * rows)
        dh = nt(d_ref[...], wd[...])
        t, up = gate_ref[at, :], up_ref[at, :]
        square = t * t
        inner = jnp.tanh(GELU_A * t * (1.0 + GELU_B * square))
        slope = 0.5 * (1.0 + inner) + 0.5 * t * (1.0 - inner * inner) * (
            GELU_A * (1.0 + 3.0 * GELU_B * square)
        )
        dgate_ref[at, :] = (dh * up * slope).astype(BF16)
        dup_ref[at, :] = (dh * (0.5 * t * (1.0 + inner))).astype(BF16)
        out = (keep_ref, send_ref)[j]
        out[...] = (nt(dgate_ref[at, :], wg[...]) + nt(dup_ref[at, :], wu[...])).astype(out.dtype)


def feed_back(dz_half, gate, up, inner_cols, outer_rows, which, keep, name):
    rows, fc = gate.shape[0] // 2, inner_cols.shape[1]
    return call(
        functools.partial(feed_back_body, rows),
        list(dz_half) + [(gate, None), (up, None)] + feed_weights(inner_cols, outer_rows, which),
        [((2 * rows, fc), BF16), ((2 * rows, fc), BF16), ((rows, D), keep), ((rows, D), BF16)],
        12 * rows * fc * D,
        name=name,
    )


def feed_weight_body(rows, packed, *refs):
    xs, dzs = refs[0:4], refs[4:8]
    dg, du, hid = refs[8:10], refs[10:12], refs[12:14]
    outs = refs[14:]
    gate = up = down = None
    for j in range(4):
        at = slice((j % 2) * rows, (j % 2 + 1) * rows)
        x = xs[j][...]
        a, b = tn(x, dg[j // 2][at, :]), tn(x, du[j // 2][at, :])
        c = tn(hid[j // 2][at, :], dzs[j][...])
        gate, up, down = (a, b, c) if j == 0 else (gate + a, up + b, down + c)
    fc = gate.shape[1]
    if not packed:
        outs[0][:D, :] = gate.astype(BF16)
        outs[0][D:, :] = up.astype(BF16)
        outs[1][...] = down.astype(BF16)
        return
    out = refs[-1]
    height = out.shape[1]
    for n, grad in enumerate((gate, up)):
        for k in range(2):
            out[2 * n + k, :, :fc] = grad[k * height : (k + 1) * height, :].astype(BF16)
    short = fc // 4
    for q in range(4):
        for g in range(D // 128):
            piece = down[q * short : (q + 1) * short, g * 128 : (g + 1) * 128].astype(BF16)
            r, c = g % 3 * short, fc + g // 3 * 128
            out[q, r : r + short, c : c + 128] = piece
    y = lax.axis_index("batch") % 2
    for i in range(2):
        outs[0][i] = out[2 * i + y]
        outs[1][i] = out[2 * i + 1 - y]


def feed_weight(xs, dzs, dgate, dup, hidden, packed, name):
    rows, fc = xs[0].shape[0], dgate[0].shape[1]
    return call(
        functools.partial(feed_weight_body, rows, packed),
        plain(xs) + list(dzs) + plain((*dgate, *dup, *hidden)),
        [((2, D // 2, fc + 256), BF16)] * 2 if packed else [((2 * D, fc), BF16), ((fc, D), BF16)],
        24 * rows * fc * D,
        [pltpu.VMEM((4, D // 2, fc + 256), BF16)] if packed else [],
        name,
    )


def send_some(mine):
    return [mine[0], seq_swap(mine[1], 1), seq_swap(mine[2], 2)]


def send_rest(got, *after):
    return [*got, seq_swap(tie(got[2], got[1], *after), 1)]


def send_blocks(mine):
    return send_rest(send_some(mine))


def place(scratch, refs, s):
    for j, ref in enumerate(refs):
        scratch[s ^ j] = ref[...] if j < 2 else ref[j - 2]


def hand_out(scratch, outs):
    outs[0][...] = scratch[0]
    outs[1][...] = scratch[1]
    outs[2][0] = scratch[2]
    outs[2][1] = scratch[3]


def sent_shapes(shape, dtype):
    return [(shape, dtype), (shape, dtype), ((2,) + shape, dtype)]


def head_pack_body(ar, gr, lines, attn_ref, gain_ref, inner_ref, *refs):
    outs, scratch = refs[0:3], refs[3]
    s = lax.axis_index("seq")
    ir, width = inner_ref.shape[0], scratch.shape[2]
    dc, room, short = D // 4, width - ar, ir // 3
    turned = attn_ref[...].T
    gains = jnp.concatenate([gain_ref[...], jnp.zeros((1, lines * room - gr), F32)], axis=1)
    for t in range(4):
        at = s ^ t
        scratch[at, :dc, ar:] = jnp.zeros((dc, room), BF16)
        scratch[at, :dc, :ar] = turned[t * dc : (t + 1) * dc, :].astype(BF16)
        for n in range(lines):
            scratch[at, n : n + 1, ar:] = gains[:, n * room : (n + 1) * room].astype(BF16)
        for q in range(4):
            low = (4 * q + t) * 128
            piece = inner_ref[:, low : low + 128].astype(BF16)
            if q < 3:
                scratch[at, dc : dc + ir, q * 128 : (q + 1) * 128] = piece
            else:
                for n in range(3):
                    scratch[at, dc + ir :, n * 128 : (n + 1) * 128] = piece[n * short : (n + 1) * short, :]
    hand_out(scratch, outs)


def head_unpack_body(ar, gr, lines, ir, *refs):
    ins, outer_ref = refs[0:4], refs[4]
    attn_ref, feed_ref, scratch = refs[5:8]
    place(scratch, ins, lax.axis_index("seq"))
    dc, room, short, orow = D // 4, scratch.shape[2] - ar, ir // 3, outer_ref.shape[0]
    pieces = []
    for k in range(4):
        attn_ref[:dc, k * ar : (k + 1) * ar] = scratch[k, :dc, :ar]
        rows = slice(k * ir, (k + 1) * ir)
        feed_ref[rows, :384] = scratch[k, dc : dc + ir, :]
        for n in range(3):
            feed_ref[k * ir + n * short : k * ir + (n + 1) * short, 384:512] = scratch[
                k, dc + ir :, n * 128 : (n + 1) * 128
            ]
        pieces += [scratch[k, n : n + 1, ar : ar + min(room, gr - n * room)].astype(F32) for n in range(lines)]
    for g in range(D // 128):
        r, c = g % 3 * orow, 512 + g // 3 * 128
        feed_ref[r : r + orow, c : c + 128] = outer_ref[:, g * 128 : (g + 1) * 128].astype(BF16)
    pieces.append(jnp.zeros((1, attn_ref.shape[1] - 4 * gr), F32))
    line = jnp.concatenate(pieces, axis=1)
    fill = jnp.zeros((attn_ref.shape[0] - dc - 1, line.shape[1]), F32)
    attn_ref[dc:, :] = jnp.concatenate([line, fill], axis=0).astype(BF16)


def head_exchange(attn_master, inner_master, outer_master, gain_master):
    ar, dc, gr = attn_master.shape[0], D // 4, gain_master.shape[0]
    ir = inner_master.shape[0]
    width = (ar // 128 + 1) * 128
    lines = -(-gr // (width - ar))
    tall = dc + ir + ir // 3
    scratch = [pltpu.VMEM((4, tall, width), BF16)]
    outs = call(
        functools.partial(head_pack_body, ar, gr, lines),
        plain([attn_master, gain_master[None], inner_master]),
        sent_shapes((tall, width), BF16),
        0,
        scratch,
        "head_pack",
    )
    return call(
        functools.partial(head_unpack_body, ar, gr, lines, ir),
        plain(send_blocks(outs) + [outer_master]),
        [((dc + 16, 4 * ar), BF16), ((4 * ir, D), BF16)],
        0,
        scratch,
        "head_unpack",
    )


def turn_pack_body(count, *refs):
    ins, outs, scratch = refs[:count], refs[count : count + 3], refs[count + 3]
    s = lax.axis_index("seq")
    dc = scratch.shape[2]
    for t in range(4):
        for g in range(count):
            scratch[s ^ t, g] = ins[g][:, t * dc : (t + 1) * dc].T
    hand_out(scratch, outs)


def turn_pack(ins, name):
    count, dc = len(ins), D // 4
    return call(
        functools.partial(turn_pack_body, count),
        ins,
        sent_shapes((count, dc, dc), BF16),
        0,
        [pltpu.VMEM((4, count, dc, dc), BF16)],
        name,
    )


def lanes_unpack_body(*refs):
    ins, out, scratch = refs[:4], refs[4], refs[5]
    place(scratch, ins, lax.axis_index("seq"))
    width = scratch.shape[3]
    for k in range(4):
        for g in range(scratch.shape[1]):
            out[g, :, k * width : (k + 1) * width] = scratch[k, g]


def lanes_unpack(got, name):
    shape = got[0].shape
    return call(
        lanes_unpack_body,
        plain(got),
        [(shape[:2] + (4 * shape[2],), BF16)],
        0,
        [pltpu.VMEM((4,) + shape, BF16)],
        name,
    )[0]


def tail_pack_body(gr, total_ref, *refs):
    outs, scratch = refs[:3], refs[3]
    s, width = lax.axis_index("seq"), scratch.shape[2]
    dc = D // 4
    for t in range(4):
        scratch[s ^ t, :dc] = total_ref[:dc, t * width : (t + 1) * width].astype(BF16)
        lines = [total_ref[dc + e : dc + e + 1, t * gr : (t + 1) * gr] for e in range(2)]
        lines = jnp.concatenate(lines + [jnp.zeros((1, width - 2 * gr), F32)] * (width > 2 * gr), axis=1)
        scratch[s ^ t, dc:] = jnp.concatenate([lines, jnp.zeros((15, width), F32)], axis=0).astype(BF16)
    hand_out(scratch, outs)


def tail_unpack_body(gr, *refs):
    ins, (out, kept_ref, sent_ref, scratch) = refs[:4], refs[4:]
    place(scratch, ins, lax.axis_index("seq"))
    dc = D // 4
    lines = None
    for k in range(4):
        out[:, k * dc : (k + 1) * dc] = scratch[k, :dc].astype(F32).T
        line = scratch[k, dc:].astype(F32)[:1]
        lines = line if k == 0 else lines + line
    halves = lines[:, :gr], lines[:, gr : 2 * gr]
    first = lax.axis_index("batch") % 2 == 0
    kept_ref[...] = jnp.where(first, halves[0], halves[1])
    sent_ref[...] = jnp.where(first, halves[1], halves[0])


def feed_pack_body(total_ref, *refs):
    outs, outer_ref, scratch = refs[:3], refs[3], refs[4]
    s, (rows, fc), orow = lax.axis_index("seq"), scratch.shape[1:], outer_ref.shape[0]
    for t in range(4):
        scratch[s ^ t] = total_ref[t * rows : (t + 1) * rows, :fc].astype(BF16)
    hand_out(scratch, outs)
    for g in range(D // 128):
        r, c = g % 3 * orow, fc + g // 3 * 128
        outer_ref[:, g * 128 : (g + 1) * 128] = total_ref[r : r + orow, c : c + 128]


def feed_pack(total, ir, fc, orow):
    outs = call(
        feed_pack_body,
        plain([total]),
        sent_shapes((ir, fc), BF16) + [((orow, D), F32)],
        0,
        [pltpu.VMEM((4, ir, fc), BF16)],
        "feed_pack",
    )
    return outs[:3], outs[3]


def feed_unpack_body(*refs):
    ins, out, scratch = refs[:4], refs[4], refs[5]
    place(scratch, ins, lax.axis_index("seq"))
    for k in range(4):
        for q in range(4):
            low = (4 * q + k) * 128
            out[:, low : low + 128] = scratch[k, :, q * 128 : (q + 1) * 128].astype(F32)


def feed_unpack(got):
    ir, fc = got[0].shape
    return call(
        feed_unpack_body, plain(got), [((ir, 4 * fc), F32)], 0, [pltpu.VMEM((4, ir, fc), BF16)], "feed_unpack"
    )[0]


def spread_body(*refs):
    out_ref = refs[6]
    count, width = out_ref.shape[0], out_ref.shape[2]
    per = 6 * D // count
    line = jnp.concatenate([x[...] for x in refs[:6]], axis=1)
    for n in range(count):
        piece = line[:, n * per : (n + 1) * per]
        out_ref[n] = jnp.concatenate([piece, jnp.zeros((1, width - per), F32)], axis=1)


def spread(rows, count, width):
    return call(spread_body, plain(rows), [((count, 1, width), F32)], 0, name="spread")[0]


def tail_pack(total, ar, gr):
    if ar % 16:
        return [total, total]
    shape = (D // 4 + 16, ar)
    mine = call(
        functools.partial(tail_pack_body, gr),
        plain([total]),
        sent_shapes(shape, BF16),
        0,
        [pltpu.VMEM((4,) + shape, BF16)],
        "tail_pack",
    )
    return send_some(mine) + [mine[1]]


def tail_unpack(mine, s, ar, gr, now, *after):
    dc = D // 4
    if ar % 16:
        got = seq_exchange(mine[0][:dc].astype(BF16).reshape(dc, 4, ar).swapaxes(0, 1), s)
        lines = lax.dynamic_slice_in_dim(sum_seq(mine[0][dc : dc + 2]), s * gr, gr, axis=1)
        y = lax.axis_index("batch") % 2
        pair = [lax.dynamic_slice_in_dim(lines, i, 1, axis=0) for i in (y, 1 - y)]
        return (got.reshape(4 * dc, ar).T.astype(F32), *pair)
    got = send_rest(mine[:3], *after)
    return call(
        functools.partial(tail_unpack_body, gr),
        plain([now(got[0]), *got[1:]]),
        [((ar, 4 * dc), F32), ((1, gr), F32), ((1, gr), F32)],
        0,
        [pltpu.VMEM((4, dc + 16, ar), BF16)],
        "tail_unpack",
    )


def split_lanes(scratch, pieces):
    width = scratch.shape[2]
    for n, piece in enumerate(pieces):
        for low in range(n * D, (n + 1) * D, D // 2):
            to = low % width
            scratch[low // width, :, to : to + D // 2] = piece[:, low - n * D : low - n * D + D // 2]


def part_pack_body(positions, *refs):
    count = len(positions)
    ins = refs[4 : 4 + 2 * count]
    kept_ref, sent_ref, squares, scratch = refs[4 + 2 * count :]
    y = lax.axis_index("batch") % 2
    place(squares, refs[:4], lax.axis_index("seq"))
    for n, position in enumerate(positions):
        pieces = [x[...] for x in ins[2 * n : 2 * n + 2]]
        pieces.insert(position, jnp.concatenate([squares[k, n] for k in range(4)], axis=1))
        split_lanes(scratch, pieces)
        kept_ref[n] = scratch[y]
        sent_ref[n] = scratch[1 - y]


def attn_parts(got, parts, width, name):
    dc = D // 4
    if width % 128 or lax.axis_size("batch") != 8:
        joined = []
        matrices = None if got is None else lanes_unpack(got, name)
        for n, (others, position) in enumerate(parts):
            pieces = list(others)
            if got is not None:
                pieces.insert(position, matrices[n])
            joined.append(jnp.concatenate(pieces, axis=1))
        joined = jnp.concatenate(joined, axis=1)
        return pair_blocks(joined.reshape(dc, -1, width).swapaxes(0, 1))
    return call(
        functools.partial(part_pack_body, [position for _, position in parts]),
        plain([*got, *(x for others, _ in parts for x in others)]),
        [((len(parts), dc, width), BF16)] * 2,
        0,
        [pltpu.VMEM((4, len(parts), dc, dc), BF16), pltpu.VMEM((2, dc, width), BF16)],
        name,
    )


def self_part_body(rows, *refs):
    x = refs[0:4]
    dq, dkt, dvt, kept_ref, sent_ref, scratch = refs[4:10]
    gq = gk = gv = None
    for j in range(4):
        at = slice(j * rows, (j + 1) * rows)
        y = x[j][...]
        a, b, c = tn(dq[at, :], y), nn(dkt[:, at], y), nn(dvt[:, at], y)
        gq, gk, gv = (a, b, c) if j == 0 else (gq + a, gk + b, gv + c)
    split_lanes(scratch, [g.astype(BF16) for g in (gq, gk, gv)])
    y = lax.axis_index("batch") % 2
    kept_ref[0] = scratch[y]
    sent_ref[0] = scratch[1 - y]


def self_part(rows, grads, width, name):
    dq, dkt, dvt = grads
    per, dc = dq.shape[0] // 4, dq.shape[1]
    if width % 128 or lax.axis_size("batch") != 8:
        gq, gk, gv = (g.reshape(4, per, dc) for g in (dq, dkt.T, dvt.T))
        made = [
            sum(tn(g[j], x.reshape(4, per, D)[j]) for j, (x, _) in enumerate(rows)).astype(BF16)
            for g in (gq, gk, gv)
        ]
        return attn_parts(None, [(made, 0)], width, name)
    return call(
        functools.partial(self_part_body, per),
        list(rows) + plain([dq, dkt, dvt]),
        [((1, dc, width), BF16)] * 2,
        0,
        [pltpu.VMEM((2, dc, width), BF16)],
        name,
    )


KINDS = ((D, 0), (D, 12), (FF, 16), (D, 18))


def group_mask(count, kind):
    per_group, offset = KINDS[kind]
    axis = 1 if kind < 3 else 0
    shape = (count, 128) if kind < 3 else (128, count)
    at = lax.axis_index(("batch", "seq")) * count + lax.broadcasted_iota(jnp.int32, shape, 1 - axis)
    low = (lax.broadcasted_iota(jnp.int32, shape, axis) - offset) * per_group
    return (at >= low) & (at < low + per_group) & (low >= 0)


def diagonal():
    return lax.broadcasted_iota(jnp.int32, (128, 128), 0) == lax.broadcasted_iota(jnp.int32, (128, 128), 1)


def by_group(values, kind):
    if kind == 3:
        mask = group_mask(values.shape[1], kind)
        column = jnp.sum(jnp.where(mask, values * values, 0.0), axis=1, keepdims=True)
        return jnp.sum(jnp.where(diagonal(), column, 0.0), axis=0, keepdims=True)
    squares = jnp.sum(values * values, axis=1, keepdims=True)
    return jnp.sum(jnp.where(group_mask(values.shape[0], kind), squares, 0.0), axis=0, keepdims=True)


def of_group(row, count, kind):
    if kind == 3:
        column = jnp.sum(jnp.where(diagonal(), row, 0.0), axis=1, keepdims=True)
        return jnp.sum(jnp.where(group_mask(count, kind), column, 0.0), axis=0, keepdims=True)
    return jnp.sum(jnp.where(group_mask(count, kind), row, 0.0), axis=1, keepdims=True)


def square_sums_body(*refs):
    total = by_group(refs[0][...], 0)
    for kind in range(1, 4):
        total = total + by_group(refs[kind][...], kind)
    refs[4][...] = total


def square_sums(masters):
    return call(square_sums_body, plain(masters), [((1, 128), F32)], 0, name="square_sums")[0]


def adam_body(kind, w_ref, m_ref, v_ref, g_ref, first_ref, second_ref, update_ref, sums_ref):
    gradient = g_ref[...]
    correction = 1.0 - 0.5**STEP
    first = 0.5 * m_ref[...] + 0.5 * gradient
    second = 0.5 * v_ref[...] + 0.5 * gradient * gradient
    update = first / correction / (jnp.sqrt(second / correction) + adam_eps)
    update = update + (decay_weight if kind < 3 else 0.0) * w_ref[...]
    first_ref[...] = first
    second_ref[...] = second
    update_ref[...] = update
    sums_ref[...] = by_group(update, kind)


def adam(kind, w, m, v, g):
    return call(
        functools.partial(adam_body, kind),
        plain([w, m, v, g]),
        [(w.shape, F32)] * 3 + [((1, 128), F32)],
        0,
        name=f"adam_{kind}",
    )


def lamb_body(*refs):
    weight_norms, update_norms = jnp.sqrt(refs[0][:, :128]), jnp.sqrt(refs[0][:, 128:])
    ratio = weight_norms / (update_norms + 1e-06)
    masters, updates, news, copies = (refs[1 + 4 * n : 5 + 4 * n] for n in range(4))
    for kind in range(4):
        w = masters[kind]
        scale = of_group(ratio, w.shape[1] if kind == 3 else w.shape[0], kind)
        new = w[...] - lamb_rate * scale * updates[kind][...]
        if kind == 3:
            new = new[0]
        news[kind][...] = new
        copies[kind][...] = new.astype(BF16)
    refs[17][...] = weight_norms[0, :24]
    refs[18][...] = update_norms[0, :24]


def lamb(squares, masters, updates):
    shapes = [w.shape for w in masters[:3]] + [masters[3].shape[1:]]
    return call(
        lamb_body,
        plain([squares, *masters, *updates]),
        [(s, F32) for s in shapes] + [(s, BF16) for s in shapes] + [((24,), F32)] * 2,
        0,
        name="lamb",
    )


def per_device(
    encoder_layer_input,
    decoder_layer_input,
    cotangent,
    encoder_used_lengths,
    decoder_used_lengths,
    attn_master,
    inner_master,
    outer_master,
    gain_master,
    attn_first,
    inner_first,
    outer_first,
    gain_first,
    attn_second,
    inner_second,
    outer_second,
    gain_second,
):
    ns, nb = lax.axis_size("seq"), lax.axis_size("batch")
    s, b = lax.axis_index("seq"), lax.axis_index("batch")
    ar, ir, orow = attn_master.shape[0], inner_master.shape[0], outer_master.shape[0]
    dc, fc = D // ns, FF // ns
    cuts = FF // (ns * orow)

    gr = gain_master.shape[0]
    packed = nb == 8 and ar % 16 == 0 and 3 * orow == ns * ir and cuts == 4
    clock = Clock()
    now, mark = clock.now, clock.mark
    masters = [attn_master, inner_master, outer_master, gain_master[None]]
    if packed:
        attn_mine, feed_mine = head_exchange(attn_master, inner_master, outer_master, gain_master)
        feeds_mine = [feed_mine]
    else:
        width = (ar // 128 + 1) * 128
        lines = -(-gr // (width - ar))
        corner = jnp.pad(gain_master.astype(BF16), (0, lines * (width - ar) - gr)).reshape(lines, width - ar)
        corner = jnp.broadcast_to(jnp.pad(corner, ((0, dc - lines), (0, 0))), (ns, dc, width - ar))
        attn_low = attn_master.astype(BF16).T.reshape(ns, dc, ar)
        got = seq_exchange(jnp.concatenate([attn_low, corner], axis=2), s)
        attn_mine = got[:, :, :ar].swapaxes(0, 1).reshape(dc, ns * ar)
        gains_mine = got[:, :lines, ar:].reshape(ns, -1)[:, :gr].reshape(1, ns * gr)
        attn_mine = jnp.concatenate([attn_mine, jnp.pad(gains_mine, ((0, 15), (0, ns * (ar - gr))))])
        inner_low = inner_master.astype(BF16).reshape(ir, cuts, ns, orow).transpose(2, 0, 1, 3)
        inner_mine = seq_exchange(inner_low.reshape(ns, ir, fc), s).reshape(ns * ir, fc)
        feeds_mine = [inner_mine, outer_master.astype(BF16)]
    attn_got = None
    attn_ring = ring_gather(attn_mine)
    next(attn_ring)
    while not isinstance(attn_got, list):
        attn_last, attn_got = attn_got, attn_ring.send(None)
    squares = square_sums(masters)
    attn_t = gathered_lanes([attn_got[0], *(tie(x, squares) for x in attn_got[1:])], "gather_attn")
    feed_rings = [ring_gather(x) for x in feeds_mine]
    for x in feed_rings:
        next(x)
        x.send(attn_last)

    def feed_step():
        for x in feed_rings:
            clock.step(x)

    gains = attn_t[dc].reshape(nb, ns * ar)[:, : ns * gr].reshape(6, D).astype(F32)
    gain = [gains[i : i + 1] for i in range(6)]
    out_mine = turn_pack([(attn_t, part((dc, D), 0, 3))], "out_pack_0")
    out_got = send_blocks(out_mine)
    out_mine = turn_pack(
        [(tie(attn_t, out_mine[1]), part((dc, D), 0, 7)), (attn_t, part((dc, D), 0, 11))], "out_pack_1"
    )
    rest_got = send_some(out_mine)

    enc_in, dec_in = encoder_layer_input[0], decoder_layer_input[0]
    er, dr = enc_in.shape[0], dec_in.shape[0]
    enc_meta = jnp.stack([s, encoder_used_lengths[0]]).astype(jnp.int32)
    dec_meta = jnp.stack([s, decoder_used_lengths[0]]).astype(jnp.int32)
    alive = (s * dr + jnp.arange(dr, dtype=jnp.int32)) < decoder_used_lengths[0]
    seed = jnp.where(alive[:, None], cotangent[0], jnp.zeros_like(cotangent[0]))
    blocks = gather_blocks(jnp.concatenate([enc_in, dec_in, seed]))
    enc_blocks = [(x, part((er, D), 0, 0)) for x in blocks]
    dec_blocks = [(x, part((dr, D), er // dr, 0)) for x in blocks]
    seed_blocks = [(x, part((dr, D), er // dr + 1, 0)) for x in blocks]

    def quarters(rows):
        return [(rows, part((rows.shape[0] // 4, D), j, 0)) for j in range(4)]

    mark(out_mine[1])
    feed_step()
    rows_a, q0, k0, v0, logs_far0, mixed_far0 = attend_far(
        tie(now(enc_meta), *out_got[1:]), enc_blocks, None, attn_t, None, 0, False, gain[0]
    )
    mark([mixed_far0, rest_got[2]])
    rest_got = send_rest(rest_got, mixed_far0)
    out_w = lanes_unpack([now(out_got[0]), *out_got[1:]], "out_unpack_0")
    kf, sf = project(mixed_far0, (out_w, 0), "project_far_0")
    mark(sf)
    feed_step()
    far = mark(far_payload(kf, now(sf)))
    x_enc = seq_swap(far, 2)
    logs_near0, mixed_near0, kn_enc, sn = attend_near(enc_meta, now(q0), k0, v0, (out_w, 0), 0, False)
    mark(sn)
    c_enc = seq_swap(sn, 1)
    out_rest = lanes_unpack([now(rest_got[0]), *rest_got[1:]], "out_unpack_1")
    mark(out_rest)
    rows_c, q1, k1, v1, logs_far1, mixed_far1, kf, sf = attend_far(
        now(dec_meta), dec_blocks, None, attn_t, (out_rest, 0), 1, True, gain[3]
    )
    mark(sf)
    feed_step()
    enc_mid, norm_b = close(now(kn_enc), c_enc, x_enc, enc_in, gain[1], "close_enc_attn")
    mark(norm_b)
    rows_b = gather_blocks(norm_b)
    x_self = seq_swap(mark(far_payload(kf, now(sf))), 2)
    logs_near1, mixed_near1, kn, sn = attend_near(dec_meta, now(q1), k1, v1, (out_rest, 0), 1, True)
    mark(sn)
    c_self = seq_swap(sn, 1)
    feed_got = [clock.finish(x) for x in feed_rings]
    if packed:
        inner_cols, outer_rows = gathered_feeds(feed_got[0], orow, "gather_feeds")
    else:
        inner_cols = gathered_rows(feed_got[0], "gather_inner")
        outer_rows = gathered_rows(feed_got[1], "gather_outer")
    inner_cols, outer_rows = inner_cols.reshape(4 * D, fc), outer_rows.reshape(2 * fc, D)
    eg1, eu1, eh1, kf, sf = feed_forward((now(rows_b[2]), rows_b[3]), inner_cols, outer_rows, 0, BF16, "enc_feed_far")
    far = mark(far_payload(kf, sf))
    x_enc = seq_swap(far, 2)
    eg0, eu0, eh0, kn_enc, sn = feed_forward((now(rows_b[0]), rows_b[1]), inner_cols, outer_rows, 0, F32, "enc_feed_near")
    mark(sn)
    c_enc = seq_swap(sn, 1)
    dec_mid, norm_d = close(now(kn), c_self, x_self, dec_in, gain[4], "close_self")
    mark(norm_d)
    enc_out, norm_e = close(now(kn_enc), c_enc, x_enc, enc_mid, gain[2], "close_enc_feed")
    mark(norm_e)
    rows_e = gather_blocks(norm_e)
    q0t, q1t = now(q0).T, now(q1).T
    mark(q1t)
    rows_d = gather_blocks(now(norm_d))
    q2, k2, v2, logs_far2, mixed_far2, kf, sf = attend_far(
        now(enc_meta), plain(rows_d), plain(rows_e), attn_t, (out_rest, 1), 2, False
    )
    far = mark(far_payload(kf, sf))
    x_dec = seq_swap(far, 2)
    logs_near2, mixed_near2, kn, sn = attend_near(enc_meta, now(q2), k2, v2, (out_rest, 1), 2, False)
    mark(sn)
    dec_late, norm_f = close(now(kn), seq_swap(tie(sn, x_dec), 1), x_dec, dec_mid, gain[5], "close_cross")
    mark(norm_f)
    rows_f = gather_blocks(norm_f)
    dg0, du0, dh0, kn_out, sn_out = feed_forward(
        (now(rows_f[0]), rows_f[1]), inner_cols, outer_rows, 1, F32, "dec_feed_near"
    )
    mark(dh0)
    a0, b0, kn_dec, sn_dec = feed_back(
        seed_blocks[:2], now(dg0), du0, inner_cols, outer_rows, 1, F32, "dec_feed_back_near"
    )
    mark(sn_dec)
    c_dec = seq_swap(sn_dec, 1)
    dg1, du1, dh1, kf_out, sf_out = feed_forward(
        (now(rows_f[2]), rows_f[3]), inner_cols, outer_rows, 1, BF16, "dec_feed_far"
    )
    mark(dh1)
    a1, b1, kf, sf = feed_back(seed_blocks[2:], now(dg1), du1, inner_cols, outer_rows, 1, BF16, "dec_feed_back_far")

    far = mark(far_payload(kf, sf))
    x_dec = seq_swap(far, 2)
    dec_feed = feed_weight(
        rows_f, seed_blocks, (now(a0), a1), (b0, b1), (dh0, dh1), packed, "dec_feed_weight"
    )
    mark(dec_feed[-1])
    up_five, low, gain_five = close_back(now(kn_dec), c_dec, x_dec, dec_late, gain[5], seed, "back_dec_feed")
    mark(low)
    dz_cross = plain(gather_blocks(low))
    half = nb // 2
    feed_shapes = [(ns * ir, fc), (orow, D)]

    def pair_send(kept, sent):
        return kept, batch_swap(mark(sent), 1)

    def feed_parts(grads):
        if packed:
            return [pair_send(*grads)]
        blocks = [now(x).reshape((half,) + shape) for x, shape in zip(grads, feed_shapes)]
        return [pair_send(*pair_blocks(x)) for x in blocks]

    dec_parts = feed_parts(dec_feed)
    far_out = mark(far_payload(kf_out, sf_out))

    q2t = mark(now(q2).T)
    out_sent = out_weight([(dz_cross, now(mixed_near2), mixed_far2)], "cross_out_weight")
    mark(out_sent[1])
    out_got = send_blocks(out_sent)
    x_out = seq_swap(tie(far_out, out_sent[1]), 2)
    c_out = seq_swap(tie(sn_out, out_sent[1]), 1)
    decoder_layer_output = (dec_late + kn_out + c_out.astype(F32) + x_out.astype(F32)).astype(BF16)
    cross_d, outs = attend_back(
        now(enc_meta), dz_cross, q2t, attn_t, (out_rest, 1), 2, (q2, k2, v2, logs_near2, logs_far2), dr, er, False, True
    )
    far = mark(far_payload(outs[6], tie(outs[7], x_out, c_out, out_got[2])))
    x_enc, c_enc = seq_swap(far, 2), seq_swap(now(outs[5]), 1)
    c_far, c_dec = seq_swap(now(outs[3]), 1), seq_swap(now(outs[1]), 1)
    kf_dec, kn_dec = outs[2], outs[0]
    cross_w = attend_weights(plain(rows_d), plain(rows_e), (now(cross_d[0]), *cross_d[1:]), "cross_weights")
    mark(cross_w[0])
    three = attn_parts([now(out_got[0]), *out_got[1:]], [(cross_w[1:], 2)], ns * ar, "part_three")
    mark(three[1])
    up_two, low, gain_two = close_back(now(outs[4]), c_enc, x_enc, enc_out, gain[2], None, "back_encoded")
    mark(low)
    dz = gather_blocks(low)
    far_dec = mark(add_low(kf_dec, now(c_far)))
    part_three = (three[0], batch_swap(three[1], 1))
    mark([far_dec] + [got for _, got in dec_parts])
    a0, b0, kn_enc, sn = feed_back(plain(dz[:2]), now(eg0), eu0, inner_cols, outer_rows, 0, F32, "enc_feed_back_near")
    mark(sn)
    c_enc = seq_swap(sn, 1)
    x_dec = seq_swap(tie(far_dec, dz[2], sn), 2)
    mark([sn, part_three[1]])
    dz = plain(dz)
    a1, b1, kf, sf = feed_back(dz[2:], now(eg1), eu1, inner_cols, outer_rows, 0, BF16, "enc_feed_back_far")
    far = mark(far_payload(kf, tie(sf, x_dec)))
    x_enc = seq_swap(far, 2)
    enc_feed = feed_weight(
        rows_b, dz, (now(a0), a1), (b0, b1), (eh0, eh1), packed, "enc_feed_weight"
    )
    mark(enc_feed[-1])
    enc_parts = feed_parts(enc_feed)
    up_four, low_self, gain_four = close_back(now(kn_dec), c_dec, x_dec, dec_mid, gain[4], up_five, "back_cross")
    mark(low_self)
    dz_self = plain(gather_blocks(low_self))
    up_one, low, gain_one = close_back(now(kn_enc), c_enc, x_enc, enc_mid, gain[1], up_two, "back_enc_feed")
    mark(low)
    dz_enc = gather_blocks(low)
    self_d, outs = attend_back(
        now(dec_meta), dz_self, q1t, attn_t, (out_rest, 0), 1, (q1, k1, v1, logs_near1, logs_far1), dr, dr, True, False
    )
    mark(outs[3])
    self_w = attend_weights(quarters(rows_c), None, (now(self_d[0]), *self_d[1:]), "self_weights")
    mark(self_w[0])
    flight = []
    feeds = [ring_reduce([e, d], "feed_hop", None, flight) for e, d in zip(enc_parts, dec_parts)]
    for x in feeds:
        next(x)
    kn_self, c_self = outs[0], seq_swap(tie(outs[1], dz_enc[2]), 1)
    sf_self = seq_swap(tie(outs[3], dz_enc[2]), 1)
    dz_enc = plain(dz_enc)
    out_late = out_weight(
        [(dz_enc, now(mixed_near0), mixed_far0), (dz_self, mixed_near1, mixed_far1)], "late_out_weight"
    )
    mark(out_late[1])
    got_late = send_blocks(out_late)
    x_self = seq_swap(mark(add_low(outs[2], now(sf_self))), 2)
    for x in feeds:
        clock.step(x)
    enc_d, outs = attend_back(
        now(enc_meta), dz_enc, q0t, attn_t, (out_w, 0), 0, (q0, k0, v0, logs_near0, logs_far0), er, er, False, False
    )
    far = mark(far_payload(outs[2], tie(outs[3], x_self, got_late[2], *flight)))
    x_enc, c_enc = seq_swap(far, 2), seq_swap(now(outs[1]), 1)
    part_zero = pair_send(
        *self_part(quarters(rows_a), (now(enc_d[0]), *enc_d[1:]), ns * ar, "part_zero")
    )
    part_middle = pair_send(
        *attn_parts(
            [now(got_late[0]), *got_late[1:]],
            [(self_w[:2], 0), ((self_w[2], cross_w[0]), 1)],
            ns * ar,
            "part_middle",
        )
    )
    for x in feeds:
        clock.step(x)
    decoder_input_gradient, _, gain_three = close_back(
        now(kn_self), c_self, x_self, dec_in, gain[3], up_four, "back_self"
    )
    mark(gain_three)
    encoder_input_gradient, _, gain_zero = close_back(
        now(outs[0]), c_enc, x_enc, enc_in, gain[0], up_one, "back_enc_attn"
    )
    mark(gain_zero)

    gain_lines = spread(
        [now(gain_zero), gain_one, gain_two, gain_three, gain_four, gain_five], nb, ns * ar
    )
    mark(gain_lines)
    last_ring = ring_reduce([part_zero, part_middle, part_three], "attn_hop", gain_lines)
    next(last_ring)
    clock.step(last_ring)
    for x in feeds:
        clock.step(x)
    clock.step(last_ring)
    feeds_done = [clock.finish(x)[0] for x in feeds]
    clock.step(last_ring)
    if packed:
        feed_sent, outer_grad = feed_pack(mark(feeds_done[0]), ir, fc, orow)
        mark(feed_sent[1])
        feed_got = send_blocks(feed_sent)
    else:
        inner_part, outer_grad = feeds_done
        inner_part = mark(now(inner_part).astype(BF16).reshape(ns, ir, fc))
        inner_part = seq_exchange(inner_part, s)
    outer_new = adam(2, outer_master, outer_first, outer_second, now(outer_grad))
    mark(outer_new[3])
    (attn_sum,) = clock.finish(last_ring)
    mine = tail_pack(mark(attn_sum), ar, gr)
    if packed:
        mark(mine[1])
        inner_grad = feed_unpack([now(feed_got[0]), *feed_got[1:]])
    else:
        inner_grad = inner_part.reshape(ns, ir, cuts, orow).transpose(1, 2, 0, 3).reshape(ir, FF).astype(F32)
    inner_new = adam(1, inner_master, inner_first, inner_second, mark(inner_grad))
    mark(inner_new[3])
    attn_grad, gain_kept, gain_sent = tail_unpack(mine, s, ar, gr, now, clock.last)
    gain_grad = gain_kept + batch_swap(gain_sent, 1)
    attn_new = adam(0, attn_master, attn_first, attn_second, attn_grad)
    gain_new = adam(3, masters[3], gain_first[None], gain_second[None], tie(gain_grad, attn_new[3]))
    results = (attn_new, inner_new, outer_new, gain_new)
    all_squares = sum_all(jnp.concatenate([squares, sum(x[3] for x in results)], axis=1))
    last = lamb(all_squares, masters, [x[2] for x in results])
    grads = (attn_grad, inner_grad, outer_grad, gain_grad)

    def flat(four):
        return (*four[:3], four[3][0])

    return (
        decoder_layer_output[None],
        encoder_input_gradient[None],
        decoder_input_gradient[None],
        *flat(grads),
        *flat([x[0] for x in results]),
        *flat([x[1] for x in results]),
        *last,
    )


def solution(mesh):
    rows = P("batch", "seq", None)
    matrix = P(("batch", "seq"), None)
    vector = P(("batch", "seq"))
    kinds = (matrix, matrix, matrix, vector)
    return jax.shard_map(
        per_device,
        mesh=mesh,
        in_specs=(rows, rows, rows, P("batch"), P("batch")) + kinds * 3,
        out_specs=(rows, rows, rows) + kinds * 5 + (P(), P()),
        check_vma=False,
    )
```

```python
import functools
import math

import jax
import jax.numpy as jnp
from jax import lax
from jax.experimental import pallas as pl
from jax.experimental.pallas import tpu as pltpu
from jax.sharding import PartitionSpec as P

D = 768
HEADS = 12
HEAD = 64
FF = 2048
STEP = 5

eps_norm = 1e-06
adam_eps = 1e-06
lamb_rate = 0.5
decay_weight = 0.01
masked_score = -1000000000.0

F32 = jnp.float32
BF16 = jnp.bfloat16

FLOPS, BYTES = 10**13, 10**10


def seq_swap(x, k):
    n = lax.axis_size("seq")
    return lax.ppermute(x, "seq", [(i, i ^ k) for i in range(n)])


def batch_swap(x, k):
    n = lax.axis_size("batch")
    return lax.ppermute(x, "batch", [(i, i ^ k) for i in range(n)])


def gather_blocks(x):
    other, near = seq_swap(x, 2), seq_swap(x, 1)
    return [x, near, other, seq_swap(tie(other, near), 1)]


def xor_blocks(x, s):
    n = x.shape[0]
    for k in (1, 2):
        swapped = jnp.stack([x[j ^ k] for j in range(n)])
        x = jnp.where((s & k) != 0, swapped, x)
    return x


def seq_exchange(blocks, s):
    n = blocks.shape[0]
    mine = xor_blocks(blocks, s)
    got = jnp.stack([mine[0]] + [seq_swap(mine[j], j) for j in range(1, n)])
    return xor_blocks(got, s)


def tie(x, *others):
    return lax.optimization_barrier((x, others))[0]


def ring_shift(x, active=None):
    nb = lax.axis_size("batch")
    return lax.ppermute(x, "batch", [(i, (i + 2) % nb) for i in (range(nb) if active is None else active)])


def ring_gather(block):
    rounds = lax.axis_size("batch") // 2
    after = yield None
    moving, got, paired = block if after is None else tie(block, after), [], None
    for k in range(rounds):
        following = None
        if k + 1 < rounds:
            payload = moving if paired is None else tie(moving, paired)
            following = ring_shift(payload)
        got.append(moving)
        paired = batch_swap(moving if following is not None or paired is None else tie(moving, paired), 1)
        got.append(paired)
        after = yield moving if following is None else payload
        if following is not None:
            moving = following if after is None else tie(following, after)
            paired = got[-1]
    yield got


def assemble_body(by_lanes, moves, count, low, *refs):
    here = len(refs) - 1 - low[1]
    ins, outs, sem = refs[:here], refs[here:-1], refs[-1]
    b = lax.axis_index("batch")
    z, y = b // 2, b % 2
    ring, copies = count // 2, []
    for i, ref in enumerate(ins):
        k, e = (low[0] + i) // 2, (low[0] + i) % 2
        at = lax.rem(z + ring - k, ring) * 2 + (y + e - 2 * y * e)
        for which, (r0, r1), (c0, c1), (to_row, to_lane) in moves:
            out = outs[which]
            rows = pl.ds(to_row, r1 - r0)
            if by_lanes:
                start = pl.multiple_of(at * (out.shape[1] // count) + to_lane, 128)
                target = out.at[rows, pl.ds(start, c1 - c0)]
            else:
                target = out.at[at, rows, pl.ds(to_lane, c1 - c0)]
            copies.append(pltpu.make_async_copy(ref.at[r0:r1, c0:c1], target, sem.at[len(copies)]))
    for copy in copies:
        copy.start()
    for copy in copies:
        copy.wait()


def assemble(blocks, moves, shapes, by_lanes, name, last=0):
    count = len(blocks)
    outs = [jax.ShapeDtypeStruct((h, count * w) if by_lanes else (count, h, w), BF16) for h, w in shapes]
    any_space = pl.BlockSpec(memory_space=pl.ANY)
    made = []
    for low, high in ((0, count - last), (count - last, count)):
        if low == high:
            continue
        part_of = blocks[low:high]

        def body(*refs, low=low, made=tuple(made), part_of=part_of):
            given = refs[: len(part_of)]
            assemble_body(by_lanes, moves, count, (low, len(outs)), *given, *refs[len(part_of) + len(made) :])

        made = pl.pallas_call(
            body,
            in_specs=[pl.BlockSpec(memory_space=pltpu.VMEM)] * len(part_of) + [any_space] * len(made),
            out_specs=[any_space] * len(outs),
            out_shape=outs,
            input_output_aliases={len(part_of) + i: i for i in range(len(made))},
            scratch_shapes=[pltpu.SemaphoreType.DMA((len(part_of) * len(moves),))],
            cost_estimate=pl.CostEstimate(flops=FLOPS, bytes_accessed=BYTES, transcendentals=0),
            name=f"{name}_{low}",
        )(*part_of, *made)
    return made


def gathered_rows(got, name):
    h, w = got[0].shape
    return assemble(got, [(0, (0, h), (0, w), (0, 0))], [(h, w)], False, name)[0]


def gathered_lanes(got, name):
    h, w = got[0].shape
    if w % 128 == 0:
        return assemble(got, [(0, (0, h), (0, w), (0, 0))], [(h, w)], True, name)[0]
    return gathered_rows(got, name).swapaxes(0, 1).reshape(h, -1)


def gathered_feeds(got, rows, name):
    h, w = got[0].shape
    fc = w - 256
    moves = [(0, (0, h), (0, fc), (0, 0))]
    for g in range(D // 128):
        r, c = g % 3 * rows, fc + g // 3 * 128
        moves.append((1, (r, r + rows), (c, c + 128), (0, 128 * g)))
    return assemble(got, moves, [(h, fc), (rows, D)], False, name, 2)


def pair_blocks(blocks):
    y = lax.axis_index("batch") % 2
    pairs = blocks.reshape((blocks.shape[0] // 2, 2) + blocks.shape[1:])
    return [lax.dynamic_index_in_dim(pairs, i, 1, keepdims=False) for i in (y, 1 - y)]


def hop_body(step, counts, moving, riding, *refs):
    count = len(counts)
    kept, got = refs[:count], refs[count : 2 * count]
    refs = list(refs[2 * count :])
    moved = refs.pop(0) if moving else None
    extra = refs.pop(0) if riding else None
    out, one, two, sem = refs
    ring = lax.axis_size("batch") // 2
    dest = lax.rem(lax.axis_index("batch") // 2 + 2 * ring - step, ring)
    for n in range(count):
        low = sum(counts[:n])

        @pl.when((dest >= low) & (dest < low + counts[n]))
        def _(n=n, low=low):
            mine = pltpu.make_async_copy(kept[n].at[dest - low], one, sem.at[0])
            other = pltpu.make_async_copy(got[n].at[dest - low], two, sem.at[1])
            mine.start()
            other.start()
            mine.wait()
            other.wait()

    total = one[...].astype(F32) + two[...].astype(F32)
    rows = one.shape[0]
    if moving:
        total = total + moved[:rows, :].astype(F32)
    out[:rows, :] = total.astype(out.dtype)
    if riding:
        lines = jnp.concatenate([extra[dest * 2], extra[dest * 2 + 1]], axis=0)
        if moving:
            lines = lines + moved[rows : rows + 2, :].astype(F32)
        out[rows:, :] = jnp.concatenate([lines, jnp.zeros((14, lines.shape[1]), F32)], axis=0).astype(out.dtype)


def hop(parts, step, moved, extra, dtype, name):
    shape = parts[0][0].shape[1:]
    arrays = [k for k, _ in parts] + [g for _, g in parts]
    specs = [pl.BlockSpec(memory_space=pl.ANY)] * len(arrays)
    for x in (moved, extra):
        if x is not None:
            arrays.append(x)
            specs.append(pl.BlockSpec(memory_space=pltpu.VMEM))
    out = shape if extra is None else (shape[0] + 16, shape[1])
    return pl.pallas_call(
        functools.partial(hop_body, step, [k.shape[0] for k, _ in parts], moved is not None, extra is not None),
        in_specs=specs,
        out_specs=pl.BlockSpec(memory_space=pltpu.VMEM),
        out_shape=jax.ShapeDtypeStruct(out, dtype),
        scratch_shapes=[pltpu.VMEM(shape, BF16), pltpu.VMEM(shape, BF16), pltpu.SemaphoreType.DMA((2,))],
        cost_estimate=pl.CostEstimate(flops=FLOPS, bytes_accessed=BYTES, transcendentals=0),
        name=f"{name}_{step}",
    )(*arrays)


def ring_reduce(parts, name, extra=None, flight=None):
    ring = lax.axis_size("batch") // 2
    after = yield None
    moved = None
    for k in range(1, ring + 1):
        if moved is None:
            held = [(kept if after is None else tie(kept, after), got) for kept, got in parts]
        else:
            held, moved = parts, tie(moved, after)
        if k == ring:
            yield [hop(held, k, moved, extra, F32, name)]
            return
        sent = hop(held, k, moved, extra, BF16, name)
        moved = ring_shift(sent)
        if flight is not None:
            flight.append(moved)
        after = yield sent


def sum_seq(x):
    for k in (1, 2):
        x = x + seq_swap(x, k)
    return x


def sum_all(x):
    x = sum_seq(x)
    k = 1
    while k < lax.axis_size("batch"):
        x = x + batch_swap(x, k)
        k *= 2
    return x


class Clock:
    def __init__(self):
        self.last = None

    def now(self, x):
        return x if self.last is None else tie(x, self.last)

    def mark(self, x):
        self.last = x
        return x

    def step(self, work):
        got = work.send(self.last)
        return got if isinstance(got, list) else self.mark(got)

    def finish(self, work):
        got = None
        while not isinstance(got, list):
            got = self.step(work)
        return got


def nt(a, b):
    return lax.dot_general(a, b, (((1,), (1,)), ((), ())), preferred_element_type=F32)


def nn(a, b):
    return lax.dot_general(a, b, (((1,), (0,)), ((), ())), preferred_element_type=F32)


def tn(a, b):
    return lax.dot_general(a, b, (((0,), (0,)), ((), ())), preferred_element_type=F32)


def whole(x):
    shape = x.shape
    return pl.BlockSpec(shape, lambda i: (0,) * len(shape))


def part(shape, *index):
    return pl.BlockSpec(shape, lambda i: index)


def plain(arrays):
    return [(x, whole(x)) for x in arrays]


SCALARS = pl.BlockSpec(memory_space=pltpu.SMEM)


def call(body, ins, outs, flops, scratch=(), name=None):
    arrays = [a for a, _ in ins]
    specs = [whole(a) if s is None else s for a, s in ins]
    shapes = [jax.ShapeDtypeStruct(s, d) for s, d in outs]
    return pl.pallas_call(
        body,
        grid=(1,),
        in_specs=specs,
        out_specs=[whole(o) for o in shapes],
        out_shape=shapes,
        scratch_shapes=list(scratch),
        cost_estimate=pl.CostEstimate(flops=FLOPS, bytes_accessed=BYTES, transcendentals=0),
        name=name,
    )(*arrays)


def positions(shape, axis, owner, rows):
    at = lax.broadcasted_iota(jnp.int32, shape, axis)
    shift = rows.bit_length() - 1
    return ((owner ^ (at >> shift)) << shift) + (at & (rows - 1))


def score_bias(meta, first_row, tile, q_rows, k_rows, causal):
    keys = positions((1, 4 * k_rows), 1, meta[0], k_rows)
    if not causal:
        return jnp.where(keys < meta[1], 0.0, masked_score)
    at = first_row + lax.broadcasted_iota(jnp.int32, (tile, 1), 0)
    shift = q_rows.bit_length() - 1
    queries = ((meta[0] ^ (at >> shift)) << shift) + (at & (q_rows - 1))
    return jnp.where((keys <= queries) & (keys < meta[1]), 0.0, masked_score)


def head_mask(shape, h):
    lane = lax.broadcasted_iota(jnp.int32, shape, 1)
    return (lane >= h * HEAD) & (lane < (h + 1) * HEAD)


def attend_tile(q, k, v, bias, heads):
    mixed = jnp.zeros(q.shape, F32)
    logs = jnp.zeros((q.shape[0], 128), F32)
    q = (q.astype(F32) * 0.125).astype(BF16)
    lane = lax.broadcasted_iota(jnp.int32, logs.shape, 1)
    for h in range(heads):
        mask = head_mask(q.shape, h)
        scores = nt(jnp.where(mask, q, jnp.zeros_like(q)), k) + bias
        peak = jnp.max(scores, axis=-1, keepdims=True)
        expo = jnp.exp(scores - peak)
        total = jnp.sum(expo, axis=-1, keepdims=True)
        probs = (expo * (1.0 / total)).astype(BF16)
        mixed = jnp.where(mask, nn(probs, v), mixed)
        logs = jnp.where(lane == h, peak + jnp.log(total), logs)
    return mixed, logs


def attend_rows(meta, q_ref, k_ref, v_ref, wo_ref, first, q_rows, k_rows, causal, outs):
    logs_ref, mixed_ref = outs[:2]
    heads, rows = q_ref.shape[1] // HEAD, 2 * q_rows
    bias = score_bias(meta, first, rows, q_rows, k_rows, causal)
    mixed, logs = attend_tile(q_ref[first : first + rows, :], k_ref[...], v_ref[...], bias, heads)
    logs_ref[...] = logs
    mixed_ref[...] = mixed.astype(BF16)
    if wo_ref is not None:
        for n in range(2):
            out = outs[2 + n]
            out[...] = nn(mixed_ref[n * q_rows : (n + 1) * q_rows, :], wo_ref[...]).astype(out.dtype)


def project_body(rows, mixed_ref, wo_ref, keep_ref, send_ref):
    for n, out in enumerate((keep_ref, send_ref)):
        out[...] = nn(mixed_ref[n * rows : (n + 1) * rows, :], wo_ref[...]).astype(out.dtype)


def project(mixed, out_w, keep, name):
    rows, dc = mixed.shape[0] // 2, mixed.shape[1]
    return call(
        functools.partial(project_body, rows),
        [(mixed, None), out_weights(out_w)],
        [((rows, D), keep), ((rows, D), BF16)],
        4 * rows * dc * D,
        name=name,
    )


def attend_far_body(cross, raw, fused, causal, q_rows, k_rows, *refs):
    refs = list(refs)
    meta = refs.pop(0)
    queries, refs = refs[:4], refs[4:]
    sources = queries
    if cross:
        sources, refs = refs[:4], refs[4:]
    if raw:
        gain = refs.pop(0)
    wq, wk, wv = refs[:3]
    refs = refs[3:]
    wo = refs.pop(0) if fused else None
    if raw:
        rows_ref = refs.pop(0)
        for j in range(4):
            h = queries[j][...].astype(F32)
            inverse = lax.rsqrt(jnp.mean(h * h, axis=-1, keepdims=True) + eps_norm)
            rows_ref[j * q_rows : (j + 1) * q_rows, :] = (h * inverse * gain[...]).astype(BF16)
        queries = sources = [rows_ref.at[j * q_rows : (j + 1) * q_rows, :] for j in range(4)]
    q_ref, k_ref, v_ref = refs[:3]
    outs = refs[3:]
    for j in range(4):
        q_ref[j * q_rows : (j + 1) * q_rows, :] = nt(queries[j][...], wq[...]).astype(BF16)
        rows = sources[j][...]
        k_ref[j * k_rows : (j + 1) * k_rows, :] = nt(rows, wk[...]).astype(BF16)
        v_ref[j * k_rows : (j + 1) * k_rows, :] = nt(rows, wv[...]).astype(BF16)
    attend_rows(meta, q_ref, k_ref, v_ref, wo, 2 * q_rows, q_rows, k_rows, causal, outs)


def attend_near_body(fused, causal, q_rows, k_rows, meta, q_ref, k_ref, v_ref, *rest):
    wo, outs = (rest[0], rest[1:]) if fused else (None, rest)
    attend_rows(meta, q_ref, k_ref, v_ref, wo, 0, q_rows, k_rows, causal, outs)


def attn_weights(attn_t, group):
    return [(attn_t, part((D // 4, D), 0, 4 * group + i)) for i in range(3)]


def out_weights(out_w):
    stack, place = out_w
    return (stack, pl.BlockSpec((None, stack.shape[1], D), lambda i: (place, 0, 0)))


def half_outs(q_rows, dc, keep):
    return [((2 * q_rows, 128), F32), ((2 * q_rows, dc), BF16), ((q_rows, D), keep), ((q_rows, D), BF16)]


def attend_far(meta, queries, sources, attn_t, out_w, group, causal, gain=None):
    cross, raw, fused = sources is not None, gain is not None, out_w is not None
    q_rows, dc = queries[0][1].block_shape[0], D // 4
    k_rows = sources[0][1].block_shape[0] if cross else q_rows
    flops = 2 * D * dc * (4 * q_rows + 8 * k_rows) + 16 * q_rows * k_rows * D
    return call(
        functools.partial(attend_far_body, cross, raw, fused, causal, q_rows, k_rows),
        [(meta, SCALARS)]
        + list(queries)
        + (list(sources) if cross else [])
        + ([(gain, None)] if raw else [])
        + attn_weights(attn_t, group)
        + ([out_weights(out_w)] if fused else []),
        ([((4 * q_rows, D), BF16)] if raw else [])
        + [((4 * q_rows, dc), BF16), ((4 * k_rows, dc), BF16), ((4 * k_rows, dc), BF16)]
        + half_outs(q_rows, dc, BF16)[: 4 if fused else 2],
        flops,
        name=f"attend_far_{group}",
    )


def attend_near(meta, q, k, v, out_w, group, causal):
    q_rows, k_rows, dc, fused = q.shape[0] // 4, k.shape[0] // 4, q.shape[1], out_w is not None
    return call(
        functools.partial(attend_near_body, fused, causal, q_rows, k_rows),
        [(meta, SCALARS), (q, part((2 * q_rows, dc), 0, 0)), (k, None), (v, None)]
        + ([out_weights(out_w)] if fused else []),
        half_outs(q_rows, dc, F32)[: 4 if fused else 2],
        16 * q_rows * k_rows * D,
        name=f"attend_near_{group}",
    )


STEPS = 1


def row_call(body, ins, outs, name):
    rows = ins[0].shape[0]

    def spec(shape):
        if shape[0] == 1:
            return pl.BlockSpec(shape, lambda i: (0, 0))
        return pl.BlockSpec((rows // STEPS,) + tuple(shape[1:]), lambda i: (i, 0))

    return pl.pallas_call(
        body,
        grid=(STEPS,),
        in_specs=[spec(x.shape) for x in ins],
        out_specs=[spec(s) for s, _ in outs],
        out_shape=[jax.ShapeDtypeStruct(s, d) for s, d in outs],
        cost_estimate=pl.CostEstimate(flops=FLOPS, bytes_accessed=BYTES, transcendentals=0),
        name=name,
    )(*ins)


def add_low(a, b):
    return (a.astype(F32) + b.astype(F32)).astype(BF16)


def far_payload(keep_far, send_far):
    return add_low(keep_far, seq_swap(send_far, 1))


def close_body(near_ref, core_ref, far_ref, residual_ref, gain_ref, out_ref, normed_ref):
    h = residual_ref[...].astype(F32) + near_ref[...] + core_ref[...].astype(F32) + far_ref[...].astype(F32)
    inverse = lax.rsqrt(jnp.mean(h * h, axis=-1, keepdims=True) + eps_norm)
    out_ref[...] = h
    normed_ref[...] = (h * inverse * gain_ref[...]).astype(BF16)


def close(near, core, far, residual, gain, name):
    return row_call(
        close_body, [near, core, far, residual, gain], [(near.shape, F32), (near.shape, BF16)], name
    )


def close_back_body(near_ref, core_ref, far_ref, stream_ref, gain_ref, *rest):
    if len(rest) == 4:
        upstream_ref, rest = rest[0], rest[1:]
    else:
        upstream_ref = None
    out_ref, low_ref, dgain_ref = rest
    h = stream_ref[...].astype(F32)
    up = near_ref[...] + core_ref[...].astype(F32) + far_ref[...].astype(F32)
    inverse = lax.rsqrt(jnp.mean(h * h, axis=-1, keepdims=True) + eps_norm)
    unit = h * inverse
    scaled = up * gain_ref[...]
    grad = inverse * (scaled - unit * jnp.mean(scaled * unit, axis=-1, keepdims=True))
    if upstream_ref is not None:
        grad = upstream_ref[...].astype(F32) + grad
    out_ref[...] = grad
    low_ref[...] = grad.astype(BF16)

    @pl.when(pl.program_id(0) == 0)
    def _():
        dgain_ref[...] = jnp.zeros_like(dgain_ref)

    dgain_ref[...] += jnp.sum(up * unit, axis=0, keepdims=True)


def close_back(near, core, far, stream, gain, upstream, name):
    shape = near.shape
    ins = [near, core, far, stream, gain] + ([] if upstream is None else [upstream])
    return row_call(close_back_body, ins, [(shape, F32), (shape, BF16), ((1, shape[1]), F32)], name)


def attend_back_body(cross, causal, q_rows, k_rows, tile, *refs):
    meta = refs[0]
    dz = refs[1:5]
    q_ref, qt_ref, k_ref, v_ref, logs_near, logs_far, wq, wk, wv, wo = refs[5:15]
    dq_ref, dkt_ref, dvt_ref = refs[15:18]
    outs = refs[18 : 18 + (8 if cross else 4)]
    do_ref, dot_ref, dkt_sum, dvt_sum, logs_ref = refs[18 + len(outs) :]
    heads = q_ref.shape[1] // HEAD
    for j in range(4):
        at = slice(j * q_rows, (j + 1) * q_rows)
        rows = dz[j][...]
        do_ref[at, :] = nt(rows, wo[...]).astype(BF16)
        dot_ref[:, at] = nt(wo[...], rows).astype(BF16)
    logs_ref[: 2 * q_rows, :] = logs_near[...]
    logs_ref[2 * q_rows :, :] = logs_far[...]
    dkt_sum[...] = jnp.zeros_like(dkt_sum)
    dvt_sum[...] = jnp.zeros_like(dvt_sum)

    def step(t, carry):
        at = pl.ds(pl.multiple_of(t * tile, tile), tile)
        q, do = q_ref[at, :], do_ref[at, :]
        q = (q.astype(F32) * 0.125).astype(BF16)
        qt, dot = qt_ref[:, at], dot_ref[:, at]
        logs = logs_ref[at, :]
        bias = score_bias(meta, t * tile, tile, q_rows, k_rows, causal)
        dq = jnp.zeros(q.shape, F32)
        for h in range(heads):
            mask = head_mask(q.shape, h)
            zero = jnp.zeros_like(q)
            probs = jnp.exp(nt(jnp.where(mask, q, zero), k_ref[...]) + bias - logs[:, h : h + 1])
            grad_probs = nt(jnp.where(mask, do, zero), v_ref[...])
            weighted = probs * grad_probs
            center = jnp.sum(weighted, axis=-1, keepdims=True)
            grad_scores = (weighted - probs * center).astype(BF16)
            feats = slice(h * HEAD, (h + 1) * HEAD)
            dvt_sum[feats, :] += nn(dot[feats, :], probs.astype(BF16))
            dkt_sum[feats, :] += nn(qt[feats, :], grad_scores)
            dq = jnp.where(mask, nn(grad_scores, k_ref[...]), dq)
        dq_ref[at, :] = (dq * 0.125).astype(BF16)
        return carry

    lax.fori_loop(0, 4 * q_rows // tile, step, 0)
    dkt_ref[...] = (dkt_sum[...] * 0.125).astype(BF16)
    dvt_ref[...] = dvt_sum[...].astype(BF16)

    def query_part(j):
        return nn(dq_ref[j * q_rows : (j + 1) * q_rows, :], wq[...])

    def source_part(j):
        at = slice(j * k_rows, (j + 1) * k_rows)
        return tn(dkt_ref[:, at], wk[...]) + tn(dvt_ref[:, at], wv[...])

    parts = (query_part, source_part) if cross else ((lambda j: query_part(j) + source_part(j)),)
    for n, make in enumerate(parts):
        for j in range(4):
            outs[4 * n + j][...] = make(j).astype(outs[4 * n + j].dtype)


def attend_back(meta, dz, qt, attn_t, out_w, group, saved, q_rows, k_rows, causal, cross):
    q, k, v, logs_near, logs_far = saved
    dc = q.shape[1]
    tile = min(512, 4 * q_rows)

    def four(rows):
        return [((rows, D), F32), ((rows, D), BF16), ((rows, D), BF16), ((rows, D), BF16)]

    outs = call(
        functools.partial(attend_back_body, cross, causal, q_rows, k_rows, tile),
        [(meta, SCALARS)]
        + list(dz)
        + [(q, None), (qt, None), (k, None), (v, None), (logs_near, None), (logs_far, None)]
        + attn_weights(attn_t, group)
        + [out_weights(out_w)],
        [((4 * q_rows, dc), BF16), ((dc, 4 * k_rows), BF16), ((dc, 4 * k_rows), BF16)]
        + (four(q_rows) + four(k_rows) if cross else four(q_rows)),
        80 * q_rows * k_rows * D + 4 * D * dc * (4 * q_rows + 4 * k_rows),
        [
            pltpu.VMEM((4 * q_rows, dc), BF16),
            pltpu.VMEM((dc, 4 * q_rows), BF16),
            pltpu.VMEM((dc, 4 * k_rows), F32),
            pltpu.VMEM((dc, 4 * k_rows), F32),
            pltpu.VMEM((4 * q_rows, 128), F32),
        ],
        f"attend_back_{group}",
    )
    return outs[:3], outs[3:]


def attend_weights_body(cross, q_rows, k_rows, *refs):
    queries = refs[0:4]
    sources = refs[4:8] if cross else queries
    dq, dkt, dvt, *outs = refs[8:] if cross else refs[4:]
    gq = gk = gv = None
    for j in range(4):
        at, ak = slice(j * q_rows, (j + 1) * q_rows), slice(j * k_rows, (j + 1) * k_rows)
        x, y = queries[j][...], sources[j][...]
        a, b, c = tn(dq[at, :], x), nn(dkt[:, ak], y), nn(dvt[:, ak], y)
        gq, gk, gv = (a, b, c) if j == 0 else (gq + a, gk + b, gv + c)
    for ref, g in zip(outs, (gq, gk, gv)):
        ref[...] = g.astype(BF16)


def attend_weights(queries, sources, grads, name):
    cross = sources is not None
    dq, dkt, dvt = grads
    q_rows, k_rows, dc = dq.shape[0] // 4, dkt.shape[1] // 4, dq.shape[1]
    return call(
        functools.partial(attend_weights_body, cross, q_rows, k_rows),
        list(queries) + (list(sources) if cross else []) + [(dq, None), (dkt, None), (dvt, None)],
        [((dc, D), BF16)] * 3,
        0,
        name=name,
    )


def out_total(dz, near, far, q_rows):
    total = None
    for j, ref in enumerate(dz):
        mixed = (near, far)[j // 2][(j % 2) * q_rows : (j % 2 + 1) * q_rows, :]
        x = tn(ref[...], mixed)
        total = x if j == 0 else total + x
    return total


def out_weight_body(sizes, *refs):
    outs, scratch = refs[6 * len(sizes) : -1], refs[-1]
    s, rows = lax.axis_index("seq"), scratch.shape[2]
    for n, q_rows in enumerate(sizes):
        total = out_total(refs[6 * n : 6 * n + 4], refs[6 * n + 4], refs[6 * n + 5], q_rows)
        for t in range(4):
            scratch[s ^ t, n] = total[t * rows : (t + 1) * rows, :].astype(BF16)
    hand_out(scratch, outs)


def out_weight(groups, name):
    dc = D // 4
    ins, sizes = [], []
    for dz, near, far in groups:
        ins += list(dz) + [(near, None), (far, None)]
        sizes.append(near.shape[0] // 2)
    return call(
        functools.partial(out_weight_body, sizes),
        ins,
        sent_shapes((len(groups), dc, dc), BF16),
        0,
        [pltpu.VMEM((4, len(groups), dc, dc), BF16)],
        name,
    )


GELU_A, GELU_B = math.sqrt(2.0 / math.pi), 0.044715


def feed_forward_body(rows, x0, x1, wg, wu, wd, gate_ref, up_ref, hidden_ref, keep_ref, send_ref):
    for j, x_ref in enumerate((x0, x1)):
        at = slice(j * rows, (j + 1) * rows)
        x = x_ref[...]
        gate, up = nn(x, wg[...]), nn(x, wu[...])
        gate_ref[at, :] = gate
        up_ref[at, :] = up
        inner = jnp.tanh(GELU_A * (gate + GELU_B * (gate * gate * gate)))
        hidden_ref[at, :] = (0.5 * gate * (1.0 + inner) * up).astype(BF16)
        out = (keep_ref, send_ref)[j]
        out[...] = nn(hidden_ref[at, :], wd[...]).astype(out.dtype)


def feed_weights(inner_cols, outer_rows, which):
    fc = inner_cols.shape[1]
    return [
        (inner_cols, part((D, fc), 2 * which, 0)),
        (inner_cols, part((D, fc), 2 * which + 1, 0)),
        (outer_rows, part((fc, D), which, 0)),
    ]


def feed_forward(half, inner_cols, outer_rows, which, keep, name):
    rows, fc = half[0].shape[0], inner_cols.shape[1]
    return call(
        functools.partial(feed_forward_body, rows),
        plain(half) + feed_weights(inner_cols, outer_rows, which),
        [((2 * rows, fc), F32), ((2 * rows, fc), F32), ((2 * rows, fc), BF16), ((rows, D), keep), ((rows, D), BF16)],
        12 * rows * fc * D,
        name=name,
    )


def feed_back_body(rows, d0, d1, gate_ref, up_ref, wg, wu, wd, dgate_ref, dup_ref, keep_ref, send_ref):
    for j, d_ref in enumerate((d0, d1)):
        at = slice(j * rows, (j + 1) * rows)
        dh = nt(d_ref[...], wd[...])
        t, up = gate_ref[at, :], up_ref[at, :]
        square = t * t
        inner = jnp.tanh(GELU_A * t * (1.0 + GELU_B * square))
        slope = 0.5 * (1.0 + inner) + 0.5 * t * (1.0 - inner * inner) * (
            GELU_A * (1.0 + 3.0 * GELU_B * square)
        )
        dgate_ref[at, :] = (dh * up * slope).astype(BF16)
        dup_ref[at, :] = (dh * (0.5 * t * (1.0 + inner))).astype(BF16)
        out = (keep_ref, send_ref)[j]
        out[...] = (nt(dgate_ref[at, :], wg[...]) + nt(dup_ref[at, :], wu[...])).astype(out.dtype)


def feed_back(dz_half, gate, up, inner_cols, outer_rows, which, keep, name):
    rows, fc = gate.shape[0] // 2, inner_cols.shape[1]
    return call(
        functools.partial(feed_back_body, rows),
        list(dz_half) + [(gate, None), (up, None)] + feed_weights(inner_cols, outer_rows, which),
        [((2 * rows, fc), BF16), ((2 * rows, fc), BF16), ((rows, D), keep), ((rows, D), BF16)],
        12 * rows * fc * D,
        name=name,
    )


def feed_weight_body(rows, packed, *refs):
    xs, dzs = refs[0:4], refs[4:8]
    dg, du, hid = refs[8:10], refs[10:12], refs[12:14]
    outs = refs[14:]
    gate = up = down = None
    for j in range(4):
        at = slice((j % 2) * rows, (j % 2 + 1) * rows)
        x = xs[j][...]
        a, b = tn(x, dg[j // 2][at, :]), tn(x, du[j // 2][at, :])
        c = tn(hid[j // 2][at, :], dzs[j][...])
        gate, up, down = (a, b, c) if j == 0 else (gate + a, up + b, down + c)
    fc = gate.shape[1]
    if not packed:
        outs[0][:D, :] = gate.astype(BF16)
        outs[0][D:, :] = up.astype(BF16)
        outs[1][...] = down.astype(BF16)
        return
    out = refs[-1]
    height = out.shape[1]
    for n, grad in enumerate((gate, up)):
        for k in range(2):
            out[2 * n + k, :, :fc] = grad[k * height : (k + 1) * height, :].astype(BF16)
    short = fc // 4
    for q in range(4):
        for g in range(D // 128):
            piece = down[q * short : (q + 1) * short, g * 128 : (g + 1) * 128].astype(BF16)
            r, c = g % 3 * short, fc + g // 3 * 128
            out[q, r : r + short, c : c + 128] = piece
    y = lax.axis_index("batch") % 2
    for i in range(2):
        outs[0][i] = out[2 * i + y]
        outs[1][i] = out[2 * i + 1 - y]


def feed_weight(xs, dzs, dgate, dup, hidden, packed, name):
    rows, fc = xs[0].shape[0], dgate[0].shape[1]
    return call(
        functools.partial(feed_weight_body, rows, packed),
        plain(xs) + list(dzs) + plain((*dgate, *dup, *hidden)),
        [((2, D // 2, fc + 256), BF16)] * 2 if packed else [((2 * D, fc), BF16), ((fc, D), BF16)],
        24 * rows * fc * D,
        [pltpu.VMEM((4, D // 2, fc + 256), BF16)] if packed else [],
        name,
    )


def send_some(mine):
    return [mine[0], seq_swap(mine[1], 1), seq_swap(mine[2], 2)]


def send_rest(got, *after):
    return [*got, seq_swap(tie(got[2], got[1], *after), 1)]


def send_blocks(mine):
    return send_rest(send_some(mine))


def place(scratch, refs, s):
    for j, ref in enumerate(refs):
        scratch[s ^ j] = ref[...] if j < 2 else ref[j - 2]


def hand_out(scratch, outs):
    outs[0][...] = scratch[0]
    outs[1][...] = scratch[1]
    outs[2][0] = scratch[2]
    outs[2][1] = scratch[3]


def sent_shapes(shape, dtype):
    return [(shape, dtype), (shape, dtype), ((2,) + shape, dtype)]


def head_pack_body(ar, gr, lines, attn_ref, gain_ref, inner_ref, *refs):
    outs, feed_outs, scratch, feed_scratch = refs[:3], refs[3:6], refs[6], refs[7]
    s = lax.axis_index("seq")
    width, ir = scratch.shape[2], inner_ref.shape[0]
    dc, room = D // 4, width - ar
    turned = attn_ref[...].T
    gains = jnp.concatenate([gain_ref[...], jnp.zeros((1, lines * room - gr), F32)], axis=1)
    for t in range(4):
        at = s ^ t
        scratch[at, :, ar:] = jnp.zeros((dc, room), BF16)
        scratch[at, :, :ar] = turned[t * dc : (t + 1) * dc, :].astype(BF16)
        for n in range(lines):
            scratch[at, n : n + 1, ar:] = gains[:, n * room : (n + 1) * room].astype(BF16)
        for q in range(4):
            low = (4 * q + t) * 128
            feed_scratch[at, :, q * 128 : (q + 1) * 128] = inner_ref[:, low : low + 128].astype(BF16)
    hand_out(scratch, outs)
    hand_out(feed_scratch, feed_outs)


def attn_unpack_body(ar, gr, lines, *refs):
    ins, (attn_ref, scratch) = refs[0:4], refs[4:]
    place(scratch, ins, lax.axis_index("seq"))
    dc, room = D // 4, scratch.shape[2] - ar
    pieces = []
    for k in range(4):
        attn_ref[:dc, k * ar : (k + 1) * ar] = scratch[k, :, :ar]
        pieces += [scratch[k, n : n + 1, ar : ar + min(room, gr - n * room)].astype(F32) for n in range(lines)]
    pieces.append(jnp.zeros((1, attn_ref.shape[1] - 4 * gr), F32))
    line = jnp.concatenate(pieces, axis=1)
    fill = jnp.zeros((attn_ref.shape[0] - dc - 1, line.shape[1]), F32)
    attn_ref[dc:, :] = jnp.concatenate([line, fill], axis=0).astype(BF16)


def feeds_unpack_body(*refs):
    ins, outer_ref, feed_ref, scratch = refs[0:4], refs[4], refs[5], refs[6]
    place(scratch, ins, lax.axis_index("seq"))
    ir, orow = scratch.shape[1], outer_ref.shape[0]
    for k in range(4):
        feed_ref[k * ir : (k + 1) * ir, :512] = scratch[k]
    for g in range(D // 128):
        r, c = g % 3 * orow, 512 + g // 3 * 128
        feed_ref[r : r + orow, c : c + 128] = outer_ref[:, g * 128 : (g + 1) * 128].astype(BF16)


def head_exchange(attn_master, inner_master, outer_master, gain_master):
    ar, dc, gr = attn_master.shape[0], D // 4, gain_master.shape[0]
    ir, fc = inner_master.shape[0], inner_master.shape[1] // 4
    width = (ar // 128 + 1) * 128
    lines = -(-gr // (width - ar))
    scratch, feed_scratch = pltpu.VMEM((4, dc, width), BF16), pltpu.VMEM((4, ir, fc), BF16)
    outs = call(
        functools.partial(head_pack_body, ar, gr, lines),
        plain([attn_master, gain_master[None], inner_master]),
        sent_shapes((dc, width), BF16) + sent_shapes((ir, fc), BF16),
        0,
        [scratch, feed_scratch],
        "head_pack",
    )
    attn = call(
        functools.partial(attn_unpack_body, ar, gr, lines),
        plain(send_blocks(outs[:3])),
        [((dc + 16, 4 * ar), BF16)],
        0,
        [scratch],
        "attn_unpack",
    )[0]
    feeds = call(
        feeds_unpack_body,
        plain(send_blocks([outs[3], tie(outs[4], attn), tie(outs[5], attn)]) + [outer_master]),
        [((4 * ir, D), BF16)],
        0,
        [feed_scratch],
        "feeds_unpack",
    )[0]
    return attn, feeds


def turn_pack_body(count, *refs):
    ins, outs, scratch = refs[:count], refs[count : count + 3], refs[count + 3]
    s = lax.axis_index("seq")
    dc = scratch.shape[2]
    for t in range(4):
        for g in range(count):
            scratch[s ^ t, g] = ins[g][:, t * dc : (t + 1) * dc].T
    hand_out(scratch, outs)


def turn_pack(ins, name):
    count, dc = len(ins), D // 4
    return call(
        functools.partial(turn_pack_body, count),
        ins,
        sent_shapes((count, dc, dc), BF16),
        0,
        [pltpu.VMEM((4, count, dc, dc), BF16)],
        name,
    )


def lanes_unpack_body(*refs):
    ins, out, scratch = refs[:4], refs[4], refs[5]
    place(scratch, ins, lax.axis_index("seq"))
    width = scratch.shape[3]
    for k in range(4):
        for g in range(scratch.shape[1]):
            out[g, :, k * width : (k + 1) * width] = scratch[k, g]


def lanes_unpack(got, name):
    shape = got[0].shape
    return call(
        lanes_unpack_body,
        plain(got),
        [(shape[:2] + (4 * shape[2],), BF16)],
        0,
        [pltpu.VMEM((4,) + shape, BF16)],
        name,
    )[0]


def tail_pack_body(gr, total_ref, *refs):
    outs, scratch = refs[:3], refs[3]
    s, width = lax.axis_index("seq"), scratch.shape[2]
    dc = D // 4
    for t in range(4):
        scratch[s ^ t, :dc] = total_ref[:dc, t * width : (t + 1) * width].astype(BF16)
        lines = [total_ref[dc + e : dc + e + 1, t * gr : (t + 1) * gr] for e in range(2)]
        lines = jnp.concatenate(lines + [jnp.zeros((1, width - 2 * gr), F32)] * (width > 2 * gr), axis=1)
        scratch[s ^ t, dc:] = jnp.concatenate([lines, jnp.zeros((15, width), F32)], axis=0).astype(BF16)
    hand_out(scratch, outs)


def tail_unpack_body(gr, *refs):
    ins, (out, kept_ref, sent_ref, scratch) = refs[:4], refs[4:]
    place(scratch, ins, lax.axis_index("seq"))
    dc = D // 4
    lines = None
    for k in range(4):
        out[:, k * dc : (k + 1) * dc] = scratch[k, :dc].astype(F32).T
        line = scratch[k, dc:].astype(F32)[:1]
        lines = line if k == 0 else lines + line
    halves = lines[:, :gr], lines[:, gr : 2 * gr]
    first = lax.axis_index("batch") % 2 == 0
    kept_ref[...] = jnp.where(first, halves[0], halves[1])
    sent_ref[...] = jnp.where(first, halves[1], halves[0])


def feed_pack_body(total_ref, *refs):
    outs, outer_ref, scratch = refs[:3], refs[3], refs[4]
    s, (rows, fc), orow = lax.axis_index("seq"), scratch.shape[1:], outer_ref.shape[0]
    for t in range(4):
        scratch[s ^ t] = total_ref[t * rows : (t + 1) * rows, :fc].astype(BF16)
    hand_out(scratch, outs)
    for g in range(D // 128):
        r, c = g % 3 * orow, fc + g // 3 * 128
        outer_ref[:, g * 128 : (g + 1) * 128] = total_ref[r : r + orow, c : c + 128]


def feed_pack(total, ir, fc, orow):
    outs = call(
        feed_pack_body,
        plain([total]),
        sent_shapes((ir, fc), BF16) + [((orow, D), F32)],
        0,
        [pltpu.VMEM((4, ir, fc), BF16)],
        "feed_pack",
    )
    return outs[:3], outs[3]


def feed_unpack_body(*refs):
    ins, out, scratch = refs[:4], refs[4], refs[5]
    place(scratch, ins, lax.axis_index("seq"))
    for k in range(4):
        for q in range(4):
            low = (4 * q + k) * 128
            out[:, low : low + 128] = scratch[k, :, q * 128 : (q + 1) * 128].astype(F32)


def feed_unpack(got):
    ir, fc = got[0].shape
    return call(
        feed_unpack_body, plain(got), [((ir, 4 * fc), F32)], 0, [pltpu.VMEM((4, ir, fc), BF16)], "feed_unpack"
    )[0]


def spread_body(*refs):
    out_ref = refs[6]
    count, width = out_ref.shape[0], out_ref.shape[2]
    per = 6 * D // count
    line = jnp.concatenate([x[...] for x in refs[:6]], axis=1)
    for n in range(count):
        piece = line[:, n * per : (n + 1) * per]
        out_ref[n] = jnp.concatenate([piece, jnp.zeros((1, width - per), F32)], axis=1)


def spread(rows, count, width):
    return call(spread_body, plain(rows), [((count, 1, width), F32)], 0, name="spread")[0]


def tail_pack(total, ar, gr):
    if ar % 16:
        return [total, total]
    shape = (D // 4 + 16, ar)
    mine = call(
        functools.partial(tail_pack_body, gr),
        plain([total]),
        sent_shapes(shape, BF16),
        0,
        [pltpu.VMEM((4,) + shape, BF16)],
        "tail_pack",
    )
    return send_some(mine) + [mine[1]]


def tail_unpack(mine, s, ar, gr, now, *after):
    dc = D // 4
    if ar % 16:
        got = seq_exchange(mine[0][:dc].astype(BF16).reshape(dc, 4, ar).swapaxes(0, 1), s)
        lines = lax.dynamic_slice_in_dim(sum_seq(mine[0][dc : dc + 2]), s * gr, gr, axis=1)
        y = lax.axis_index("batch") % 2
        pair = [lax.dynamic_slice_in_dim(lines, i, 1, axis=0) for i in (y, 1 - y)]
        return (got.reshape(4 * dc, ar).T.astype(F32), *pair)
    got = send_rest(mine[:3], *after)
    return call(
        functools.partial(tail_unpack_body, gr),
        plain([now(got[0]), *got[1:]]),
        [((ar, 4 * dc), F32), ((1, gr), F32), ((1, gr), F32)],
        0,
        [pltpu.VMEM((4, dc + 16, ar), BF16)],
        "tail_unpack",
    )


def split_lanes(scratch, pieces):
    width = scratch.shape[2]
    for n, piece in enumerate(pieces):
        for low in range(n * D, (n + 1) * D, D // 2):
            to = low % width
            scratch[low // width, :, to : to + D // 2] = piece[:, low - n * D : low - n * D + D // 2]


def part_pack_body(positions, *refs):
    count = len(positions)
    ins = refs[4 : 4 + 2 * count]
    kept_ref, sent_ref, squares, scratch = refs[4 + 2 * count :]
    y = lax.axis_index("batch") % 2
    place(squares, refs[:4], lax.axis_index("seq"))
    for n, position in enumerate(positions):
        pieces = [x[...] for x in ins[2 * n : 2 * n + 2]]
        pieces.insert(position, jnp.concatenate([squares[k, n] for k in range(4)], axis=1))
        split_lanes(scratch, pieces)
        kept_ref[n] = scratch[y]
        sent_ref[n] = scratch[1 - y]


def attn_parts(got, parts, width, name):
    dc = D // 4
    if width % 128 or lax.axis_size("batch") != 8:
        joined = []
        matrices = None if got is None else lanes_unpack(got, name)
        for n, (others, position) in enumerate(parts):
            pieces = list(others)
            if got is not None:
                pieces.insert(position, matrices[n])
            joined.append(jnp.concatenate(pieces, axis=1))
        joined = jnp.concatenate(joined, axis=1)
        return pair_blocks(joined.reshape(dc, -1, width).swapaxes(0, 1))
    return call(
        functools.partial(part_pack_body, [position for _, position in parts]),
        plain([*got, *(x for others, _ in parts for x in others)]),
        [((len(parts), dc, width), BF16)] * 2,
        0,
        [pltpu.VMEM((4, len(parts), dc, dc), BF16), pltpu.VMEM((2, dc, width), BF16)],
        name,
    )


def self_part_body(rows, *refs):
    x = refs[0:4]
    dq, dkt, dvt, kept_ref, sent_ref, scratch = refs[4:10]
    gq = gk = gv = None
    for j in range(4):
        at = slice(j * rows, (j + 1) * rows)
        y = x[j][...]
        a, b, c = tn(dq[at, :], y), nn(dkt[:, at], y), nn(dvt[:, at], y)
        gq, gk, gv = (a, b, c) if j == 0 else (gq + a, gk + b, gv + c)
    split_lanes(scratch, [g.astype(BF16) for g in (gq, gk, gv)])
    y = lax.axis_index("batch") % 2
    kept_ref[0] = scratch[y]
    sent_ref[0] = scratch[1 - y]


def self_part(rows, grads, width, name):
    dq, dkt, dvt = grads
    per, dc = dq.shape[0] // 4, dq.shape[1]
    if width % 128 or lax.axis_size("batch") != 8:
        gq, gk, gv = (g.reshape(4, per, dc) for g in (dq, dkt.T, dvt.T))
        made = [
            sum(tn(g[j], x.reshape(4, per, D)[j]) for j, (x, _) in enumerate(rows)).astype(BF16)
            for g in (gq, gk, gv)
        ]
        return attn_parts(None, [(made, 0)], width, name)
    return call(
        functools.partial(self_part_body, per),
        list(rows) + plain([dq, dkt, dvt]),
        [((1, dc, width), BF16)] * 2,
        0,
        [pltpu.VMEM((2, dc, width), BF16)],
        name,
    )


KINDS = ((D, 0), (D, 12), (FF, 16), (D, 18))


def group_mask(count, kind):
    per_group, offset = KINDS[kind]
    axis = 1 if kind < 3 else 0
    shape = (count, 128) if kind < 3 else (128, count)
    at = lax.axis_index(("batch", "seq")) * count + lax.broadcasted_iota(jnp.int32, shape, 1 - axis)
    low = (lax.broadcasted_iota(jnp.int32, shape, axis) - offset) * per_group
    return (at >= low) & (at < low + per_group) & (low >= 0)


def diagonal():
    return lax.broadcasted_iota(jnp.int32, (128, 128), 0) == lax.broadcasted_iota(jnp.int32, (128, 128), 1)


def by_group(values, kind):
    if kind == 3:
        mask = group_mask(values.shape[1], kind)
        column = jnp.sum(jnp.where(mask, values * values, 0.0), axis=1, keepdims=True)
        return jnp.sum(jnp.where(diagonal(), column, 0.0), axis=0, keepdims=True)
    squares = jnp.sum(values * values, axis=1, keepdims=True)
    return jnp.sum(jnp.where(group_mask(values.shape[0], kind), squares, 0.0), axis=0, keepdims=True)


def of_group(row, count, kind):
    if kind == 3:
        column = jnp.sum(jnp.where(diagonal(), row, 0.0), axis=1, keepdims=True)
        return jnp.sum(jnp.where(group_mask(count, kind), column, 0.0), axis=0, keepdims=True)
    return jnp.sum(jnp.where(group_mask(count, kind), row, 0.0), axis=1, keepdims=True)


def square_sums_body(*refs):
    total = by_group(refs[0][...], 0)
    for kind in range(1, 4):
        total = total + by_group(refs[kind][...], kind)
    refs[4][...] = total


def square_sums(masters):
    return call(square_sums_body, plain(masters), [((1, 128), F32)], 0, name="square_sums")[0]


def adam_body(kind, w_ref, m_ref, v_ref, g_ref, first_ref, second_ref, update_ref, sums_ref):
    gradient = g_ref[...]
    correction = 1.0 - 0.5**STEP
    first = 0.5 * m_ref[...] + 0.5 * gradient
    second = 0.5 * v_ref[...] + 0.5 * gradient * gradient
    update = first / correction / (jnp.sqrt(second / correction) + adam_eps)
    update = update + (decay_weight if kind < 3 else 0.0) * w_ref[...]
    first_ref[...] = first
    second_ref[...] = second
    update_ref[...] = update
    sums_ref[...] = by_group(update, kind)


def adam(kind, w, m, v, g):
    return call(
        functools.partial(adam_body, kind),
        plain([w, m, v, g]),
        [(w.shape, F32)] * 3 + [((1, 128), F32)],
        0,
        name=f"adam_{kind}",
    )


def gain_body(kept_ref, got_ref, w_ref, m_ref, v_ref, weights_ref, s0, s1, s2, grad_ref, *outs):
    grad_ref[...] = kept_ref[...] + got_ref[...]
    first_ref, second_ref, update_ref, sums_ref = *outs[:3], outs[4]
    adam_body(3, w_ref, m_ref, v_ref, grad_ref, first_ref, second_ref, update_ref, sums_ref)
    outs[3][:, :128] = weights_ref[...]
    outs[3][:, 128:] = sums_ref[...] + s0[...] + s1[...] + s2[...]


def gain_adam(kept, got, w, m, v, weight_sums, sums):
    return call(
        gain_body,
        plain([kept, got, w, m, v, weight_sums, *sums]),
        [(w.shape, F32)] * 4 + [((1, 256), F32)],
        0,
        [pltpu.VMEM((1, 128), F32)],
        "adam_3",
    )


def lamb_body(*refs):
    weight_norms, update_norms = jnp.sqrt(refs[0][:, :128]), jnp.sqrt(refs[0][:, 128:])
    ratio = weight_norms / (update_norms + 1e-06)
    masters, updates, news, copies = (refs[1 + 4 * n : 5 + 4 * n] for n in range(4))
    for kind in range(4):
        w = masters[kind]
        scale = of_group(ratio, w.shape[1] if kind == 3 else w.shape[0], kind)
        new = w[...] - lamb_rate * scale * updates[kind][...]
        if kind == 3:
            new = new[0]
        news[kind][...] = new
        copies[kind][...] = new.astype(BF16)
    refs[17][...] = weight_norms[0, :24]
    refs[18][...] = update_norms[0, :24]


def lamb(squares, masters, updates):
    shapes = [w.shape for w in masters[:3]] + [masters[3].shape[1:]]
    return call(
        lamb_body,
        plain([squares, *masters, *updates]),
        [(s, F32) for s in shapes] + [(s, BF16) for s in shapes] + [((24,), F32)] * 2,
        0,
        name="lamb",
    )


def per_device(
    encoder_layer_input,
    decoder_layer_input,
    cotangent,
    encoder_used_lengths,
    decoder_used_lengths,
    attn_master,
    inner_master,
    outer_master,
    gain_master,
    attn_first,
    inner_first,
    outer_first,
    gain_first,
    attn_second,
    inner_second,
    outer_second,
    gain_second,
):
    ns, nb = lax.axis_size("seq"), lax.axis_size("batch")
    s, b = lax.axis_index("seq"), lax.axis_index("batch")
    ar, ir, orow = attn_master.shape[0], inner_master.shape[0], outer_master.shape[0]
    dc, fc = D // ns, FF // ns
    cuts = FF // (ns * orow)

    gr = gain_master.shape[0]
    packed = nb == 8 and ar % 16 == 0 and 3 * orow == ns * ir and cuts == 4
    clock = Clock()
    now, mark = clock.now, clock.mark
    masters = [attn_master, inner_master, outer_master, gain_master[None]]
    if packed:
        attn_mine, feed_mine = head_exchange(attn_master, inner_master, outer_master, gain_master)
        feeds_mine = [feed_mine]
    else:
        width = (ar // 128 + 1) * 128
        lines = -(-gr // (width - ar))
        corner = jnp.pad(gain_master.astype(BF16), (0, lines * (width - ar) - gr)).reshape(lines, width - ar)
        corner = jnp.broadcast_to(jnp.pad(corner, ((0, dc - lines), (0, 0))), (ns, dc, width - ar))
        attn_low = attn_master.astype(BF16).T.reshape(ns, dc, ar)
        got = seq_exchange(jnp.concatenate([attn_low, corner], axis=2), s)
        attn_mine = got[:, :, :ar].swapaxes(0, 1).reshape(dc, ns * ar)
        gains_mine = got[:, :lines, ar:].reshape(ns, -1)[:, :gr].reshape(1, ns * gr)
        attn_mine = jnp.concatenate([attn_mine, jnp.pad(gains_mine, ((0, 15), (0, ns * (ar - gr))))])
        inner_low = inner_master.astype(BF16).reshape(ir, cuts, ns, orow).transpose(2, 0, 1, 3)
        inner_mine = seq_exchange(inner_low.reshape(ns, ir, fc), s).reshape(ns * ir, fc)
        feeds_mine = [inner_mine, outer_master.astype(BF16)]
    attn_got = None
    attn_ring = ring_gather(attn_mine)
    next(attn_ring)
    while not isinstance(attn_got, list):
        attn_last, attn_got = attn_got, attn_ring.send(None)
    squares = square_sums(masters)
    attn_t = gathered_lanes([attn_got[0], *(tie(x, squares) for x in attn_got[1:])], "gather_attn")
    feed_rings = [ring_gather(x) for x in feeds_mine]
    for x in feed_rings:
        next(x)
        x.send(attn_last)

    def feed_step():
        for x in feed_rings:
            clock.step(x)

    gains = attn_t[dc].reshape(nb, ns * ar)[:, : ns * gr].reshape(6, D).astype(F32)
    gain = [gains[i : i + 1] for i in range(6)]
    out_mine = turn_pack([(attn_t, part((dc, D), 0, 4 * g + 3)) for g in range(3)], "out_pack")
    out_got = send_some(out_mine)

    enc_in, dec_in = encoder_layer_input[0], decoder_layer_input[0]
    er, dr = enc_in.shape[0], dec_in.shape[0]
    enc_meta = jnp.stack([s, encoder_used_lengths[0]]).astype(jnp.int32)
    dec_meta = jnp.stack([s, decoder_used_lengths[0]]).astype(jnp.int32)
    alive = (s * dr + jnp.arange(dr, dtype=jnp.int32)) < decoder_used_lengths[0]
    seed = jnp.where(alive[:, None], cotangent[0], jnp.zeros_like(cotangent[0]))
    blocks = gather_blocks(jnp.concatenate([enc_in, dec_in, seed]))
    enc_blocks = [(x, part((er, D), 0, 0)) for x in blocks]
    dec_blocks = [(x, part((dr, D), er // dr, 0)) for x in blocks]
    seed_blocks = [(x, part((dr, D), er // dr + 1, 0)) for x in blocks]

    def quarters(rows):
        return [(rows, part((rows.shape[0] // 4, D), j, 0)) for j in range(4)]

    mark(out_mine[1])
    feed_step()
    rows_a, q0, k0, v0, logs_far0, mixed_far0 = attend_far(
        now(enc_meta), enc_blocks, None, attn_t, None, 0, False, gain[0]
    )
    mark(mixed_far0)
    logs_near0, mixed_near0 = attend_near(enc_meta, now(q0), k0, v0, None, 0, False)
    mark([mixed_near0, out_got[2]])
    feed_step()
    out_w = lanes_unpack(send_rest([now(out_got[0]), *out_got[1:]], mixed_near0), "out_unpack")
    kf, sf = project(mixed_far0, (out_w, 0), BF16, "project_far_0")
    mark(sf)
    kn_enc, sn = project(now(mixed_near0), (out_w, 0), F32, "project_near_0")
    mark(sn)
    far = mark(add_low(now(kf), seq_swap(sf, 1)))
    x_enc, c_enc = seq_swap(far, 2), seq_swap(sn, 1)
    rows_c, q1, k1, v1, logs_far1, mixed_far1, kf, sf = attend_far(
        now(dec_meta), dec_blocks, None, attn_t, (out_w, 1), 1, True, gain[3]
    )
    mark(sf)
    feed_step()
    enc_mid, norm_b = close(now(kn_enc), c_enc, x_enc, enc_in, gain[1], "close_enc_attn")
    mark(norm_b)
    rows_b = gather_blocks(norm_b)
    x_self = seq_swap(mark(far_payload(kf, now(sf))), 2)
    logs_near1, mixed_near1, kn, sn = attend_near(dec_meta, now(q1), k1, v1, (out_w, 1), 1, True)
    mark(sn)
    c_self = seq_swap(sn, 1)
    feed_got = [clock.finish(x) for x in feed_rings]
    feed_got = [[now(got[0]), *got[1:]] for got in feed_got]
    if packed:
        inner_cols, outer_rows = gathered_feeds(feed_got[0], orow, "gather_feeds")
    else:
        inner_cols = gathered_rows(feed_got[0], "gather_inner")
        outer_rows = gathered_rows(feed_got[1], "gather_outer")
    inner_cols, outer_rows = inner_cols.reshape(4 * D, fc), outer_rows.reshape(2 * fc, D)
    eg1, eu1, eh1, kf, sf = feed_forward((now(rows_b[2]), rows_b[3]), inner_cols, outer_rows, 0, BF16, "enc_feed_far")
    far = mark(far_payload(kf, sf))
    x_enc = seq_swap(far, 2)
    eg0, eu0, eh0, kn_enc, sn = feed_forward((now(rows_b[0]), rows_b[1]), inner_cols, outer_rows, 0, F32, "enc_feed_near")
    mark(sn)
    c_enc = seq_swap(sn, 1)
    dec_mid, norm_d = close(now(kn), c_self, x_self, dec_in, gain[4], "close_self")
    mark(norm_d)
    enc_out, norm_e = close(now(kn_enc), c_enc, x_enc, enc_mid, gain[2], "close_enc_feed")
    mark(norm_e)
    rows_e = gather_blocks(norm_e)
    q0t, q1t = now(q0).T, now(q1).T
    mark(q1t)
    rows_d = gather_blocks(now(norm_d))
    q2, k2, v2, logs_far2, mixed_far2, kf, sf = attend_far(
        now(enc_meta), plain(rows_d), plain(rows_e), attn_t, (out_w, 2), 2, False
    )
    far = mark(far_payload(kf, sf))
    x_dec = seq_swap(far, 2)
    logs_near2, mixed_near2, kn, sn = attend_near(enc_meta, now(q2), k2, v2, (out_w, 2), 2, False)
    mark(sn)
    dec_late, norm_f = close(now(kn), seq_swap(tie(sn, x_dec), 1), x_dec, dec_mid, gain[5], "close_cross")
    mark(norm_f)
    rows_f = gather_blocks(norm_f)
    dg0, du0, dh0, kn_out, sn_out = feed_forward(
        (now(rows_f[0]), rows_f[1]), inner_cols, outer_rows, 1, F32, "dec_feed_near"
    )
    mark(dh0)
    a0, b0, kn_dec, sn_dec = feed_back(
        seed_blocks[:2], now(dg0), du0, inner_cols, outer_rows, 1, F32, "dec_feed_back_near"
    )
    mark(sn_dec)
    c_dec = seq_swap(sn_dec, 1)
    dg1, du1, dh1, kf_out, sf_out = feed_forward(
        (now(rows_f[2]), rows_f[3]), inner_cols, outer_rows, 1, BF16, "dec_feed_far"
    )
    mark(dh1)
    a1, b1, kf, sf = feed_back(seed_blocks[2:], now(dg1), du1, inner_cols, outer_rows, 1, BF16, "dec_feed_back_far")

    far = mark(far_payload(kf, sf))
    x_dec = seq_swap(far, 2)
    dec_feed = feed_weight(
        rows_f, seed_blocks, (now(a0), a1), (b0, b1), (dh0, dh1), packed, "dec_feed_weight"
    )
    mark(dec_feed[-1])
    up_five, low, gain_five = close_back(now(kn_dec), c_dec, x_dec, dec_late, gain[5], seed, "back_dec_feed")
    mark(low)
    dz_cross = plain(gather_blocks(low))
    half = nb // 2
    feed_shapes = [(ns * ir, fc), (orow, D)]

    def pair_send(kept, sent):
        return kept, batch_swap(mark(sent), 1)

    def feed_parts(grads):
        if packed:
            return [pair_send(*grads)]
        blocks = [now(x).reshape((half,) + shape) for x, shape in zip(grads, feed_shapes)]
        return [pair_send(*pair_blocks(x)) for x in blocks]

    dec_parts = feed_parts(dec_feed)
    far_out = mark(far_payload(kf_out, sf_out))

    q2t = mark(now(q2).T)
    out_sent = out_weight([(dz_cross, now(mixed_near2), mixed_far2)], "cross_out_weight")
    mark(out_sent[1])
    out_got = send_blocks(out_sent)
    x_out = seq_swap(tie(far_out, out_sent[1]), 2)
    c_out = seq_swap(tie(sn_out, out_sent[1]), 1)
    decoder_layer_output = (dec_late + kn_out + c_out.astype(F32) + x_out.astype(F32)).astype(BF16)
    cross_d, outs = attend_back(
        now(enc_meta), dz_cross, q2t, attn_t, (out_w, 2), 2, (q2, k2, v2, logs_near2, logs_far2), dr, er, False, True
    )
    far = mark(far_payload(outs[6], tie(outs[7], x_out, c_out, out_got[2])))
    x_enc, c_enc = seq_swap(far, 2), seq_swap(now(outs[5]), 1)
    c_far, c_dec = seq_swap(now(outs[3]), 1), seq_swap(now(outs[1]), 1)
    kf_dec, kn_dec = outs[2], outs[0]
    cross_w = attend_weights(plain(rows_d), plain(rows_e), (now(cross_d[0]), *cross_d[1:]), "cross_weights")
    mark(cross_w[0])
    three = attn_parts([now(out_got[0]), *out_got[1:]], [(cross_w[1:], 2)], ns * ar, "part_three")
    mark(three[1])
    up_two, low, gain_two = close_back(now(outs[4]), c_enc, x_enc, enc_out, gain[2], None, "back_encoded")
    mark(low)
    dz = gather_blocks(low)
    far_dec = mark(add_low(kf_dec, now(c_far)))
    part_three = (three[0], batch_swap(three[1], 1))
    mark([far_dec] + [got for _, got in dec_parts])
    a0, b0, kn_enc, sn = feed_back(plain(dz[:2]), now(eg0), eu0, inner_cols, outer_rows, 0, F32, "enc_feed_back_near")
    mark(sn)
    c_enc = seq_swap(sn, 1)
    x_dec = seq_swap(tie(far_dec, dz[2], sn), 2)
    mark([sn, part_three[1]])
    dz = plain(dz)
    a1, b1, kf, sf = feed_back(dz[2:], now(eg1), eu1, inner_cols, outer_rows, 0, BF16, "enc_feed_back_far")
    far = mark(far_payload(kf, tie(sf, x_dec)))
    x_enc = seq_swap(far, 2)
    enc_feed = feed_weight(
        rows_b, dz, (now(a0), a1), (b0, b1), (eh0, eh1), packed, "enc_feed_weight"
    )
    mark(enc_feed[-1])
    enc_parts = feed_parts(enc_feed)
    up_four, low_self, gain_four = close_back(now(kn_dec), c_dec, x_dec, dec_mid, gain[4], up_five, "back_cross")
    mark(low_self)
    dz_self = plain(gather_blocks(low_self))
    up_one, low, gain_one = close_back(now(kn_enc), c_enc, x_enc, enc_mid, gain[1], up_two, "back_enc_feed")
    mark(low)
    dz_enc = gather_blocks(low)
    self_d, outs = attend_back(
        now(dec_meta), dz_self, q1t, attn_t, (out_w, 1), 1, (q1, k1, v1, logs_near1, logs_far1), dr, dr, True, False
    )
    mark(outs[3])
    self_w = attend_weights(quarters(rows_c), None, (now(self_d[0]), *self_d[1:]), "self_weights")
    mark(self_w[0])
    flight = []
    feeds = [ring_reduce([e, d], "feed_hop", None, flight) for e, d in zip(enc_parts, dec_parts)]
    for x in feeds:
        next(x)
    kn_self, c_self = outs[0], seq_swap(tie(outs[1], dz_enc[2]), 1)
    sf_self = seq_swap(tie(outs[3], dz_enc[2]), 1)
    dz_enc = plain(dz_enc)
    out_late = out_weight(
        [(dz_enc, now(mixed_near0), mixed_far0), (dz_self, mixed_near1, mixed_far1)], "late_out_weight"
    )
    mark(out_late[1])
    got_late = send_blocks(out_late)
    x_self = seq_swap(mark(add_low(outs[2], now(sf_self))), 2)
    for x in feeds:
        clock.step(x)
    enc_d, outs = attend_back(
        now(enc_meta), dz_enc, q0t, attn_t, (out_w, 0), 0, (q0, k0, v0, logs_near0, logs_far0), er, er, False, False
    )
    mark([outs[3], x_self, got_late[2], *flight])
    c_far, c_enc = seq_swap(outs[3], 1), seq_swap(now(outs[1]), 1)
    part_zero = pair_send(
        *self_part(quarters(rows_a), (now(enc_d[0]), *enc_d[1:]), ns * ar, "part_zero")
    )
    for x in feeds:
        clock.step(x)
    part_middle = pair_send(
        *attn_parts(
            [now(got_late[0]), *got_late[1:]],
            [(self_w[:2], 0), ((self_w[2], cross_w[0]), 1)],
            ns * ar,
            "part_middle",
        )
    )
    far = mark(add_low(now(outs[2]), c_far))
    x_enc = seq_swap(far, 2)
    decoder_input_gradient, _, gain_three = close_back(
        now(kn_self), c_self, x_self, dec_in, gain[3], up_four, "back_self"
    )
    mark(gain_three)
    for x in feeds:
        clock.step(x)
    encoder_input_gradient, _, gain_zero = close_back(
        now(outs[0]), c_enc, x_enc, enc_in, gain[0], up_one, "back_enc_attn"
    )
    mark(gain_zero)

    gain_lines = spread(
        [now(gain_zero), gain_one, gain_two, gain_three, gain_four, gain_five], nb, ns * ar
    )
    mark(gain_lines)
    last_ring = ring_reduce([part_zero, part_middle, part_three], "attn_hop", gain_lines)
    next(last_ring)
    clock.step(last_ring)
    feeds_done = [clock.finish(x)[0] for x in feeds]
    if packed:
        feed_sent, outer_grad = feed_pack(mark(feeds_done[0]), ir, fc, orow)
        mark(feed_sent[1])
        feed_got = send_some(feed_sent)
    else:
        inner_part, outer_grad = feeds_done
        inner_part = mark(now(inner_part).astype(BF16).reshape(ns, ir, fc))
        inner_part = seq_exchange(inner_part, s)
    clock.step(last_ring)
    outer_new = adam(2, outer_master, outer_first, outer_second, now(outer_grad))
    mark(outer_new[3])
    clock.step(last_ring)
    if packed:
        inner_grad = feed_unpack(send_rest([now(feed_got[0]), *feed_got[1:]], clock.last))
    else:
        inner_grad = inner_part.reshape(ns, ir, cuts, orow).transpose(1, 2, 0, 3).reshape(ir, FF).astype(F32)
    mark(inner_grad)
    (attn_sum,) = clock.finish(last_ring)
    mine = tail_pack(mark(attn_sum), ar, gr)
    mark(mine[-1])
    inner_new = adam(1, inner_master, inner_first, inner_second, now(inner_grad))
    mark(inner_new[3])
    attn_grad, gain_kept, gain_sent = tail_unpack(mine, s, ar, gr, now, clock.last)
    gain_got = batch_swap(gain_sent, 1)
    attn_new = adam(0, attn_master, attn_first, attn_second, attn_grad)
    others = (attn_new, inner_new, outer_new)
    gain_grad, *gain_new, own_squares = gain_adam(
        gain_kept, tie(gain_got, attn_new[3]), masters[3], gain_first[None], gain_second[None], squares, [x[3] for x in others]
    )
    results = (*others, gain_new)
    all_squares = sum_all(own_squares)
    last = lamb(all_squares, masters, [x[2] for x in results])
    grads = (attn_grad, inner_grad, outer_grad, gain_grad)

    def flat(four):
        return (*four[:3], four[3][0])

    return (
        decoder_layer_output[None],
        encoder_input_gradient[None],
        decoder_input_gradient[None],
        *flat(grads),
        *flat([x[0] for x in results]),
        *flat([x[1] for x in results]),
        *last,
    )


def solution(mesh):
    rows = P("batch", "seq", None)
    matrix = P(("batch", "seq"), None)
    vector = P(("batch", "seq"))
    kinds = (matrix, matrix, matrix, vector)
    return jax.shard_map(
        per_device,
        mesh=mesh,
        in_specs=(rows, rows, rows, P("batch"), P("batch")) + kinds * 3,
        out_specs=(rows, rows, rows) + kinds * 5 + (P(), P()),
        check_vma=False,
    )
```

```python
import functools
import math

import jax
import jax.numpy as jnp
from jax import lax
from jax.experimental import pallas as pl
from jax.experimental.pallas import tpu as pltpu
from jax.sharding import PartitionSpec as P

D = 768
HEADS = 12
HEAD = 64
FF = 2048
STEP = 5

eps_norm = 1e-06
adam_eps = 1e-06
lamb_rate = 0.5
decay_weight = 0.01
masked_score = -1000000000.0

F32 = jnp.float32
BF16 = jnp.bfloat16

FLOPS, BYTES = 10**13, 10**10


def seq_swap(x, k):
    n = lax.axis_size("seq")
    return lax.ppermute(x, "seq", [(i, i ^ k) for i in range(n)])


def batch_swap(x, k):
    n = lax.axis_size("batch")
    return lax.ppermute(x, "batch", [(i, i ^ k) for i in range(n)])


def gather_blocks(x):
    other, near = seq_swap(x, 2), seq_swap(x, 1)
    return [x, near, other, seq_swap(tie(other, near), 1)]


def xor_blocks(x, s):
    n = x.shape[0]
    for k in (1, 2):
        swapped = jnp.stack([x[j ^ k] for j in range(n)])
        x = jnp.where((s & k) != 0, swapped, x)
    return x


def seq_exchange(blocks, s):
    n = blocks.shape[0]
    mine = xor_blocks(blocks, s)
    got = jnp.stack([mine[0]] + [seq_swap(mine[j], j) for j in range(1, n)])
    return xor_blocks(got, s)


def tie(x, *others):
    return lax.optimization_barrier((x, others))[0]


def ring_shift(x, active=None):
    nb = lax.axis_size("batch")
    return lax.ppermute(x, "batch", [(i, (i + 2) % nb) for i in (range(nb) if active is None else active)])


def ring_gather(block):
    rounds = lax.axis_size("batch") // 2
    after = yield None
    moving, got, paired = block if after is None else tie(block, after), [], None
    for k in range(rounds):
        following = None
        if k + 1 < rounds:
            payload = moving if paired is None else tie(moving, paired)
            following = ring_shift(payload)
        got.append(moving)
        paired = batch_swap(moving if following is not None or paired is None else tie(moving, paired), 1)
        got.append(paired)
        after = yield moving if following is None else payload
        if following is not None:
            moving = following if after is None else tie(following, after)
            paired = got[-1]
    yield got


def assemble_body(by_lanes, moves, count, low, *refs):
    here = len(refs) - 1 - low[1]
    ins, outs, sem = refs[:here], refs[here:-1], refs[-1]
    b = lax.axis_index("batch")
    z, y = b // 2, b % 2
    ring, copies = count // 2, []
    for i, ref in enumerate(ins):
        k, e = (low[0] + i) // 2, (low[0] + i) % 2
        at = lax.rem(z + ring - k, ring) * 2 + (y + e - 2 * y * e)
        for which, (r0, r1), (c0, c1), (to_row, to_lane) in moves:
            out = outs[which]
            rows = pl.ds(to_row, r1 - r0)
            if by_lanes:
                start = pl.multiple_of(at * (out.shape[1] // count) + to_lane, 128)
                target = out.at[rows, pl.ds(start, c1 - c0)]
            else:
                target = out.at[at, rows, pl.ds(to_lane, c1 - c0)]
            copies.append(pltpu.make_async_copy(ref.at[r0:r1, c0:c1], target, sem.at[len(copies)]))
    for copy in copies:
        copy.start()
    for copy in copies:
        copy.wait()


def assemble(blocks, moves, shapes, by_lanes, name, last=0):
    count = len(blocks)
    outs = [jax.ShapeDtypeStruct((h, count * w) if by_lanes else (count, h, w), BF16) for h, w in shapes]
    any_space = pl.BlockSpec(memory_space=pl.ANY)
    made = []
    for low, high in ((0, count - last), (count - last, count)):
        if low == high:
            continue
        part_of = blocks[low:high]

        def body(*refs, low=low, made=tuple(made), part_of=part_of):
            given = refs[: len(part_of)]
            assemble_body(by_lanes, moves, count, (low, len(outs)), *given, *refs[len(part_of) + len(made) :])

        made = pl.pallas_call(
            body,
            in_specs=[pl.BlockSpec(memory_space=pltpu.VMEM)] * len(part_of) + [any_space] * len(made),
            out_specs=[any_space] * len(outs),
            out_shape=outs,
            input_output_aliases={len(part_of) + i: i for i in range(len(made))},
            scratch_shapes=[pltpu.SemaphoreType.DMA((len(part_of) * len(moves),))],
            cost_estimate=pl.CostEstimate(flops=FLOPS, bytes_accessed=BYTES, transcendentals=0),
            name=f"{name}_{low}",
        )(*part_of, *made)
    return made


def gathered_rows(got, name):
    h, w = got[0].shape
    return assemble(got, [(0, (0, h), (0, w), (0, 0))], [(h, w)], False, name)[0]


def gathered_lanes(got, name):
    h, w = got[0].shape
    if w % 128 == 0:
        return assemble(got, [(0, (0, h), (0, w), (0, 0))], [(h, w)], True, name)[0]
    return gathered_rows(got, name).swapaxes(0, 1).reshape(h, -1)


def gathered_feeds(got, rows, name):
    h, w = got[0].shape
    fc = w - 256
    moves = [(0, (0, h), (0, fc), (0, 0))]
    for g in range(D // 128):
        r, c = g % 3 * rows, fc + g // 3 * 128
        moves.append((1, (r, r + rows), (c, c + 128), (0, 128 * g)))
    return assemble(got, moves, [(h, fc), (rows, D)], False, name, 2)


def pair_blocks(blocks):
    y = lax.axis_index("batch") % 2
    pairs = blocks.reshape((blocks.shape[0] // 2, 2) + blocks.shape[1:])
    return [lax.dynamic_index_in_dim(pairs, i, 1, keepdims=False) for i in (y, 1 - y)]


def hop_body(step, counts, moving, riding, *refs):
    count = len(counts)
    kept, got = refs[:count], refs[count : 2 * count]
    refs = list(refs[2 * count :])
    moved = refs.pop(0) if moving else None
    extra = refs.pop(0) if riding else None
    out, one, two, sem = refs
    ring = lax.axis_size("batch") // 2
    dest = lax.rem(lax.axis_index("batch") // 2 + 2 * ring - step, ring)
    for n in range(count):
        low = sum(counts[:n])

        @pl.when((dest >= low) & (dest < low + counts[n]))
        def _(n=n, low=low):
            mine = pltpu.make_async_copy(kept[n].at[dest - low], one, sem.at[0])
            other = pltpu.make_async_copy(got[n].at[dest - low], two, sem.at[1])
            mine.start()
            other.start()
            mine.wait()
            other.wait()

    total = one[...].astype(F32) + two[...].astype(F32)
    rows = one.shape[0]
    if moving:
        total = total + moved[:rows, :].astype(F32)
    out[:rows, :] = total.astype(out.dtype)
    if riding:
        lines = jnp.concatenate([extra[dest * 2], extra[dest * 2 + 1]], axis=0)
        if moving:
            lines = lines + moved[rows : rows + 2, :].astype(F32)
        out[rows:, :] = jnp.concatenate([lines, jnp.zeros((14, lines.shape[1]), F32)], axis=0).astype(out.dtype)


def hop(parts, step, moved, extra, dtype, name):
    shape = parts[0][0].shape[1:]
    arrays = [k for k, _ in parts] + [g for _, g in parts]
    specs = [pl.BlockSpec(memory_space=pl.ANY)] * len(arrays)
    for x in (moved, extra):
        if x is not None:
            arrays.append(x)
            specs.append(pl.BlockSpec(memory_space=pltpu.VMEM))
    out = shape if extra is None else (shape[0] + 16, shape[1])
    return pl.pallas_call(
        functools.partial(hop_body, step, [k.shape[0] for k, _ in parts], moved is not None, extra is not None),
        in_specs=specs,
        out_specs=pl.BlockSpec(memory_space=pltpu.VMEM),
        out_shape=jax.ShapeDtypeStruct(out, dtype),
        scratch_shapes=[pltpu.VMEM(shape, BF16), pltpu.VMEM(shape, BF16), pltpu.SemaphoreType.DMA((2,))],
        cost_estimate=pl.CostEstimate(flops=FLOPS, bytes_accessed=BYTES, transcendentals=0),
        name=f"{name}_{step}",
    )(*arrays)


def ring_reduce(parts, name, extra=None, flight=None):
    ring = lax.axis_size("batch") // 2
    after = yield None
    moved = None
    for k in range(1, ring + 1):
        if moved is None:
            held = [(kept if after is None else tie(kept, after), got) for kept, got in parts]
        else:
            held, moved = parts, tie(moved, after)
        if k == ring:
            yield [hop(held, k, moved, extra, F32, name)]
            return
        sent = hop(held, k, moved, extra, BF16, name)
        moved = ring_shift(sent)
        if flight is not None:
            flight.append(moved)
        after = yield sent


def sum_seq(x):
    for k in (1, 2):
        x = x + seq_swap(x, k)
    return x


def sum_all(x):
    x = sum_seq(x)
    k = 1
    while k < lax.axis_size("batch"):
        x = x + batch_swap(x, k)
        k *= 2
    return x


class Clock:
    def __init__(self):
        self.last = None

    def now(self, x):
        return x if self.last is None else tie(x, self.last)

    def mark(self, x):
        self.last = x
        return x

    def step(self, work):
        got = work.send(self.last)
        return got if isinstance(got, list) else self.mark(got)

    def finish(self, work):
        got = None
        while not isinstance(got, list):
            got = self.step(work)
        return got


def nt(a, b):
    return lax.dot_general(a, b, (((1,), (1,)), ((), ())), preferred_element_type=F32)


def nn(a, b):
    return lax.dot_general(a, b, (((1,), (0,)), ((), ())), preferred_element_type=F32)


def tn(a, b):
    return lax.dot_general(a, b, (((0,), (0,)), ((), ())), preferred_element_type=F32)


def whole(x):
    shape = x.shape
    return pl.BlockSpec(shape, lambda i: (0,) * len(shape))


def part(shape, *index):
    return pl.BlockSpec(shape, lambda i: index)


def plain(arrays):
    return [(x, whole(x)) for x in arrays]


SCALARS = pl.BlockSpec(memory_space=pltpu.SMEM)


def call(body, ins, outs, flops, scratch=(), name=None):
    arrays = [a for a, _ in ins]
    specs = [whole(a) if s is None else s for a, s in ins]
    shapes = [jax.ShapeDtypeStruct(s, d) for s, d in outs]
    return pl.pallas_call(
        body,
        grid=(1,),
        in_specs=specs,
        out_specs=[whole(o) for o in shapes],
        out_shape=shapes,
        scratch_shapes=list(scratch),
        cost_estimate=pl.CostEstimate(flops=FLOPS, bytes_accessed=BYTES, transcendentals=0),
        name=name,
    )(*arrays)


def positions(shape, axis, owner, rows):
    at = lax.broadcasted_iota(jnp.int32, shape, axis)
    shift = rows.bit_length() - 1
    return ((owner ^ (at >> shift)) << shift) + (at & (rows - 1))


def score_bias(meta, first_row, tile, q_rows, k_rows, causal):
    keys = positions((1, 4 * k_rows), 1, meta[0], k_rows)
    if not causal:
        return jnp.where(keys < meta[1], 0.0, masked_score)
    at = first_row + lax.broadcasted_iota(jnp.int32, (tile, 1), 0)
    shift = q_rows.bit_length() - 1
    queries = ((meta[0] ^ (at >> shift)) << shift) + (at & (q_rows - 1))
    return jnp.where((keys <= queries) & (keys < meta[1]), 0.0, masked_score)


def head_mask(shape, h):
    lane = lax.broadcasted_iota(jnp.int32, shape, 1)
    return (lane >= h * HEAD) & (lane < (h + 1) * HEAD)


def attend_tile(q, k, v, bias, heads):
    mixed = jnp.zeros(q.shape, F32)
    logs = jnp.zeros((q.shape[0], 128), F32)
    q = (q.astype(F32) * 0.125).astype(BF16)
    lane = lax.broadcasted_iota(jnp.int32, logs.shape, 1)
    for h in range(heads):
        mask = head_mask(q.shape, h)
        scores = nt(jnp.where(mask, q, jnp.zeros_like(q)), k) + bias
        peak = jnp.max(scores, axis=-1, keepdims=True)
        expo = jnp.exp(scores - peak)
        total = jnp.sum(expo, axis=-1, keepdims=True)
        probs = (expo * (1.0 / total)).astype(BF16)
        mixed = jnp.where(mask, nn(probs, v), mixed)
        logs = jnp.where(lane == h, peak + jnp.log(total), logs)
    return mixed, logs


def attend_rows(meta, q_ref, k_ref, v_ref, wo_ref, first, q_rows, k_rows, causal, outs):
    logs_ref, mixed_ref = outs[:2]
    heads, rows = q_ref.shape[1] // HEAD, 2 * q_rows
    bias = score_bias(meta, first, rows, q_rows, k_rows, causal)
    mixed, logs = attend_tile(q_ref[first : first + rows, :], k_ref[...], v_ref[...], bias, heads)
    logs_ref[...] = logs
    mixed_ref[...] = mixed.astype(BF16)
    if wo_ref is not None:
        for n in range(2):
            out = outs[2 + n]
            out[...] = nn(mixed_ref[n * q_rows : (n + 1) * q_rows, :], wo_ref[...]).astype(out.dtype)


def project_body(rows, mixed_ref, wo_ref, keep_ref, send_ref):
    for n, out in enumerate((keep_ref, send_ref)):
        out[...] = nn(mixed_ref[n * rows : (n + 1) * rows, :], wo_ref[...]).astype(out.dtype)


def project(mixed, out_w, keep, name):
    rows, dc = mixed.shape[0] // 2, mixed.shape[1]
    return call(
        functools.partial(project_body, rows),
        [(mixed, None), out_weights(out_w)],
        [((rows, D), keep), ((rows, D), BF16)],
        4 * rows * dc * D,
        name=name,
    )


def attend_far_body(cross, raw, fused, causal, q_rows, k_rows, *refs):
    refs = list(refs)
    meta = refs.pop(0)
    queries, refs = refs[:4], refs[4:]
    sources = queries
    if cross:
        sources, refs = refs[:4], refs[4:]
    if raw:
        gain = refs.pop(0)
    wq, wk, wv = refs[:3]
    refs = refs[3:]
    wo = refs.pop(0) if fused else None
    if raw:
        rows_ref = refs.pop(0)
        for j in range(4):
            h = queries[j][...].astype(F32)
            inverse = lax.rsqrt(jnp.mean(h * h, axis=-1, keepdims=True) + eps_norm)
            rows_ref[j * q_rows : (j + 1) * q_rows, :] = (h * inverse * gain[...]).astype(BF16)
        queries = sources = [rows_ref.at[j * q_rows : (j + 1) * q_rows, :] for j in range(4)]
    q_ref, k_ref, v_ref = refs[:3]
    outs = refs[3:]
    for j in range(4):
        q_ref[j * q_rows : (j + 1) * q_rows, :] = nt(queries[j][...], wq[...]).astype(BF16)
        rows = sources[j][...]
        k_ref[j * k_rows : (j + 1) * k_rows, :] = nt(rows, wk[...]).astype(BF16)
        v_ref[j * k_rows : (j + 1) * k_rows, :] = nt(rows, wv[...]).astype(BF16)
    attend_rows(meta, q_ref, k_ref, v_ref, wo, 2 * q_rows, q_rows, k_rows, causal, outs)


def attend_near_body(fused, causal, q_rows, k_rows, meta, q_ref, k_ref, v_ref, *rest):
    wo, outs = (rest[0], rest[1:]) if fused else (None, rest)
    attend_rows(meta, q_ref, k_ref, v_ref, wo, 0, q_rows, k_rows, causal, outs)


def attn_weights(attn_t, group):
    return [(attn_t, part((D // 4, D), 0, 4 * group + i)) for i in range(3)]


def out_weights(out_w):
    stack, place = out_w
    return (stack, pl.BlockSpec((None, stack.shape[1], D), lambda i: (place, 0, 0)))


def half_outs(q_rows, dc, keep):
    return [((2 * q_rows, 128), F32), ((2 * q_rows, dc), BF16), ((q_rows, D), keep), ((q_rows, D), BF16)]


def attend_far(meta, queries, sources, attn_t, out_w, group, causal, gain=None):
    cross, raw, fused = sources is not None, gain is not None, out_w is not None
    q_rows, dc = queries[0][1].block_shape[0], D // 4
    k_rows = sources[0][1].block_shape[0] if cross else q_rows
    flops = 2 * D * dc * (4 * q_rows + 8 * k_rows) + 16 * q_rows * k_rows * D
    return call(
        functools.partial(attend_far_body, cross, raw, fused, causal, q_rows, k_rows),
        [(meta, SCALARS)]
        + list(queries)
        + (list(sources) if cross else [])
        + ([(gain, None)] if raw else [])
        + attn_weights(attn_t, group)
        + ([out_weights(out_w)] if fused else []),
        ([((4 * q_rows, D), BF16)] if raw else [])
        + [((4 * q_rows, dc), BF16), ((4 * k_rows, dc), BF16), ((4 * k_rows, dc), BF16)]
        + half_outs(q_rows, dc, BF16)[: 4 if fused else 2],
        flops,
        name=f"attend_far_{group}",
    )


def attend_near(meta, q, k, v, out_w, group, causal):
    q_rows, k_rows, dc, fused = q.shape[0] // 4, k.shape[0] // 4, q.shape[1], out_w is not None
    return call(
        functools.partial(attend_near_body, fused, causal, q_rows, k_rows),
        [(meta, SCALARS), (q, part((2 * q_rows, dc), 0, 0)), (k, None), (v, None)]
        + ([out_weights(out_w)] if fused else []),
        half_outs(q_rows, dc, F32)[: 4 if fused else 2],
        16 * q_rows * k_rows * D,
        name=f"attend_near_{group}",
    )


STEPS = 1


def row_call(body, ins, outs, name):
    rows = ins[0].shape[0]

    def spec(shape):
        if shape[0] == 1:
            return pl.BlockSpec(shape, lambda i: (0, 0))
        return pl.BlockSpec((rows // STEPS,) + tuple(shape[1:]), lambda i: (i, 0))

    return pl.pallas_call(
        body,
        grid=(STEPS,),
        in_specs=[spec(x.shape) for x in ins],
        out_specs=[spec(s) for s, _ in outs],
        out_shape=[jax.ShapeDtypeStruct(s, d) for s, d in outs],
        cost_estimate=pl.CostEstimate(flops=FLOPS, bytes_accessed=BYTES, transcendentals=0),
        name=name,
    )(*ins)


def add_low(a, b):
    return (a.astype(F32) + b.astype(F32)).astype(BF16)


def far_payload(keep_far, send_far):
    return add_low(keep_far, seq_swap(send_far, 1))


def close_body(near_ref, core_ref, far_ref, residual_ref, gain_ref, out_ref, normed_ref):
    h = residual_ref[...].astype(F32) + near_ref[...] + core_ref[...].astype(F32) + far_ref[...].astype(F32)
    inverse = lax.rsqrt(jnp.mean(h * h, axis=-1, keepdims=True) + eps_norm)
    out_ref[...] = h
    normed_ref[...] = (h * inverse * gain_ref[...]).astype(BF16)


def close(near, core, far, residual, gain, name):
    return row_call(
        close_body, [near, core, far, residual, gain], [(near.shape, F32), (near.shape, BF16)], name
    )


def close_back_body(near_ref, core_ref, far_ref, stream_ref, gain_ref, *rest):
    if len(rest) == 4:
        upstream_ref, rest = rest[0], rest[1:]
    else:
        upstream_ref = None
    out_ref, low_ref, dgain_ref = rest
    h = stream_ref[...].astype(F32)
    up = near_ref[...] + core_ref[...].astype(F32) + far_ref[...].astype(F32)
    inverse = lax.rsqrt(jnp.mean(h * h, axis=-1, keepdims=True) + eps_norm)
    unit = h * inverse
    scaled = up * gain_ref[...]
    grad = inverse * (scaled - unit * jnp.mean(scaled * unit, axis=-1, keepdims=True))
    if upstream_ref is not None:
        grad = upstream_ref[...].astype(F32) + grad
    out_ref[...] = grad
    low_ref[...] = grad.astype(BF16)

    @pl.when(pl.program_id(0) == 0)
    def _():
        dgain_ref[...] = jnp.zeros_like(dgain_ref)

    dgain_ref[...] += jnp.sum(up * unit, axis=0, keepdims=True)


def close_back(near, core, far, stream, gain, upstream, name):
    shape = near.shape
    ins = [near, core, far, stream, gain] + ([] if upstream is None else [upstream])
    return row_call(close_back_body, ins, [(shape, F32), (shape, BF16), ((1, shape[1]), F32)], name)


def attend_back_body(cross, causal, q_rows, k_rows, tile, *refs):
    meta = refs[0]
    dz = refs[1:5]
    q_ref, qt_ref, k_ref, v_ref, logs_near, logs_far, wq, wk, wv, wo = refs[5:15]
    dq_ref, dkt_ref, dvt_ref = refs[15:18]
    outs = refs[18 : 18 + (8 if cross else 4)]
    do_ref, dot_ref, dkt_sum, dvt_sum, logs_ref = refs[18 + len(outs) :]
    heads = q_ref.shape[1] // HEAD
    for j in range(4):
        at = slice(j * q_rows, (j + 1) * q_rows)
        rows = dz[j][...]
        do_ref[at, :] = nt(rows, wo[...]).astype(BF16)
        dot_ref[:, at] = nt(wo[...], rows).astype(BF16)
    logs_ref[: 2 * q_rows, :] = logs_near[...]
    logs_ref[2 * q_rows :, :] = logs_far[...]
    dkt_sum[...] = jnp.zeros_like(dkt_sum)
    dvt_sum[...] = jnp.zeros_like(dvt_sum)

    def step(t, carry):
        at = pl.ds(pl.multiple_of(t * tile, tile), tile)
        q, do = q_ref[at, :], do_ref[at, :]
        q = (q.astype(F32) * 0.125).astype(BF16)
        qt, dot = qt_ref[:, at], dot_ref[:, at]
        logs = logs_ref[at, :]
        bias = score_bias(meta, t * tile, tile, q_rows, k_rows, causal)
        dq = jnp.zeros(q.shape, F32)
        for h in range(heads):
            mask = head_mask(q.shape, h)
            zero = jnp.zeros_like(q)
            probs = jnp.exp(nt(jnp.where(mask, q, zero), k_ref[...]) + bias - logs[:, h : h + 1])
            grad_probs = nt(jnp.where(mask, do, zero), v_ref[...])
            weighted = probs * grad_probs
            center = jnp.sum(weighted, axis=-1, keepdims=True)
            grad_scores = (weighted - probs * center).astype(BF16)
            feats = slice(h * HEAD, (h + 1) * HEAD)
            dvt_sum[feats, :] += nn(dot[feats, :], probs.astype(BF16))
            dkt_sum[feats, :] += nn(qt[feats, :], grad_scores)
            dq = jnp.where(mask, nn(grad_scores, k_ref[...]), dq)
        dq_ref[at, :] = (dq * 0.125).astype(BF16)
        return carry

    lax.fori_loop(0, 4 * q_rows // tile, step, 0)
    dkt_ref[...] = (dkt_sum[...] * 0.125).astype(BF16)
    dvt_ref[...] = dvt_sum[...].astype(BF16)

    def query_part(j):
        return nn(dq_ref[j * q_rows : (j + 1) * q_rows, :], wq[...])

    def source_part(j):
        at = slice(j * k_rows, (j + 1) * k_rows)
        return tn(dkt_ref[:, at], wk[...]) + tn(dvt_ref[:, at], wv[...])

    parts = (query_part, source_part) if cross else ((lambda j: query_part(j) + source_part(j)),)
    for n, make in enumerate(parts):
        for j in range(4):
            outs[4 * n + j][...] = make(j).astype(outs[4 * n + j].dtype)


def attend_back(meta, dz, qt, attn_t, out_w, group, saved, q_rows, k_rows, causal, cross):
    q, k, v, logs_near, logs_far = saved
    dc = q.shape[1]
    tile = min(1024, 4 * q_rows)

    def four(rows):
        return [((rows, D), F32), ((rows, D), BF16), ((rows, D), BF16), ((rows, D), BF16)]

    outs = call(
        functools.partial(attend_back_body, cross, causal, q_rows, k_rows, tile),
        [(meta, SCALARS)]
        + list(dz)
        + [(q, None), (qt, None), (k, None), (v, None), (logs_near, None), (logs_far, None)]
        + attn_weights(attn_t, group)
        + [out_weights(out_w)],
        [((4 * q_rows, dc), BF16), ((dc, 4 * k_rows), BF16), ((dc, 4 * k_rows), BF16)]
        + (four(q_rows) + four(k_rows) if cross else four(q_rows)),
        80 * q_rows * k_rows * D + 4 * D * dc * (4 * q_rows + 4 * k_rows),
        [
            pltpu.VMEM((4 * q_rows, dc), BF16),
            pltpu.VMEM((dc, 4 * q_rows), BF16),
            pltpu.VMEM((dc, 4 * k_rows), F32),
            pltpu.VMEM((dc, 4 * k_rows), F32),
            pltpu.VMEM((4 * q_rows, 128), F32),
        ],
        f"attend_back_{group}",
    )
    return outs[:3], outs[3:]


def attend_weights_body(cross, q_rows, k_rows, *refs):
    queries = refs[0:4]
    sources = refs[4:8] if cross else queries
    dq, dkt, dvt, *outs = refs[8:] if cross else refs[4:]
    gq = gk = gv = None
    for j in range(4):
        at, ak = slice(j * q_rows, (j + 1) * q_rows), slice(j * k_rows, (j + 1) * k_rows)
        x, y = queries[j][...], sources[j][...]
        a, b, c = tn(dq[at, :], x), nn(dkt[:, ak], y), nn(dvt[:, ak], y)
        gq, gk, gv = (a, b, c) if j == 0 else (gq + a, gk + b, gv + c)
    for ref, g in zip(outs, (gq, gk, gv)):
        ref[...] = g.astype(BF16)


def attend_weights(queries, sources, grads, name):
    cross = sources is not None
    dq, dkt, dvt = grads
    q_rows, k_rows, dc = dq.shape[0] // 4, dkt.shape[1] // 4, dq.shape[1]
    return call(
        functools.partial(attend_weights_body, cross, q_rows, k_rows),
        list(queries) + (list(sources) if cross else []) + [(dq, None), (dkt, None), (dvt, None)],
        [((dc, D), BF16)] * 3,
        0,
        name=name,
    )


def out_total(dz, near, far, q_rows):
    total = None
    for j, ref in enumerate(dz):
        mixed = (near, far)[j // 2][(j % 2) * q_rows : (j % 2 + 1) * q_rows, :]
        x = tn(ref[...], mixed)
        total = x if j == 0 else total + x
    return total


def out_weight_body(sizes, *refs):
    outs, scratch = refs[6 * len(sizes) : -1], refs[-1]
    s, rows = lax.axis_index("seq"), scratch.shape[2]
    for n, q_rows in enumerate(sizes):
        total = out_total(refs[6 * n : 6 * n + 4], refs[6 * n + 4], refs[6 * n + 5], q_rows)
        for t in range(4):
            scratch[s ^ t, n] = total[t * rows : (t + 1) * rows, :].astype(BF16)
    hand_out(scratch, outs)


def out_weight(groups, name):
    dc = D // 4
    ins, sizes = [], []
    for dz, near, far in groups:
        ins += list(dz) + [(near, None), (far, None)]
        sizes.append(near.shape[0] // 2)
    return call(
        functools.partial(out_weight_body, sizes),
        ins,
        sent_shapes((len(groups), dc, dc), BF16),
        0,
        [pltpu.VMEM((4, len(groups), dc, dc), BF16)],
        name,
    )


GELU_A, GELU_B = math.sqrt(2.0 / math.pi), 0.044715


def feed_forward_body(rows, x0, x1, wg, wu, wd, gate_ref, up_ref, hidden_ref, keep_ref, send_ref):
    for j, x_ref in enumerate((x0, x1)):
        at = slice(j * rows, (j + 1) * rows)
        x = x_ref[...]
        gate, up = nn(x, wg[...]), nn(x, wu[...])
        gate_ref[at, :] = gate
        up_ref[at, :] = up
        inner = jnp.tanh(GELU_A * (gate + GELU_B * (gate * gate * gate)))
        hidden_ref[at, :] = (0.5 * gate * (1.0 + inner) * up).astype(BF16)
        out = (keep_ref, send_ref)[j]
        out[...] = nn(hidden_ref[at, :], wd[...]).astype(out.dtype)


def feed_weights(inner_cols, outer_rows, which):
    fc = inner_cols.shape[1]
    return [
        (inner_cols, part((D, fc), 2 * which, 0)),
        (inner_cols, part((D, fc), 2 * which + 1, 0)),
        (outer_rows, part((fc, D), which, 0)),
    ]


def feed_forward(half, inner_cols, outer_rows, which, keep, name):
    rows, fc = half[0].shape[0], inner_cols.shape[1]
    return call(
        functools.partial(feed_forward_body, rows),
        plain(half) + feed_weights(inner_cols, outer_rows, which),
        [((2 * rows, fc), F32), ((2 * rows, fc), F32), ((2 * rows, fc), BF16), ((rows, D), keep), ((rows, D), BF16)],
        12 * rows * fc * D,
        name=name,
    )


def feed_back_body(rows, d0, d1, gate_ref, up_ref, wg, wu, wd, dgate_ref, dup_ref, keep_ref, send_ref):
    for j, d_ref in enumerate((d0, d1)):
        at = slice(j * rows, (j + 1) * rows)
        dh = nt(d_ref[...], wd[...])
        t, up = gate_ref[at, :], up_ref[at, :]
        square = t * t
        inner = jnp.tanh(GELU_A * t * (1.0 + GELU_B * square))
        slope = 0.5 * (1.0 + inner) + 0.5 * t * (1.0 - inner * inner) * (
            GELU_A * (1.0 + 3.0 * GELU_B * square)
        )
        dgate_ref[at, :] = (dh * up * slope).astype(BF16)
        dup_ref[at, :] = (dh * (0.5 * t * (1.0 + inner))).astype(BF16)
        out = (keep_ref, send_ref)[j]
        out[...] = (nt(dgate_ref[at, :], wg[...]) + nt(dup_ref[at, :], wu[...])).astype(out.dtype)


def feed_back(dz_half, gate, up, inner_cols, outer_rows, which, keep, name):
    rows, fc = gate.shape[0] // 2, inner_cols.shape[1]
    return call(
        functools.partial(feed_back_body, rows),
        list(dz_half) + [(gate, None), (up, None)] + feed_weights(inner_cols, outer_rows, which),
        [((2 * rows, fc), BF16), ((2 * rows, fc), BF16), ((rows, D), keep), ((rows, D), BF16)],
        12 * rows * fc * D,
        name=name,
    )


def feed_weight_body(rows, packed, *refs):
    xs, dzs = refs[0:4], refs[4:8]
    dg, du, hid = refs[8:10], refs[10:12], refs[12:14]
    outs = refs[14:]
    gate = up = down = None
    for j in range(4):
        at = slice((j % 2) * rows, (j % 2 + 1) * rows)
        x = xs[j][...]
        a, b = tn(x, dg[j // 2][at, :]), tn(x, du[j // 2][at, :])
        c = tn(hid[j // 2][at, :], dzs[j][...])
        gate, up, down = (a, b, c) if j == 0 else (gate + a, up + b, down + c)
    fc = gate.shape[1]
    if not packed:
        outs[0][:D, :] = gate.astype(BF16)
        outs[0][D:, :] = up.astype(BF16)
        outs[1][...] = down.astype(BF16)
        return
    out = refs[-1]
    height = out.shape[1]
    for n, grad in enumerate((gate, up)):
        for k in range(2):
            out[2 * n + k, :, :fc] = grad[k * height : (k + 1) * height, :].astype(BF16)
    short = fc // 4
    for q in range(4):
        for g in range(D // 128):
            piece = down[q * short : (q + 1) * short, g * 128 : (g + 1) * 128].astype(BF16)
            r, c = g % 3 * short, fc + g // 3 * 128
            out[q, r : r + short, c : c + 128] = piece
    y = lax.axis_index("batch") % 2
    for i in range(2):
        outs[0][i] = out[2 * i + y]
        outs[1][i] = out[2 * i + 1 - y]


def feed_weight(xs, dzs, dgate, dup, hidden, packed, name):
    rows, fc = xs[0].shape[0], dgate[0].shape[1]
    return call(
        functools.partial(feed_weight_body, rows, packed),
        plain(xs) + list(dzs) + plain((*dgate, *dup, *hidden)),
        [((2, D // 2, fc + 256), BF16)] * 2 if packed else [((2 * D, fc), BF16), ((fc, D), BF16)],
        24 * rows * fc * D,
        [pltpu.VMEM((4, D // 2, fc + 256), BF16)] if packed else [],
        name,
    )


def send_some(mine):
    return [mine[0], seq_swap(mine[1], 1), seq_swap(mine[2], 2)]


def send_rest(got, *after):
    return [*got, seq_swap(tie(got[2], got[1], *after), 1)]


def send_blocks(mine):
    return send_rest(send_some(mine))


def place(scratch, refs, s):
    for j, ref in enumerate(refs):
        scratch[s ^ j] = ref[...] if j < 2 else ref[j - 2]


def hand_out(scratch, outs):
    outs[0][...] = scratch[0]
    outs[1][...] = scratch[1]
    outs[2][0] = scratch[2]
    outs[2][1] = scratch[3]


def sent_shapes(shape, dtype):
    return [(shape, dtype), (shape, dtype), ((2,) + shape, dtype)]


def head_pack_body(ar, gr, lines, attn_ref, gain_ref, inner_ref, *refs):
    outs, feed_outs, scratch, feed_scratch = refs[:3], refs[3:6], refs[6], refs[7]
    s = lax.axis_index("seq")
    width, ir = scratch.shape[2], inner_ref.shape[0]
    dc, room = D // 4, width - ar
    turned = attn_ref[...].T
    gains = jnp.concatenate([gain_ref[...], jnp.zeros((1, lines * room - gr), F32)], axis=1)
    for t in range(4):
        at = s ^ t
        scratch[at, :, ar:] = jnp.zeros((dc, room), BF16)
        scratch[at, :, :ar] = turned[t * dc : (t + 1) * dc, :].astype(BF16)
        for n in range(lines):
            scratch[at, n : n + 1, ar:] = gains[:, n * room : (n + 1) * room].astype(BF16)
        for q in range(4):
            low = (4 * q + t) * 128
            feed_scratch[at, :, q * 128 : (q + 1) * 128] = inner_ref[:, low : low + 128].astype(BF16)
    hand_out(scratch, outs)
    hand_out(feed_scratch, feed_outs)


def attn_unpack_body(ar, gr, lines, *refs):
    ins, (attn_ref, scratch) = refs[0:4], refs[4:]
    place(scratch, ins, lax.axis_index("seq"))
    dc, room = D // 4, scratch.shape[2] - ar
    pieces = []
    for k in range(4):
        attn_ref[:dc, k * ar : (k + 1) * ar] = scratch[k, :, :ar]
        pieces += [scratch[k, n : n + 1, ar : ar + min(room, gr - n * room)].astype(F32) for n in range(lines)]
    pieces.append(jnp.zeros((1, attn_ref.shape[1] - 4 * gr), F32))
    line = jnp.concatenate(pieces, axis=1)
    fill = jnp.zeros((attn_ref.shape[0] - dc - 1, line.shape[1]), F32)
    attn_ref[dc:, :] = jnp.concatenate([line, fill], axis=0).astype(BF16)


def feeds_unpack_body(*refs):
    ins, outer_ref, feed_ref, scratch = refs[0:4], refs[4], refs[5], refs[6]
    place(scratch, ins, lax.axis_index("seq"))
    ir, orow = scratch.shape[1], outer_ref.shape[0]
    for k in range(4):
        feed_ref[k * ir : (k + 1) * ir, :512] = scratch[k]
    for g in range(D // 128):
        r, c = g % 3 * orow, 512 + g // 3 * 128
        feed_ref[r : r + orow, c : c + 128] = outer_ref[:, g * 128 : (g + 1) * 128].astype(BF16)


def head_exchange(attn_master, inner_master, outer_master, gain_master):
    ar, dc, gr = attn_master.shape[0], D // 4, gain_master.shape[0]
    ir, fc = inner_master.shape[0], inner_master.shape[1] // 4
    width = (ar // 128 + 1) * 128
    lines = -(-gr // (width - ar))
    scratch, feed_scratch = pltpu.VMEM((4, dc, width), BF16), pltpu.VMEM((4, ir, fc), BF16)
    outs = call(
        functools.partial(head_pack_body, ar, gr, lines),
        plain([attn_master, gain_master[None], inner_master]),
        sent_shapes((dc, width), BF16) + sent_shapes((ir, fc), BF16),
        0,
        [scratch, feed_scratch],
        "head_pack",
    )
    attn = call(
        functools.partial(attn_unpack_body, ar, gr, lines),
        plain(send_blocks(outs[:3])),
        [((dc + 16, 4 * ar), BF16)],
        0,
        [scratch],
        "attn_unpack",
    )[0]
    feeds = call(
        feeds_unpack_body,
        plain(send_blocks([outs[3], tie(outs[4], attn), tie(outs[5], attn)]) + [outer_master]),
        [((4 * ir, D), BF16)],
        0,
        [feed_scratch],
        "feeds_unpack",
    )[0]
    return attn, feeds


def turn_pack_body(count, *refs):
    ins, outs, scratch = refs[:count], refs[count : count + 3], refs[count + 3]
    s = lax.axis_index("seq")
    dc = scratch.shape[2]
    for t in range(4):
        for g in range(count):
            scratch[s ^ t, g] = ins[g][:, t * dc : (t + 1) * dc].T
    hand_out(scratch, outs)


def turn_pack(ins, name):
    count, dc = len(ins), D // 4
    return call(
        functools.partial(turn_pack_body, count),
        ins,
        sent_shapes((count, dc, dc), BF16),
        0,
        [pltpu.VMEM((4, count, dc, dc), BF16)],
        name,
    )


def lanes_unpack_body(*refs):
    ins, out, scratch = refs[:4], refs[4], refs[5]
    place(scratch, ins, lax.axis_index("seq"))
    width = scratch.shape[3]
    for k in range(4):
        for g in range(scratch.shape[1]):
            out[g, :, k * width : (k + 1) * width] = scratch[k, g]


def lanes_unpack(got, name):
    shape = got[0].shape
    return call(
        lanes_unpack_body,
        plain(got),
        [(shape[:2] + (4 * shape[2],), BF16)],
        0,
        [pltpu.VMEM((4,) + shape, BF16)],
        name,
    )[0]


def tail_pack_body(gr, total_ref, *refs):
    outs, scratch = refs[:3], refs[3]
    s, width = lax.axis_index("seq"), scratch.shape[2]
    dc = D // 4
    for t in range(4):
        scratch[s ^ t, :dc] = total_ref[:dc, t * width : (t + 1) * width].astype(BF16)
        lines = [total_ref[dc + e : dc + e + 1, t * gr : (t + 1) * gr] for e in range(2)]
        lines = jnp.concatenate(lines + [jnp.zeros((1, width - 2 * gr), F32)] * (width > 2 * gr), axis=1)
        scratch[s ^ t, dc:] = jnp.concatenate([lines, jnp.zeros((15, width), F32)], axis=0).astype(BF16)
    hand_out(scratch, outs)


def tail_unpack_body(gr, *refs):
    ins, (out, kept_ref, sent_ref, scratch) = refs[:4], refs[4:]
    place(scratch, ins, lax.axis_index("seq"))
    dc = D // 4
    lines = None
    for k in range(4):
        out[:, k * dc : (k + 1) * dc] = scratch[k, :dc].astype(F32).T
        line = scratch[k, dc:].astype(F32)[:1]
        lines = line if k == 0 else lines + line
    halves = lines[:, :gr], lines[:, gr : 2 * gr]
    first = lax.axis_index("batch") % 2 == 0
    kept_ref[...] = jnp.where(first, halves[0], halves[1])
    sent_ref[...] = jnp.where(first, halves[1], halves[0])


def feed_pack_body(total_ref, *refs):
    outs, outer_ref, scratch = refs[:3], refs[3], refs[4]
    s, (rows, fc), orow = lax.axis_index("seq"), scratch.shape[1:], outer_ref.shape[0]
    for t in range(4):
        scratch[s ^ t] = total_ref[t * rows : (t + 1) * rows, :fc].astype(BF16)
    hand_out(scratch, outs)
    for g in range(D // 128):
        r, c = g % 3 * orow, fc + g // 3 * 128
        outer_ref[:, g * 128 : (g + 1) * 128] = total_ref[r : r + orow, c : c + 128]


def feed_pack(total, ir, fc, orow):
    outs = call(
        feed_pack_body,
        plain([total]),
        sent_shapes((ir, fc), BF16) + [((orow, D), F32)],
        0,
        [pltpu.VMEM((4, ir, fc), BF16)],
        "feed_pack",
    )
    return outs[:3], outs[3]


def feed_unpack_body(*refs):
    ins, out, scratch = refs[:4], refs[4], refs[5]
    place(scratch, ins, lax.axis_index("seq"))
    for k in range(4):
        for q in range(4):
            low = (4 * q + k) * 128
            out[:, low : low + 128] = scratch[k, :, q * 128 : (q + 1) * 128].astype(F32)


def feed_unpack(got):
    ir, fc = got[0].shape
    return call(
        feed_unpack_body, plain(got), [((ir, 4 * fc), F32)], 0, [pltpu.VMEM((4, ir, fc), BF16)], "feed_unpack"
    )[0]


def spread_body(*refs):
    out_ref = refs[6]
    count, width = out_ref.shape[0], out_ref.shape[2]
    per = 6 * D // count
    line = jnp.concatenate([x[...] for x in refs[:6]], axis=1)
    for n in range(count):
        piece = line[:, n * per : (n + 1) * per]
        out_ref[n] = jnp.concatenate([piece, jnp.zeros((1, width - per), F32)], axis=1)


def spread(rows, count, width):
    return call(spread_body, plain(rows), [((count, 1, width), F32)], 0, name="spread")[0]


def tail_pack(total, ar, gr):
    if ar % 16:
        return [total, total]
    shape = (D // 4 + 16, ar)
    mine = call(
        functools.partial(tail_pack_body, gr),
        plain([total]),
        sent_shapes(shape, BF16),
        0,
        [pltpu.VMEM((4,) + shape, BF16)],
        "tail_pack",
    )
    return send_some(mine) + [mine[1]]


def tail_unpack(mine, s, ar, gr, now, *after):
    dc = D // 4
    if ar % 16:
        got = seq_exchange(mine[0][:dc].astype(BF16).reshape(dc, 4, ar).swapaxes(0, 1), s)
        lines = lax.dynamic_slice_in_dim(sum_seq(mine[0][dc : dc + 2]), s * gr, gr, axis=1)
        y = lax.axis_index("batch") % 2
        pair = [lax.dynamic_slice_in_dim(lines, i, 1, axis=0) for i in (y, 1 - y)]
        return (got.reshape(4 * dc, ar).T.astype(F32), *pair)
    got = send_rest(mine[:3], *after)
    return call(
        functools.partial(tail_unpack_body, gr),
        plain([now(got[0]), *got[1:]]),
        [((ar, 4 * dc), F32), ((1, gr), F32), ((1, gr), F32)],
        0,
        [pltpu.VMEM((4, dc + 16, ar), BF16)],
        "tail_unpack",
    )


def split_lanes(scratch, pieces):
    width = scratch.shape[2]
    for n, piece in enumerate(pieces):
        for low in range(n * D, (n + 1) * D, D // 2):
            to = low % width
            scratch[low // width, :, to : to + D // 2] = piece[:, low - n * D : low - n * D + D // 2]


def part_pack_body(positions, *refs):
    count = len(positions)
    ins = refs[4 : 4 + 2 * count]
    kept_ref, sent_ref, squares, scratch = refs[4 + 2 * count :]
    y = lax.axis_index("batch") % 2
    place(squares, refs[:4], lax.axis_index("seq"))
    for n, position in enumerate(positions):
        pieces = [x[...] for x in ins[2 * n : 2 * n + 2]]
        pieces.insert(position, jnp.concatenate([squares[k, n] for k in range(4)], axis=1))
        split_lanes(scratch, pieces)
        kept_ref[n] = scratch[y]
        sent_ref[n] = scratch[1 - y]


def attn_parts(got, parts, width, name):
    dc = D // 4
    if width % 128 or lax.axis_size("batch") != 8:
        joined = []
        matrices = None if got is None else lanes_unpack(got, name)
        for n, (others, position) in enumerate(parts):
            pieces = list(others)
            if got is not None:
                pieces.insert(position, matrices[n])
            joined.append(jnp.concatenate(pieces, axis=1))
        joined = jnp.concatenate(joined, axis=1)
        return pair_blocks(joined.reshape(dc, -1, width).swapaxes(0, 1))
    return call(
        functools.partial(part_pack_body, [position for _, position in parts]),
        plain([*got, *(x for others, _ in parts for x in others)]),
        [((len(parts), dc, width), BF16)] * 2,
        0,
        [pltpu.VMEM((4, len(parts), dc, dc), BF16), pltpu.VMEM((2, dc, width), BF16)],
        name,
    )


def self_part_body(rows, *refs):
    x = refs[0:4]
    dq, dkt, dvt, kept_ref, sent_ref, scratch = refs[4:10]
    gq = gk = gv = None
    for j in range(4):
        at = slice(j * rows, (j + 1) * rows)
        y = x[j][...]
        a, b, c = tn(dq[at, :], y), nn(dkt[:, at], y), nn(dvt[:, at], y)
        gq, gk, gv = (a, b, c) if j == 0 else (gq + a, gk + b, gv + c)
    split_lanes(scratch, [g.astype(BF16) for g in (gq, gk, gv)])
    y = lax.axis_index("batch") % 2
    kept_ref[0] = scratch[y]
    sent_ref[0] = scratch[1 - y]


def self_part(rows, grads, width, name):
    dq, dkt, dvt = grads
    per, dc = dq.shape[0] // 4, dq.shape[1]
    if width % 128 or lax.axis_size("batch") != 8:
        gq, gk, gv = (g.reshape(4, per, dc) for g in (dq, dkt.T, dvt.T))
        made = [
            sum(tn(g[j], x.reshape(4, per, D)[j]) for j, (x, _) in enumerate(rows)).astype(BF16)
            for g in (gq, gk, gv)
        ]
        return attn_parts(None, [(made, 0)], width, name)
    return call(
        functools.partial(self_part_body, per),
        list(rows) + plain([dq, dkt, dvt]),
        [((1, dc, width), BF16)] * 2,
        0,
        [pltpu.VMEM((2, dc, width), BF16)],
        name,
    )


KINDS = ((D, 0), (D, 12), (FF, 16), (D, 18))


def group_mask(count, kind):
    per_group, offset = KINDS[kind]
    axis = 1 if kind < 3 else 0
    shape = (count, 128) if kind < 3 else (128, count)
    at = lax.axis_index(("batch", "seq")) * count + lax.broadcasted_iota(jnp.int32, shape, 1 - axis)
    low = (lax.broadcasted_iota(jnp.int32, shape, axis) - offset) * per_group
    return (at >= low) & (at < low + per_group) & (low >= 0)


def diagonal():
    return lax.broadcasted_iota(jnp.int32, (128, 128), 0) == lax.broadcasted_iota(jnp.int32, (128, 128), 1)


def by_group(values, kind):
    if kind == 3:
        mask = group_mask(values.shape[1], kind)
        column = jnp.sum(jnp.where(mask, values * values, 0.0), axis=1, keepdims=True)
        return jnp.sum(jnp.where(diagonal(), column, 0.0), axis=0, keepdims=True)
    squares = jnp.sum(values * values, axis=1, keepdims=True)
    return jnp.sum(jnp.where(group_mask(values.shape[0], kind), squares, 0.0), axis=0, keepdims=True)


def of_group(row, count, kind):
    if kind == 3:
        column = jnp.sum(jnp.where(diagonal(), row, 0.0), axis=1, keepdims=True)
        return jnp.sum(jnp.where(group_mask(count, kind), column, 0.0), axis=0, keepdims=True)
    return jnp.sum(jnp.where(group_mask(count, kind), row, 0.0), axis=1, keepdims=True)


def square_sums_body(*refs):
    total = by_group(refs[0][...], 0)
    for kind in range(1, 4):
        total = total + by_group(refs[kind][...], kind)
    refs[4][...] = total


def square_sums(masters):
    return call(square_sums_body, plain(masters), [((1, 128), F32)], 0, name="square_sums")[0]


def adam_body(kind, w_ref, m_ref, v_ref, g_ref, first_ref, second_ref, update_ref, sums_ref):
    gradient = g_ref[...]
    correction = 1.0 - 0.5**STEP
    first = 0.5 * m_ref[...] + 0.5 * gradient
    second = 0.5 * v_ref[...] + 0.5 * gradient * gradient
    update = first / correction / (jnp.sqrt(second / correction) + adam_eps)
    update = update + (decay_weight if kind < 3 else 0.0) * w_ref[...]
    first_ref[...] = first
    second_ref[...] = second
    update_ref[...] = update
    sums_ref[...] = by_group(update, kind)


def adam(kind, w, m, v, g):
    return call(
        functools.partial(adam_body, kind),
        plain([w, m, v, g]),
        [(w.shape, F32)] * 3 + [((1, 128), F32)],
        0,
        name=f"adam_{kind}",
    )


def gain_body(kept_ref, got_ref, w_ref, m_ref, v_ref, weights_ref, s0, s1, s2, grad_ref, *outs):
    grad_ref[...] = kept_ref[...] + got_ref[...]
    first_ref, second_ref, update_ref, sums_ref = *outs[:3], outs[4]
    adam_body(3, w_ref, m_ref, v_ref, grad_ref, first_ref, second_ref, update_ref, sums_ref)
    outs[3][:, :128] = weights_ref[...]
    outs[3][:, 128:] = sums_ref[...] + s0[...] + s1[...] + s2[...]


def gain_adam(kept, got, w, m, v, weight_sums, sums):
    return call(
        gain_body,
        plain([kept, got, w, m, v, weight_sums, *sums]),
        [(w.shape, F32)] * 4 + [((1, 256), F32)],
        0,
        [pltpu.VMEM((1, 128), F32)],
        "adam_3",
    )


def lamb_body(*refs):
    weight_norms, update_norms = jnp.sqrt(refs[0][:, :128]), jnp.sqrt(refs[0][:, 128:])
    ratio = weight_norms / (update_norms + 1e-06)
    masters, updates, news, copies = (refs[1 + 4 * n : 5 + 4 * n] for n in range(4))
    for kind in range(4):
        w = masters[kind]
        scale = of_group(ratio, w.shape[1] if kind == 3 else w.shape[0], kind)
        new = w[...] - lamb_rate * scale * updates[kind][...]
        if kind == 3:
            new = new[0]
        news[kind][...] = new
        copies[kind][...] = new.astype(BF16)
    refs[17][...] = weight_norms[0, :24]
    refs[18][...] = update_norms[0, :24]


def lamb(squares, masters, updates):
    shapes = [w.shape for w in masters[:3]] + [masters[3].shape[1:]]
    return call(
        lamb_body,
        plain([squares, *masters, *updates]),
        [(s, F32) for s in shapes] + [(s, BF16) for s in shapes] + [((24,), F32)] * 2,
        0,
        name="lamb",
    )


def per_device(
    encoder_layer_input,
    decoder_layer_input,
    cotangent,
    encoder_used_lengths,
    decoder_used_lengths,
    attn_master,
    inner_master,
    outer_master,
    gain_master,
    attn_first,
    inner_first,
    outer_first,
    gain_first,
    attn_second,
    inner_second,
    outer_second,
    gain_second,
):
    ns, nb = lax.axis_size("seq"), lax.axis_size("batch")
    s, b = lax.axis_index("seq"), lax.axis_index("batch")
    ar, ir, orow = attn_master.shape[0], inner_master.shape[0], outer_master.shape[0]
    dc, fc = D // ns, FF // ns
    cuts = FF // (ns * orow)

    gr = gain_master.shape[0]
    packed = nb == 8 and ar % 16 == 0 and 3 * orow == ns * ir and cuts == 4
    clock = Clock()
    now, mark = clock.now, clock.mark
    masters = [attn_master, inner_master, outer_master, gain_master[None]]
    if packed:
        attn_mine, feed_mine = head_exchange(attn_master, inner_master, outer_master, gain_master)
        feeds_mine = [feed_mine]
    else:
        width = (ar // 128 + 1) * 128
        lines = -(-gr // (width - ar))
        corner = jnp.pad(gain_master.astype(BF16), (0, lines * (width - ar) - gr)).reshape(lines, width - ar)
        corner = jnp.broadcast_to(jnp.pad(corner, ((0, dc - lines), (0, 0))), (ns, dc, width - ar))
        attn_low = attn_master.astype(BF16).T.reshape(ns, dc, ar)
        got = seq_exchange(jnp.concatenate([attn_low, corner], axis=2), s)
        attn_mine = got[:, :, :ar].swapaxes(0, 1).reshape(dc, ns * ar)
        gains_mine = got[:, :lines, ar:].reshape(ns, -1)[:, :gr].reshape(1, ns * gr)
        attn_mine = jnp.concatenate([attn_mine, jnp.pad(gains_mine, ((0, 15), (0, ns * (ar - gr))))])
        inner_low = inner_master.astype(BF16).reshape(ir, cuts, ns, orow).transpose(2, 0, 1, 3)
        inner_mine = seq_exchange(inner_low.reshape(ns, ir, fc), s).reshape(ns * ir, fc)
        feeds_mine = [inner_mine, outer_master.astype(BF16)]
    attn_got = None
    attn_ring = ring_gather(attn_mine)
    next(attn_ring)
    while not isinstance(attn_got, list):
        attn_last, attn_got = attn_got, attn_ring.send(None)
    squares = square_sums(masters)
    attn_t = gathered_lanes([attn_got[0], *(tie(x, squares) for x in attn_got[1:])], "gather_attn")
    feed_rings = [ring_gather(x) for x in feeds_mine]
    for x in feed_rings:
        next(x)
        x.send(attn_last)

    def feed_step():
        for x in feed_rings:
            clock.step(x)

    gains = attn_t[dc].reshape(nb, ns * ar)[:, : ns * gr].reshape(6, D).astype(F32)
    gain = [gains[i : i + 1] for i in range(6)]
    out_mine = turn_pack([(attn_t, part((dc, D), 0, 4 * g + 3)) for g in range(3)], "out_pack")
    out_got = send_some(out_mine)

    enc_in, dec_in = encoder_layer_input[0], decoder_layer_input[0]
    er, dr = enc_in.shape[0], dec_in.shape[0]
    enc_meta = jnp.stack([s, encoder_used_lengths[0]]).astype(jnp.int32)
    dec_meta = jnp.stack([s, decoder_used_lengths[0]]).astype(jnp.int32)
    alive = (s * dr + jnp.arange(dr, dtype=jnp.int32)) < decoder_used_lengths[0]
    seed = jnp.where(alive[:, None], cotangent[0], jnp.zeros_like(cotangent[0]))
    blocks = gather_blocks(jnp.concatenate([enc_in, dec_in, seed]))
    enc_blocks = [(x, part((er, D), 0, 0)) for x in blocks]
    dec_blocks = [(x, part((dr, D), er // dr, 0)) for x in blocks]
    seed_blocks = [(x, part((dr, D), er // dr + 1, 0)) for x in blocks]

    def quarters(rows):
        return [(rows, part((rows.shape[0] // 4, D), j, 0)) for j in range(4)]

    mark(out_mine[1])
    feed_step()
    rows_a, q0, k0, v0, logs_far0, mixed_far0 = attend_far(
        now(enc_meta), enc_blocks, None, attn_t, None, 0, False, gain[0]
    )
    mark(mixed_far0)
    logs_near0, mixed_near0 = attend_near(enc_meta, now(q0), k0, v0, None, 0, False)
    mark([mixed_near0, out_got[2]])
    feed_step()
    out_w = lanes_unpack(send_rest([now(out_got[0]), *out_got[1:]], mixed_near0), "out_unpack")
    kf, sf = project(mixed_far0, (out_w, 0), BF16, "project_far_0")
    mark(sf)
    kn_enc, sn = project(now(mixed_near0), (out_w, 0), F32, "project_near_0")
    mark(sn)
    far = mark(add_low(now(kf), seq_swap(sf, 1)))
    x_enc, c_enc = seq_swap(far, 2), seq_swap(sn, 1)
    rows_c, q1, k1, v1, logs_far1, mixed_far1, kf, sf = attend_far(
        now(dec_meta), dec_blocks, None, attn_t, (out_w, 1), 1, True, gain[3]
    )
    mark(sf)
    feed_step()
    enc_mid, norm_b = close(now(kn_enc), c_enc, x_enc, enc_in, gain[1], "close_enc_attn")
    mark(norm_b)
    rows_b = gather_blocks(norm_b)
    x_self = seq_swap(mark(far_payload(kf, now(sf))), 2)
    logs_near1, mixed_near1, kn, sn = attend_near(dec_meta, now(q1), k1, v1, (out_w, 1), 1, True)
    mark(sn)
    c_self = seq_swap(sn, 1)
    feed_got = [clock.finish(x) for x in feed_rings]
    feed_got = [[now(got[0]), *got[1:]] for got in feed_got]
    if packed:
        inner_cols, outer_rows = gathered_feeds(feed_got[0], orow, "gather_feeds")
    else:
        inner_cols = gathered_rows(feed_got[0], "gather_inner")
        outer_rows = gathered_rows(feed_got[1], "gather_outer")
    inner_cols, outer_rows = inner_cols.reshape(4 * D, fc), outer_rows.reshape(2 * fc, D)
    eg1, eu1, eh1, kf, sf = feed_forward((now(rows_b[2]), rows_b[3]), inner_cols, outer_rows, 0, BF16, "enc_feed_far")
    far = mark(far_payload(kf, sf))
    x_enc = seq_swap(far, 2)
    eg0, eu0, eh0, kn_enc, sn = feed_forward((now(rows_b[0]), rows_b[1]), inner_cols, outer_rows, 0, F32, "enc_feed_near")
    mark(sn)
    c_enc = seq_swap(sn, 1)
    dec_mid, norm_d = close(now(kn), c_self, x_self, dec_in, gain[4], "close_self")
    mark(norm_d)
    rows_d = gather_blocks(norm_d)
    enc_out, norm_e = close(now(kn_enc), c_enc, x_enc, enc_mid, gain[2], "close_enc_feed")
    mark(norm_e)
    rows_e = gather_blocks(norm_e)
    mark([norm_e, rows_d[2]])
    q0t, q1t = now(q0).T, now(q1).T
    mark(q1t)
    q2, k2, v2, logs_far2, mixed_far2, kf, sf = attend_far(
        now(enc_meta), plain(rows_d), plain(rows_e), attn_t, (out_w, 2), 2, False
    )
    far = mark(far_payload(kf, sf))
    x_dec = seq_swap(far, 2)
    logs_near2, mixed_near2, kn, sn = attend_near(enc_meta, now(q2), k2, v2, (out_w, 2), 2, False)
    mark(sn)
    dec_late, norm_f = close(now(kn), seq_swap(tie(sn, x_dec), 1), x_dec, dec_mid, gain[5], "close_cross")
    mark(norm_f)
    rows_f = gather_blocks(norm_f)
    dg0, du0, dh0, kn_out, sn_out = feed_forward(
        (now(rows_f[0]), rows_f[1]), inner_cols, outer_rows, 1, F32, "dec_feed_near"
    )
    mark(dh0)
    a0, b0, kn_dec, sn_dec = feed_back(
        seed_blocks[:2], now(dg0), du0, inner_cols, outer_rows, 1, F32, "dec_feed_back_near"
    )
    mark(sn_dec)
    c_dec = seq_swap(sn_dec, 1)
    dg1, du1, dh1, kf_out, sf_out = feed_forward(
        (now(rows_f[2]), rows_f[3]), inner_cols, outer_rows, 1, BF16, "dec_feed_far"
    )
    mark(dh1)
    a1, b1, kf, sf = feed_back(seed_blocks[2:], now(dg1), du1, inner_cols, outer_rows, 1, BF16, "dec_feed_back_far")

    far = mark(far_payload(kf, sf))
    x_dec = seq_swap(far, 2)
    dec_feed = feed_weight(
        rows_f, seed_blocks, (now(a0), a1), (b0, b1), (dh0, dh1), packed, "dec_feed_weight"
    )
    mark(dec_feed[-1])
    up_five, low, gain_five = close_back(now(kn_dec), c_dec, x_dec, dec_late, gain[5], seed, "back_dec_feed")
    mark(low)
    dz_cross = plain(gather_blocks(low))
    half = nb // 2
    feed_shapes = [(ns * ir, fc), (orow, D)]

    def pair_send(kept, sent):
        return kept, batch_swap(mark(sent), 1)

    def feed_parts(grads):
        if packed:
            return [pair_send(*grads)]
        blocks = [now(x).reshape((half,) + shape) for x, shape in zip(grads, feed_shapes)]
        return [pair_send(*pair_blocks(x)) for x in blocks]

    dec_parts = feed_parts(dec_feed)
    far_out = mark(far_payload(kf_out, sf_out))

    q2t = mark(now(q2).T)
    out_sent = out_weight([(dz_cross, now(mixed_near2), mixed_far2)], "cross_out_weight")
    mark(out_sent[1])
    out_got = send_blocks(out_sent)
    x_out = seq_swap(tie(far_out, out_sent[1]), 2)
    c_out = seq_swap(tie(sn_out, out_sent[1]), 1)
    decoder_layer_output = (dec_late + kn_out + c_out.astype(F32) + x_out.astype(F32)).astype(BF16)
    cross_d, outs = attend_back(
        now(enc_meta), dz_cross, q2t, attn_t, (out_w, 2), 2, (q2, k2, v2, logs_near2, logs_far2), dr, er, False, True
    )
    far = mark(far_payload(outs[6], tie(outs[7], x_out, c_out, out_got[2])))
    x_enc, c_enc = seq_swap(far, 2), seq_swap(now(outs[5]), 1)
    c_far, c_dec = seq_swap(now(outs[3]), 1), seq_swap(now(outs[1]), 1)
    kf_dec, kn_dec = outs[2], outs[0]
    cross_w = attend_weights(plain(rows_d), plain(rows_e), (now(cross_d[0]), *cross_d[1:]), "cross_weights")
    mark(cross_w[0])
    three = attn_parts([now(out_got[0]), *out_got[1:]], [(cross_w[1:], 2)], ns * ar, "part_three")
    mark(three[1])
    up_two, low, gain_two = close_back(now(outs[4]), c_enc, x_enc, enc_out, gain[2], None, "back_encoded")
    mark(low)
    dz = gather_blocks(low)
    far_dec = mark(add_low(kf_dec, now(c_far)))
    part_three = (three[0], batch_swap(three[1], 1))
    mark([far_dec] + [got for _, got in dec_parts])
    a0, b0, kn_enc, sn = feed_back(plain(dz[:2]), now(eg0), eu0, inner_cols, outer_rows, 0, F32, "enc_feed_back_near")
    mark(sn)
    c_enc = seq_swap(sn, 1)
    x_dec = seq_swap(tie(far_dec, dz[2], sn), 2)
    mark([sn, part_three[1]])
    dz = plain(dz)
    a1, b1, kf, sf = feed_back(dz[2:], now(eg1), eu1, inner_cols, outer_rows, 0, BF16, "enc_feed_back_far")
    far = mark(far_payload(kf, tie(sf, x_dec)))
    x_enc = seq_swap(far, 2)
    enc_feed = feed_weight(
        rows_b, dz, (now(a0), a1), (b0, b1), (eh0, eh1), packed, "enc_feed_weight"
    )
    mark(enc_feed[-1])
    enc_parts = feed_parts(enc_feed)
    up_four, low_self, gain_four = close_back(now(kn_dec), c_dec, x_dec, dec_mid, gain[4], up_five, "back_cross")
    mark(low_self)
    dz_self = plain(gather_blocks(low_self))
    up_one, low, gain_one = close_back(now(kn_enc), c_enc, x_enc, enc_mid, gain[1], up_two, "back_enc_feed")
    mark(low)
    dz_enc = gather_blocks(low)
    self_d, outs = attend_back(
        now(dec_meta), dz_self, q1t, attn_t, (out_w, 1), 1, (q1, k1, v1, logs_near1, logs_far1), dr, dr, True, False
    )
    mark(outs[3])
    self_w = attend_weights(quarters(rows_c), None, (now(self_d[0]), *self_d[1:]), "self_weights")
    mark(self_w[0])
    flight = []
    feeds = [ring_reduce([e, d], "feed_hop", None, flight) for e, d in zip(enc_parts, dec_parts)]
    for x in feeds:
        next(x)
    kn_self, c_self = outs[0], seq_swap(tie(outs[1], dz_enc[2]), 1)
    sf_self = seq_swap(tie(outs[3], dz_enc[2]), 1)
    dz_enc = plain(dz_enc)
    out_late = out_weight(
        [(dz_enc, now(mixed_near0), mixed_far0), (dz_self, mixed_near1, mixed_far1)], "late_out_weight"
    )
    mark(out_late[1])
    got_late = send_blocks(out_late)
    x_self = seq_swap(mark(add_low(outs[2], now(sf_self))), 2)
    for x in feeds:
        clock.step(x)
    enc_d, outs = attend_back(
        now(enc_meta), dz_enc, q0t, attn_t, (out_w, 0), 0, (q0, k0, v0, logs_near0, logs_far0), er, er, False, False
    )
    mark([outs[3], x_self, got_late[2], *flight])
    c_far, c_enc = seq_swap(outs[3], 1), seq_swap(now(outs[1]), 1)
    part_zero = pair_send(
        *self_part(quarters(rows_a), (now(enc_d[0]), *enc_d[1:]), ns * ar, "part_zero")
    )
    for x in feeds:
        clock.step(x)
    part_middle = pair_send(
        *attn_parts(
            [now(got_late[0]), *got_late[1:]],
            [(self_w[:2], 0), ((self_w[2], cross_w[0]), 1)],
            ns * ar,
            "part_middle",
        )
    )
    far = mark(add_low(now(outs[2]), c_far))
    x_enc = seq_swap(far, 2)
    decoder_input_gradient, _, gain_three = close_back(
        now(kn_self), c_self, x_self, dec_in, gain[3], up_four, "back_self"
    )
    mark(gain_three)
    for x in feeds:
        clock.step(x)
    encoder_input_gradient, _, gain_zero = close_back(
        now(outs[0]), c_enc, x_enc, enc_in, gain[0], up_one, "back_enc_attn"
    )
    mark(gain_zero)

    gain_lines = spread(
        [now(gain_zero), gain_one, gain_two, gain_three, gain_four, gain_five], nb, ns * ar
    )
    mark(gain_lines)
    last_ring = ring_reduce([part_zero, part_middle, part_three], "attn_hop", gain_lines)
    next(last_ring)
    clock.step(last_ring)
    feeds_done = [clock.finish(x)[0] for x in feeds]
    if packed:
        feed_sent, outer_grad = feed_pack(mark(feeds_done[0]), ir, fc, orow)
        mark(feed_sent[1])
        feed_got = send_some(feed_sent)
    else:
        inner_part, outer_grad = feeds_done
        inner_part = mark(now(inner_part).astype(BF16).reshape(ns, ir, fc))
        inner_part = seq_exchange(inner_part, s)
    clock.step(last_ring)
    outer_new = adam(2, outer_master, outer_first, outer_second, now(outer_grad))
    mark(outer_new[3])
    clock.step(last_ring)
    if not packed:
        inner_grad = inner_part.reshape(ns, ir, cuts, orow).transpose(1, 2, 0, 3).reshape(ir, FF).astype(F32)
    (attn_sum,) = clock.finish(last_ring)
    mine = tail_pack(mark(attn_sum), ar, gr)
    mark(mine[-1])
    if packed:
        inner_grad = feed_unpack(send_rest([now(feed_got[0]), *feed_got[1:]]))
    inner_new = adam(1, inner_master, inner_first, inner_second, now(inner_grad))
    mark(inner_new[3])
    attn_grad, gain_kept, gain_sent = tail_unpack(mine, s, ar, gr, now, clock.last)
    gain_got = batch_swap(gain_sent, 1)
    attn_new = adam(0, attn_master, attn_first, attn_second, attn_grad)
    others = (attn_new, inner_new, outer_new)
    gain_grad, *gain_new, own_squares = gain_adam(
        gain_kept, tie(gain_got, attn_new[3]), masters[3], gain_first[None], gain_second[None], squares, [x[3] for x in others]
    )
    results = (*others, gain_new)
    all_squares = sum_all(own_squares)
    last = lamb(all_squares, masters, [x[2] for x in results])
    grads = (attn_grad, inner_grad, outer_grad, gain_grad)

    def flat(four):
        return (*four[:3], four[3][0])

    return (
        decoder_layer_output[None],
        encoder_input_gradient[None],
        decoder_input_gradient[None],
        *flat(grads),
        *flat([x[0] for x in results]),
        *flat([x[1] for x in results]),
        *last,
    )


def solution(mesh):
    rows = P("batch", "seq", None)
    matrix = P(("batch", "seq"), None)
    vector = P(("batch", "seq"))
    kinds = (matrix, matrix, matrix, vector)
    return jax.shard_map(
        per_device,
        mesh=mesh,
        in_specs=(rows, rows, rows, P("batch"), P("batch")) + kinds * 3,
        out_specs=(rows, rows, rows) + kinds * 5 + (P(), P()),
        check_vma=False,
    )
```

```python
import functools
import math

import jax
import jax.numpy as jnp
from jax import lax
from jax.experimental import pallas as pl
from jax.experimental.pallas import tpu as pltpu
from jax.sharding import PartitionSpec as P

D = 768
HEADS = 12
HEAD = 64
FF = 2048
STEP = 5

eps_norm = 1e-06
adam_eps = 1e-06
lamb_rate = 0.5
decay_weight = 0.01
masked_score = -1000000000.0

F32 = jnp.float32
BF16 = jnp.bfloat16

FLOPS, BYTES = 10**13, 10**10


def seq_swap(x, k):
    n = lax.axis_size("seq")
    return lax.ppermute(x, "seq", [(i, i ^ k) for i in range(n)])


def batch_swap(x, k):
    n = lax.axis_size("batch")
    return lax.ppermute(x, "batch", [(i, i ^ k) for i in range(n)])


def gather_blocks(x):
    other, near = seq_swap(x, 2), seq_swap(x, 1)
    return [x, near, other, seq_swap(tie(other, near), 1)]


def xor_blocks(x, s):
    n = x.shape[0]
    for k in (1, 2):
        swapped = jnp.stack([x[j ^ k] for j in range(n)])
        x = jnp.where((s & k) != 0, swapped, x)
    return x


def seq_exchange(blocks, s):
    n = blocks.shape[0]
    mine = xor_blocks(blocks, s)
    got = jnp.stack([mine[0]] + [seq_swap(mine[j], j) for j in range(1, n)])
    return xor_blocks(got, s)


def tie(x, *others):
    return lax.optimization_barrier((x, others))[0]


def ring_shift(x, active=None):
    nb = lax.axis_size("batch")
    return lax.ppermute(x, "batch", [(i, (i + 2) % nb) for i in (range(nb) if active is None else active)])


def ring_gather(block):
    rounds = lax.axis_size("batch") // 2
    after = yield None
    moving, got, paired = block if after is None else tie(block, after), [], None
    for k in range(rounds):
        following = None
        if k + 1 < rounds:
            payload = moving if paired is None else tie(moving, paired)
            following = ring_shift(payload)
        got.append(moving)
        paired = batch_swap(moving if following is not None or paired is None else tie(moving, paired), 1)
        got.append(paired)
        after = yield moving if following is None else payload
        if following is not None:
            moving = following if after is None else tie(following, after)
            paired = got[-1]
    yield got


def assemble_body(by_lanes, moves, count, low, *refs):
    here = len(refs) - 1 - low[1]
    ins, outs, sem = refs[:here], refs[here:-1], refs[-1]
    b = lax.axis_index("batch")
    z, y = b // 2, b % 2
    ring, copies = count // 2, []
    for i, ref in enumerate(ins):
        k, e = (low[0] + i) // 2, (low[0] + i) % 2
        at = lax.rem(z + ring - k, ring) * 2 + (y + e - 2 * y * e)
        for which, (r0, r1), (c0, c1), (to_row, to_lane) in moves:
            out = outs[which]
            rows = pl.ds(to_row, r1 - r0)
            if by_lanes:
                start = pl.multiple_of(at * (out.shape[1] // count) + to_lane, 128)
                target = out.at[rows, pl.ds(start, c1 - c0)]
            else:
                target = out.at[at, rows, pl.ds(to_lane, c1 - c0)]
            copies.append(pltpu.make_async_copy(ref.at[r0:r1, c0:c1], target, sem.at[len(copies)]))
    for copy in copies:
        copy.start()
    for copy in copies:
        copy.wait()


def assemble(blocks, moves, shapes, by_lanes, name, last=0):
    count = len(blocks)
    outs = [jax.ShapeDtypeStruct((h, count * w) if by_lanes else (count, h, w), BF16) for h, w in shapes]
    any_space = pl.BlockSpec(memory_space=pl.ANY)
    made = []
    for low, high in ((0, count - last), (count - last, count)):
        if low == high:
            continue
        part_of = blocks[low:high]

        def body(*refs, low=low, made=tuple(made), part_of=part_of):
            given = refs[: len(part_of)]
            assemble_body(by_lanes, moves, count, (low, len(outs)), *given, *refs[len(part_of) + len(made) :])

        made = pl.pallas_call(
            body,
            in_specs=[pl.BlockSpec(memory_space=pltpu.VMEM)] * len(part_of) + [any_space] * len(made),
            out_specs=[any_space] * len(outs),
            out_shape=outs,
            input_output_aliases={len(part_of) + i: i for i in range(len(made))},
            scratch_shapes=[pltpu.SemaphoreType.DMA((len(part_of) * len(moves),))],
            cost_estimate=pl.CostEstimate(flops=FLOPS, bytes_accessed=BYTES, transcendentals=0),
            name=f"{name}_{low}",
        )(*part_of, *made)
    return made


def gathered_rows(got, name):
    h, w = got[0].shape
    return assemble(got, [(0, (0, h), (0, w), (0, 0))], [(h, w)], False, name)[0]


def gathered_lanes(got, name):
    h, w = got[0].shape
    if w % 128 == 0:
        return assemble(got, [(0, (0, h), (0, w), (0, 0))], [(h, w)], True, name)[0]
    return gathered_rows(got, name).swapaxes(0, 1).reshape(h, -1)


def gathered_feeds(got, rows, name):
    h, w = got[0].shape
    fc = w - 256
    moves = [(0, (0, h), (0, fc), (0, 0))]
    for g in range(D // 128):
        r, c = g % 3 * rows, fc + g // 3 * 128
        moves.append((1, (r, r + rows), (c, c + 128), (0, 128 * g)))
    return assemble(got, moves, [(h, fc), (rows, D)], False, name, 2)


def pair_blocks(blocks):
    y = lax.axis_index("batch") % 2
    pairs = blocks.reshape((blocks.shape[0] // 2, 2) + blocks.shape[1:])
    return [lax.dynamic_index_in_dim(pairs, i, 1, keepdims=False) for i in (y, 1 - y)]


def hop_body(step, counts, moving, riding, *refs):
    count = len(counts)
    kept, got = refs[:count], refs[count : 2 * count]
    refs = list(refs[2 * count :])
    moved = refs.pop(0) if moving else None
    extra = refs.pop(0) if riding else None
    out, one, two, sem = refs
    ring = lax.axis_size("batch") // 2
    dest = lax.rem(lax.axis_index("batch") // 2 + 2 * ring - step, ring)
    for n in range(count):
        low = sum(counts[:n])

        @pl.when((dest >= low) & (dest < low + counts[n]))
        def _(n=n, low=low):
            mine = pltpu.make_async_copy(kept[n].at[dest - low], one, sem.at[0])
            other = pltpu.make_async_copy(got[n].at[dest - low], two, sem.at[1])
            mine.start()
            other.start()
            mine.wait()
            other.wait()

    total = one[...].astype(F32) + two[...].astype(F32)
    rows = one.shape[0]
    if moving:
        total = total + moved[:rows, :].astype(F32)
    out[:rows, :] = total.astype(out.dtype)
    if riding:
        lines = jnp.concatenate([extra[dest * 2], extra[dest * 2 + 1]], axis=0)
        if moving:
            lines = lines + moved[rows : rows + 2, :].astype(F32)
        out[rows:, :] = jnp.concatenate([lines, jnp.zeros((14, lines.shape[1]), F32)], axis=0).astype(out.dtype)


def hop(parts, step, moved, extra, dtype, name):
    shape = parts[0][0].shape[1:]
    arrays = [k for k, _ in parts] + [g for _, g in parts]
    specs = [pl.BlockSpec(memory_space=pl.ANY)] * len(arrays)
    for x in (moved, extra):
        if x is not None:
            arrays.append(x)
            specs.append(pl.BlockSpec(memory_space=pltpu.VMEM))
    out = shape if extra is None else (shape[0] + 16, shape[1])
    return pl.pallas_call(
        functools.partial(hop_body, step, [k.shape[0] for k, _ in parts], moved is not None, extra is not None),
        in_specs=specs,
        out_specs=pl.BlockSpec(memory_space=pltpu.VMEM),
        out_shape=jax.ShapeDtypeStruct(out, dtype),
        scratch_shapes=[pltpu.VMEM(shape, BF16), pltpu.VMEM(shape, BF16), pltpu.SemaphoreType.DMA((2,))],
        cost_estimate=pl.CostEstimate(flops=FLOPS, bytes_accessed=BYTES, transcendentals=0),
        name=f"{name}_{step}",
    )(*arrays)


def ring_reduce(parts, name, extra=None, flight=None):
    ring = lax.axis_size("batch") // 2
    after = yield None
    moved = None
    for k in range(1, ring + 1):
        if moved is None:
            held = [(kept if after is None else tie(kept, after), got) for kept, got in parts]
        else:
            held, moved = parts, tie(moved, after)
        if k == ring:
            yield [hop(held, k, moved, extra, F32, name)]
            return
        sent = hop(held, k, moved, extra, BF16, name)
        moved = ring_shift(sent)
        if flight is not None:
            flight.append(moved)
        after = yield sent


def sum_seq(x):
    for k in (1, 2):
        x = x + seq_swap(x, k)
    return x


def sum_all(x):
    x = sum_seq(x)
    k = 1
    while k < lax.axis_size("batch"):
        x = x + batch_swap(x, k)
        k *= 2
    return x


class Clock:
    def __init__(self):
        self.last = None

    def now(self, x):
        return x if self.last is None else tie(x, self.last)

    def mark(self, x):
        self.last = x
        return x

    def step(self, work):
        got = work.send(self.last)
        return got if isinstance(got, list) else self.mark(got)

    def finish(self, work):
        got = None
        while not isinstance(got, list):
            got = self.step(work)
        return got


def nt(a, b):
    return lax.dot_general(a, b, (((1,), (1,)), ((), ())), preferred_element_type=F32)


def nn(a, b):
    return lax.dot_general(a, b, (((1,), (0,)), ((), ())), preferred_element_type=F32)


def tn(a, b):
    return lax.dot_general(a, b, (((0,), (0,)), ((), ())), preferred_element_type=F32)


def whole(x):
    shape = x.shape
    return pl.BlockSpec(shape, lambda i: (0,) * len(shape))


def part(shape, *index):
    return pl.BlockSpec(shape, lambda i: index)


def plain(arrays):
    return [(x, whole(x)) for x in arrays]


SCALARS = pl.BlockSpec(memory_space=pltpu.SMEM)


def call(body, ins, outs, flops, scratch=(), name=None):
    arrays = [a for a, _ in ins]
    specs = [whole(a) if s is None else s for a, s in ins]
    shapes = [jax.ShapeDtypeStruct(s, d) for s, d in outs]
    return pl.pallas_call(
        body,
        grid=(1,),
        in_specs=specs,
        out_specs=[whole(o) for o in shapes],
        out_shape=shapes,
        scratch_shapes=list(scratch),
        cost_estimate=pl.CostEstimate(flops=FLOPS, bytes_accessed=BYTES, transcendentals=0),
        name=name,
    )(*arrays)


def positions(shape, axis, owner, rows):
    at = lax.broadcasted_iota(jnp.int32, shape, axis)
    shift = rows.bit_length() - 1
    return ((owner ^ (at >> shift)) << shift) + (at & (rows - 1))


def score_bias(meta, first_row, tile, q_rows, k_rows, causal):
    keys = positions((1, 4 * k_rows), 1, meta[0], k_rows)
    if not causal:
        return jnp.where(keys < meta[1], 0.0, masked_score)
    at = first_row + lax.broadcasted_iota(jnp.int32, (tile, 1), 0)
    shift = q_rows.bit_length() - 1
    queries = ((meta[0] ^ (at >> shift)) << shift) + (at & (q_rows - 1))
    return jnp.where((keys <= queries) & (keys < meta[1]), 0.0, masked_score)


def head_mask(shape, h):
    lane = lax.broadcasted_iota(jnp.int32, shape, 1)
    return (lane >= h * HEAD) & (lane < (h + 1) * HEAD)


def attend_tile(q, k, v, bias, heads):
    mixed = jnp.zeros(q.shape, F32)
    logs = jnp.zeros((q.shape[0], 128), F32)
    q = (q.astype(F32) * 0.125).astype(BF16)
    lane = lax.broadcasted_iota(jnp.int32, logs.shape, 1)
    for h in range(heads):
        mask = head_mask(q.shape, h)
        scores = nt(jnp.where(mask, q, jnp.zeros_like(q)), k) + bias
        peak = jnp.max(scores, axis=-1, keepdims=True)
        expo = jnp.exp(scores - peak)
        total = jnp.sum(expo, axis=-1, keepdims=True)
        probs = (expo * (1.0 / total)).astype(BF16)
        mixed = jnp.where(mask, nn(probs, v), mixed)
        logs = jnp.where(lane == h, peak + jnp.log(total), logs)
    return mixed, logs


def attend_rows(meta, q_ref, k_ref, v_ref, wo_ref, first, q_rows, k_rows, causal, outs):
    logs_ref, mixed_ref = outs[:2]
    heads, rows = q_ref.shape[1] // HEAD, 2 * q_rows
    bias = score_bias(meta, first, rows, q_rows, k_rows, causal)
    mixed, logs = attend_tile(q_ref[first : first + rows, :], k_ref[...], v_ref[...], bias, heads)
    logs_ref[...] = logs
    mixed_ref[...] = mixed.astype(BF16)
    if wo_ref is not None:
        for n in range(2):
            out = outs[2 + n]
            out[...] = nn(mixed_ref[n * q_rows : (n + 1) * q_rows, :], wo_ref[...]).astype(out.dtype)


def project_body(rows, mixed_ref, wo_ref, keep_ref, send_ref):
    for n, out in enumerate((keep_ref, send_ref)):
        out[...] = nn(mixed_ref[n * rows : (n + 1) * rows, :], wo_ref[...]).astype(out.dtype)


def project(mixed, out_w, keep, name):
    rows, dc = mixed.shape[0] // 2, mixed.shape[1]
    return call(
        functools.partial(project_body, rows),
        [(mixed, None), out_weights(out_w)],
        [((rows, D), keep), ((rows, D), BF16)],
        4 * rows * dc * D,
        name=name,
    )


def attend_far_body(cross, raw, fused, causal, q_rows, k_rows, *refs):
    refs = list(refs)
    meta = refs.pop(0)
    queries, refs = refs[:4], refs[4:]
    sources = queries
    if cross:
        sources, refs = refs[:4], refs[4:]
    if raw:
        gain = refs.pop(0)
    wq, wk, wv = refs[:3]
    refs = refs[3:]
    wo = refs.pop(0) if fused else None
    if raw:
        rows_ref = refs.pop(0)
        for j in range(4):
            h = queries[j][...].astype(F32)
            inverse = lax.rsqrt(jnp.mean(h * h, axis=-1, keepdims=True) + eps_norm)
            rows_ref[j * q_rows : (j + 1) * q_rows, :] = (h * inverse * gain[...]).astype(BF16)
        queries = sources = [rows_ref.at[j * q_rows : (j + 1) * q_rows, :] for j in range(4)]
    q_ref, k_ref, v_ref = refs[:3]
    outs = refs[3:]
    for j in range(4):
        q_ref[j * q_rows : (j + 1) * q_rows, :] = nt(queries[j][...], wq[...]).astype(BF16)
        rows = sources[j][...]
        k_ref[j * k_rows : (j + 1) * k_rows, :] = nt(rows, wk[...]).astype(BF16)
        v_ref[j * k_rows : (j + 1) * k_rows, :] = nt(rows, wv[...]).astype(BF16)
    attend_rows(meta, q_ref, k_ref, v_ref, wo, 2 * q_rows, q_rows, k_rows, causal, outs)


def attend_near_body(fused, causal, q_rows, k_rows, meta, q_ref, k_ref, v_ref, *rest):
    wo, outs = (rest[0], rest[1:]) if fused else (None, rest)
    attend_rows(meta, q_ref, k_ref, v_ref, wo, 0, q_rows, k_rows, causal, outs)


def attn_weights(attn_t, group):
    return [(attn_t, part((D // 4, D), 0, 4 * group + i)) for i in range(3)]


def out_weights(out_w):
    stack, place = out_w
    return (stack, pl.BlockSpec((None, stack.shape[1], D), lambda i: (place, 0, 0)))


def half_outs(q_rows, dc, keep):
    return [((2 * q_rows, 128), F32), ((2 * q_rows, dc), BF16), ((q_rows, D), keep), ((q_rows, D), BF16)]


def attend_far(meta, queries, sources, attn_t, out_w, group, causal, gain=None):
    cross, raw, fused = sources is not None, gain is not None, out_w is not None
    q_rows, dc = queries[0][1].block_shape[0], D // 4
    k_rows = sources[0][1].block_shape[0] if cross else q_rows
    flops = 2 * D * dc * (4 * q_rows + 8 * k_rows) + 16 * q_rows * k_rows * D
    return call(
        functools.partial(attend_far_body, cross, raw, fused, causal, q_rows, k_rows),
        [(meta, SCALARS)]
        + list(queries)
        + (list(sources) if cross else [])
        + ([(gain, None)] if raw else [])
        + attn_weights(attn_t, group)
        + ([out_weights(out_w)] if fused else []),
        ([((4 * q_rows, D), BF16)] if raw else [])
        + [((4 * q_rows, dc), BF16), ((4 * k_rows, dc), BF16), ((4 * k_rows, dc), BF16)]
        + half_outs(q_rows, dc, BF16)[: 4 if fused else 2],
        flops,
        name=f"attend_far_{group}",
    )


def attend_near(meta, q, k, v, out_w, group, causal):
    q_rows, k_rows, dc, fused = q.shape[0] // 4, k.shape[0] // 4, q.shape[1], out_w is not None
    return call(
        functools.partial(attend_near_body, fused, causal, q_rows, k_rows),
        [(meta, SCALARS), (q, part((2 * q_rows, dc), 0, 0)), (k, None), (v, None)]
        + ([out_weights(out_w)] if fused else []),
        half_outs(q_rows, dc, F32)[: 4 if fused else 2],
        16 * q_rows * k_rows * D,
        name=f"attend_near_{group}",
    )


STEPS = 1


def row_call(body, ins, outs, name):
    rows = ins[0].shape[0]

    def spec(shape):
        if shape[0] == 1:
            return pl.BlockSpec(shape, lambda i: (0, 0))
        return pl.BlockSpec((rows // STEPS,) + tuple(shape[1:]), lambda i: (i, 0))

    return pl.pallas_call(
        body,
        grid=(STEPS,),
        in_specs=[spec(x.shape) for x in ins],
        out_specs=[spec(s) for s, _ in outs],
        out_shape=[jax.ShapeDtypeStruct(s, d) for s, d in outs],
        cost_estimate=pl.CostEstimate(flops=FLOPS, bytes_accessed=BYTES, transcendentals=0),
        name=name,
    )(*ins)


def add_low(a, b):
    return (a.astype(F32) + b.astype(F32)).astype(BF16)


def far_payload(keep_far, send_far):
    return add_low(keep_far, seq_swap(send_far, 1))


def close_body(near_ref, core_ref, far_ref, residual_ref, gain_ref, out_ref, normed_ref):
    h = residual_ref[...].astype(F32) + near_ref[...] + core_ref[...].astype(F32) + far_ref[...].astype(F32)
    inverse = lax.rsqrt(jnp.mean(h * h, axis=-1, keepdims=True) + eps_norm)
    out_ref[...] = h
    normed_ref[...] = (h * inverse * gain_ref[...]).astype(BF16)


def close(near, core, far, residual, gain, name):
    return row_call(
        close_body, [near, core, far, residual, gain], [(near.shape, F32), (near.shape, BF16)], name
    )


def close_back_body(near_ref, core_ref, far_ref, stream_ref, gain_ref, *rest):
    if len(rest) == 4:
        upstream_ref, rest = rest[0], rest[1:]
    else:
        upstream_ref = None
    out_ref, low_ref, dgain_ref = rest
    h = stream_ref[...].astype(F32)
    up = near_ref[...] + core_ref[...].astype(F32) + far_ref[...].astype(F32)
    inverse = lax.rsqrt(jnp.mean(h * h, axis=-1, keepdims=True) + eps_norm)
    unit = h * inverse
    scaled = up * gain_ref[...]
    grad = inverse * (scaled - unit * jnp.mean(scaled * unit, axis=-1, keepdims=True))
    if upstream_ref is not None:
        grad = upstream_ref[...].astype(F32) + grad
    out_ref[...] = grad
    low_ref[...] = grad.astype(BF16)

    @pl.when(pl.program_id(0) == 0)
    def _():
        dgain_ref[...] = jnp.zeros_like(dgain_ref)

    dgain_ref[...] += jnp.sum(up * unit, axis=0, keepdims=True)


def close_back(near, core, far, stream, gain, upstream, name):
    shape = near.shape
    ins = [near, core, far, stream, gain] + ([] if upstream is None else [upstream])
    return row_call(close_back_body, ins, [(shape, F32), (shape, BF16), ((1, shape[1]), F32)], name)


def attend_back_body(cross, causal, q_rows, k_rows, tile, *refs):
    meta = refs[0]
    dz = refs[1:5]
    q_ref, qt_ref, k_ref, v_ref, logs_near, logs_far, wq, wk, wv, wo = refs[5:15]
    dq_ref, dkt_ref, dvt_ref = refs[15:18]
    outs = refs[18 : 18 + (8 if cross else 4)]
    do_ref, dot_ref, dkt_sum, dvt_sum, logs_ref = refs[18 + len(outs) :]
    heads = q_ref.shape[1] // HEAD
    for j in range(4):
        at = slice(j * q_rows, (j + 1) * q_rows)
        rows = dz[j][...]
        do_ref[at, :] = nt(rows, wo[...]).astype(BF16)
        dot_ref[:, at] = nt(wo[...], rows).astype(BF16)
    logs_ref[: 2 * q_rows, :] = logs_near[...]
    logs_ref[2 * q_rows :, :] = logs_far[...]
    dkt_sum[...] = jnp.zeros_like(dkt_sum)
    dvt_sum[...] = jnp.zeros_like(dvt_sum)

    def step(t, carry):
        at = pl.ds(pl.multiple_of(t * tile, tile), tile)
        q, do = q_ref[at, :], do_ref[at, :]
        q = (q.astype(F32) * 0.125).astype(BF16)
        qt, dot = qt_ref[:, at], dot_ref[:, at]
        logs = logs_ref[at, :]
        bias = score_bias(meta, t * tile, tile, q_rows, k_rows, causal)
        dq = jnp.zeros(q.shape, F32)
        for h in range(heads):
            mask = head_mask(q.shape, h)
            zero = jnp.zeros_like(q)
            probs = jnp.exp(nt(jnp.where(mask, q, zero), k_ref[...]) + bias - logs[:, h : h + 1])
            grad_probs = nt(jnp.where(mask, do, zero), v_ref[...])
            weighted = probs * grad_probs
            center = jnp.sum(weighted, axis=-1, keepdims=True)
            grad_scores = (weighted - probs * center).astype(BF16)
            feats = slice(h * HEAD, (h + 1) * HEAD)
            dvt_sum[feats, :] += nn(dot[feats, :], probs.astype(BF16))
            dkt_sum[feats, :] += nn(qt[feats, :], grad_scores)
            dq = jnp.where(mask, nn(grad_scores, k_ref[...]), dq)
        dq_ref[at, :] = (dq * 0.125).astype(BF16)
        return carry

    lax.fori_loop(0, 4 * q_rows // tile, step, 0)
    dkt_ref[...] = (dkt_sum[...] * 0.125).astype(BF16)
    dvt_ref[...] = dvt_sum[...].astype(BF16)

    def query_part(j):
        return nn(dq_ref[j * q_rows : (j + 1) * q_rows, :], wq[...])

    def source_part(j):
        at = slice(j * k_rows, (j + 1) * k_rows)
        return tn(dkt_ref[:, at], wk[...]) + tn(dvt_ref[:, at], wv[...])

    parts = (query_part, source_part) if cross else ((lambda j: query_part(j) + source_part(j)),)
    for n, make in enumerate(parts):
        for j in range(4):
            outs[4 * n + j][...] = make(j).astype(outs[4 * n + j].dtype)


def attend_back(meta, dz, qt, attn_t, out_w, group, saved, q_rows, k_rows, causal, cross):
    q, k, v, logs_near, logs_far = saved
    dc = q.shape[1]
    tile = min(1024, 4 * q_rows)

    def four(rows):
        return [((rows, D), F32), ((rows, D), BF16), ((rows, D), BF16), ((rows, D), BF16)]

    outs = call(
        functools.partial(attend_back_body, cross, causal, q_rows, k_rows, tile),
        [(meta, SCALARS)]
        + list(dz)
        + [(q, None), (qt, None), (k, None), (v, None), (logs_near, None), (logs_far, None)]
        + attn_weights(attn_t, group)
        + [out_weights(out_w)],
        [((4 * q_rows, dc), BF16), ((dc, 4 * k_rows), BF16), ((dc, 4 * k_rows), BF16)]
        + (four(q_rows) + four(k_rows) if cross else four(q_rows)),
        80 * q_rows * k_rows * D + 4 * D * dc * (4 * q_rows + 4 * k_rows),
        [
            pltpu.VMEM((4 * q_rows, dc), BF16),
            pltpu.VMEM((dc, 4 * q_rows), BF16),
            pltpu.VMEM((dc, 4 * k_rows), F32),
            pltpu.VMEM((dc, 4 * k_rows), F32),
            pltpu.VMEM((4 * q_rows, 128), F32),
        ],
        f"attend_back_{group}",
    )
    return outs[:3], outs[3:]


def attend_weights_body(cross, q_rows, k_rows, *refs):
    queries = refs[0:4]
    sources = refs[4:8] if cross else queries
    dq, dkt, dvt, *outs = refs[8:] if cross else refs[4:]
    gq = gk = gv = None
    for j in range(4):
        at, ak = slice(j * q_rows, (j + 1) * q_rows), slice(j * k_rows, (j + 1) * k_rows)
        x, y = queries[j][...], sources[j][...]
        a, b, c = tn(dq[at, :], x), nn(dkt[:, ak], y), nn(dvt[:, ak], y)
        gq, gk, gv = (a, b, c) if j == 0 else (gq + a, gk + b, gv + c)
    for ref, g in zip(outs, (gq, gk, gv)):
        ref[...] = g.astype(BF16)


def attend_weights(queries, sources, grads, name):
    cross = sources is not None
    dq, dkt, dvt = grads
    q_rows, k_rows, dc = dq.shape[0] // 4, dkt.shape[1] // 4, dq.shape[1]
    return call(
        functools.partial(attend_weights_body, cross, q_rows, k_rows),
        list(queries) + (list(sources) if cross else []) + [(dq, None), (dkt, None), (dvt, None)],
        [((dc, D), BF16)] * 3,
        0,
        name=name,
    )


def out_total(dz, near, far, q_rows):
    total = None
    for j, ref in enumerate(dz):
        mixed = (near, far)[j // 2][(j % 2) * q_rows : (j % 2 + 1) * q_rows, :]
        x = tn(ref[...], mixed)
        total = x if j == 0 else total + x
    return total


def out_weight_body(sizes, *refs):
    outs, scratch = refs[6 * len(sizes) : -1], refs[-1]
    s, rows = lax.axis_index("seq"), scratch.shape[2]
    for n, q_rows in enumerate(sizes):
        total = out_total(refs[6 * n : 6 * n + 4], refs[6 * n + 4], refs[6 * n + 5], q_rows)
        for t in range(4):
            scratch[s ^ t, n] = total[t * rows : (t + 1) * rows, :].astype(BF16)
    hand_out(scratch, outs)


def out_weight(groups, name):
    dc = D // 4
    ins, sizes = [], []
    for dz, near, far in groups:
        ins += list(dz) + [(near, None), (far, None)]
        sizes.append(near.shape[0] // 2)
    return call(
        functools.partial(out_weight_body, sizes),
        ins,
        sent_shapes((len(groups), dc, dc), BF16),
        0,
        [pltpu.VMEM((4, len(groups), dc, dc), BF16)],
        name,
    )


GELU_A, GELU_B = math.sqrt(2.0 / math.pi), 0.044715


def feed_forward_body(rows, x0, x1, wg, wu, wd, gate_ref, up_ref, hidden_ref, keep_ref, send_ref):
    for j, x_ref in enumerate((x0, x1)):
        at = slice(j * rows, (j + 1) * rows)
        x = x_ref[...]
        gate, up = nn(x, wg[...]), nn(x, wu[...])
        gate_ref[at, :] = gate
        up_ref[at, :] = up
        inner = jnp.tanh(GELU_A * (gate + GELU_B * (gate * gate * gate)))
        hidden_ref[at, :] = (0.5 * gate * (1.0 + inner) * up).astype(BF16)
        out = (keep_ref, send_ref)[j]
        out[...] = nn(hidden_ref[at, :], wd[...]).astype(out.dtype)


def feed_weights(inner_cols, outer_rows, which):
    fc = inner_cols.shape[1]
    return [
        (inner_cols, part((D, fc), 2 * which, 0)),
        (inner_cols, part((D, fc), 2 * which + 1, 0)),
        (outer_rows, part((fc, D), which, 0)),
    ]


def feed_forward(half, inner_cols, outer_rows, which, keep, name):
    rows, fc = half[0].shape[0], inner_cols.shape[1]
    return call(
        functools.partial(feed_forward_body, rows),
        plain(half) + feed_weights(inner_cols, outer_rows, which),
        [((2 * rows, fc), F32), ((2 * rows, fc), F32), ((2 * rows, fc), BF16), ((rows, D), keep), ((rows, D), BF16)],
        12 * rows * fc * D,
        name=name,
    )


def feed_back_body(rows, d0, d1, gate_ref, up_ref, wg, wu, wd, dgate_ref, dup_ref, keep_ref, send_ref):
    for j, d_ref in enumerate((d0, d1)):
        at = slice(j * rows, (j + 1) * rows)
        dh = nt(d_ref[...], wd[...])
        t, up = gate_ref[at, :], up_ref[at, :]
        square = t * t
        inner = jnp.tanh(GELU_A * t * (1.0 + GELU_B * square))
        slope = 0.5 * (1.0 + inner) + 0.5 * t * (1.0 - inner * inner) * (
            GELU_A * (1.0 + 3.0 * GELU_B * square)
        )
        dgate_ref[at, :] = (dh * up * slope).astype(BF16)
        dup_ref[at, :] = (dh * (0.5 * t * (1.0 + inner))).astype(BF16)
        out = (keep_ref, send_ref)[j]
        out[...] = (nt(dgate_ref[at, :], wg[...]) + nt(dup_ref[at, :], wu[...])).astype(out.dtype)


def feed_back(dz_half, gate, up, inner_cols, outer_rows, which, keep, name):
    rows, fc = gate.shape[0] // 2, inner_cols.shape[1]
    return call(
        functools.partial(feed_back_body, rows),
        list(dz_half) + [(gate, None), (up, None)] + feed_weights(inner_cols, outer_rows, which),
        [((2 * rows, fc), BF16), ((2 * rows, fc), BF16), ((rows, D), keep), ((rows, D), BF16)],
        12 * rows * fc * D,
        name=name,
    )


def feed_both_body(rows, x0, x1, d0, d1, wg, wu, wd, hidden_ref, keep_ref, send_ref, dgate_ref, dup_ref, *backs):
    for j, (x_ref, d_ref) in enumerate(((x0, d0), (x1, d1))):
        at = slice(j * rows, (j + 1) * rows)
        x = x_ref[...]
        t, up = nn(x, wg[...]), nn(x, wu[...])
        dh = nt(d_ref[...], wd[...])
        square = t * t
        inner = jnp.tanh(GELU_A * t * (1.0 + GELU_B * square))
        act = 0.5 * t * (1.0 + inner)
        slope = 0.5 * (1.0 + inner) + 0.5 * t * (1.0 - inner * inner) * (
            GELU_A * (1.0 + 3.0 * GELU_B * square)
        )
        hidden_ref[at, :] = (act * up).astype(BF16)
        dgate_ref[at, :] = (dh * up * slope).astype(BF16)
        dup_ref[at, :] = (dh * act).astype(BF16)
        out, back = (keep_ref, send_ref)[j], backs[j]
        back[...] = (nt(dgate_ref[at, :], wg[...]) + nt(dup_ref[at, :], wu[...])).astype(back.dtype)
        out[...] = nn(hidden_ref[at, :], wd[...]).astype(out.dtype)


def feed_both(half, dz_half, inner_cols, outer_rows, which, keep, name):
    rows, fc = half[0].shape[0], inner_cols.shape[1]
    wide, tall = ((2 * rows, fc), BF16), [((rows, D), keep), ((rows, D), BF16)]
    return call(
        functools.partial(feed_both_body, rows),
        plain(half) + list(dz_half) + feed_weights(inner_cols, outer_rows, which),
        [wide] + tall + [wide, wide] + tall,
        24 * rows * fc * D,
        name=name,
    )


def feed_weight_body(rows, packed, *refs):
    xs, dzs = refs[0:4], refs[4:8]
    dg, du, hid = refs[8:10], refs[10:12], refs[12:14]
    outs = refs[14:]
    gate = up = down = None
    for j in range(4):
        at = slice((j % 2) * rows, (j % 2 + 1) * rows)
        x = xs[j][...]
        a, b = tn(x, dg[j // 2][at, :]), tn(x, du[j // 2][at, :])
        c = tn(hid[j // 2][at, :], dzs[j][...])
        gate, up, down = (a, b, c) if j == 0 else (gate + a, up + b, down + c)
    fc = gate.shape[1]
    if not packed:
        outs[0][:D, :] = gate.astype(BF16)
        outs[0][D:, :] = up.astype(BF16)
        outs[1][...] = down.astype(BF16)
        return
    out = refs[-1]
    height = out.shape[1]
    for n, grad in enumerate((gate, up)):
        for k in range(2):
            out[2 * n + k, :, :fc] = grad[k * height : (k + 1) * height, :].astype(BF16)
    short = fc // 4
    for q in range(4):
        for g in range(D // 128):
            piece = down[q * short : (q + 1) * short, g * 128 : (g + 1) * 128].astype(BF16)
            r, c = g % 3 * short, fc + g // 3 * 128
            out[q, r : r + short, c : c + 128] = piece
    y = lax.axis_index("batch") % 2
    for i in range(2):
        outs[0][i] = out[2 * i + y]
        outs[1][i] = out[2 * i + 1 - y]


def feed_weight(xs, dzs, dgate, dup, hidden, packed, name):
    rows, fc = xs[0].shape[0], dgate[0].shape[1]
    return call(
        functools.partial(feed_weight_body, rows, packed),
        plain(xs) + list(dzs) + plain((*dgate, *dup, *hidden)),
        [((2, D // 2, fc + 256), BF16)] * 2 if packed else [((2 * D, fc), BF16), ((fc, D), BF16)],
        24 * rows * fc * D,
        [pltpu.VMEM((4, D // 2, fc + 256), BF16)] if packed else [],
        name,
    )


def send_some(mine):
    return [mine[0], seq_swap(mine[1], 1), seq_swap(mine[2], 2)]


def send_rest(got, *after):
    return [*got, seq_swap(tie(got[2], got[1], *after), 1)]


def send_blocks(mine):
    return send_rest(send_some(mine))


def place(scratch, refs, s):
    for j, ref in enumerate(refs):
        scratch[s ^ j] = ref[...] if j < 2 else ref[j - 2]


def hand_out(scratch, outs):
    outs[0][...] = scratch[0]
    outs[1][...] = scratch[1]
    outs[2][0] = scratch[2]
    outs[2][1] = scratch[3]


def sent_shapes(shape, dtype):
    return [(shape, dtype), (shape, dtype), ((2,) + shape, dtype)]


def head_pack_body(ar, gr, lines, attn_ref, gain_ref, inner_ref, *refs):
    outs, feed_outs, scratch, feed_scratch = refs[:3], refs[3:6], refs[6], refs[7]
    s = lax.axis_index("seq")
    width, ir = scratch.shape[2], inner_ref.shape[0]
    dc, room = D // 4, width - ar
    turned = attn_ref[...].T
    gains = jnp.concatenate([gain_ref[...], jnp.zeros((1, lines * room - gr), F32)], axis=1)
    for t in range(4):
        at = s ^ t
        scratch[at, :, ar:] = jnp.zeros((dc, room), BF16)
        scratch[at, :, :ar] = turned[t * dc : (t + 1) * dc, :].astype(BF16)
        for n in range(lines):
            scratch[at, n : n + 1, ar:] = gains[:, n * room : (n + 1) * room].astype(BF16)
        for q in range(4):
            low = (4 * q + t) * 128
            feed_scratch[at, :, q * 128 : (q + 1) * 128] = inner_ref[:, low : low + 128].astype(BF16)
    hand_out(scratch, outs)
    hand_out(feed_scratch, feed_outs)


def attn_unpack_body(ar, gr, lines, *refs):
    ins, (attn_ref, scratch) = refs[0:4], refs[4:]
    place(scratch, ins, lax.axis_index("seq"))
    dc, room = D // 4, scratch.shape[2] - ar
    pieces = []
    for k in range(4):
        attn_ref[:dc, k * ar : (k + 1) * ar] = scratch[k, :, :ar]
        pieces += [scratch[k, n : n + 1, ar : ar + min(room, gr - n * room)].astype(F32) for n in range(lines)]
    pieces.append(jnp.zeros((1, attn_ref.shape[1] - 4 * gr), F32))
    line = jnp.concatenate(pieces, axis=1)
    fill = jnp.zeros((attn_ref.shape[0] - dc - 1, line.shape[1]), F32)
    attn_ref[dc:, :] = jnp.concatenate([line, fill], axis=0).astype(BF16)


def feeds_unpack_body(*refs):
    ins, outer_ref, feed_ref, scratch = refs[0:4], refs[4], refs[5], refs[6]
    place(scratch, ins, lax.axis_index("seq"))
    ir, orow = scratch.shape[1], outer_ref.shape[0]
    for k in range(4):
        feed_ref[k * ir : (k + 1) * ir, :512] = scratch[k]
    for g in range(D // 128):
        r, c = g % 3 * orow, 512 + g // 3 * 128
        feed_ref[r : r + orow, c : c + 128] = outer_ref[:, g * 128 : (g + 1) * 128].astype(BF16)


def head_exchange(attn_master, inner_master, outer_master, gain_master):
    ar, dc, gr = attn_master.shape[0], D // 4, gain_master.shape[0]
    ir, fc = inner_master.shape[0], inner_master.shape[1] // 4
    width = (ar // 128 + 1) * 128
    lines = -(-gr // (width - ar))
    scratch, feed_scratch = pltpu.VMEM((4, dc, width), BF16), pltpu.VMEM((4, ir, fc), BF16)
    outs = call(
        functools.partial(head_pack_body, ar, gr, lines),
        plain([attn_master, gain_master[None], inner_master]),
        sent_shapes((dc, width), BF16) + sent_shapes((ir, fc), BF16),
        0,
        [scratch, feed_scratch],
        "head_pack",
    )
    attn = call(
        functools.partial(attn_unpack_body, ar, gr, lines),
        plain(send_blocks(outs[:3])),
        [((dc + 16, 4 * ar), BF16)],
        0,
        [scratch],
        "attn_unpack",
    )[0]
    feeds = call(
        feeds_unpack_body,
        plain(send_blocks([outs[3], tie(outs[4], attn), tie(outs[5], attn)]) + [outer_master]),
        [((4 * ir, D), BF16)],
        0,
        [feed_scratch],
        "feeds_unpack",
    )[0]
    return attn, feeds


def turn_pack_body(count, *refs):
    ins, outs, scratch = refs[:count], refs[count : count + 3], refs[count + 3]
    s = lax.axis_index("seq")
    dc = scratch.shape[2]
    for t in range(4):
        for g in range(count):
            scratch[s ^ t, g] = ins[g][:, t * dc : (t + 1) * dc].T
    hand_out(scratch, outs)


def turn_pack(ins, name):
    count, dc = len(ins), D // 4
    return call(
        functools.partial(turn_pack_body, count),
        ins,
        sent_shapes((count, dc, dc), BF16),
        0,
        [pltpu.VMEM((4, count, dc, dc), BF16)],
        name,
    )


def lanes_unpack_body(*refs):
    ins, out, scratch = refs[:4], refs[4], refs[5]
    place(scratch, ins, lax.axis_index("seq"))
    width = scratch.shape[3]
    for k in range(4):
        for g in range(scratch.shape[1]):
            out[g, :, k * width : (k + 1) * width] = scratch[k, g]


def lanes_unpack(got, name):
    shape = got[0].shape
    return call(
        lanes_unpack_body,
        plain(got),
        [(shape[:2] + (4 * shape[2],), BF16)],
        0,
        [pltpu.VMEM((4,) + shape, BF16)],
        name,
    )[0]


def tail_pack_body(gr, total_ref, *refs):
    outs, scratch = refs[:3], refs[3]
    s, width = lax.axis_index("seq"), scratch.shape[2]
    dc = D // 4
    for t in range(4):
        scratch[s ^ t, :dc] = total_ref[:dc, t * width : (t + 1) * width].astype(BF16)
        lines = [total_ref[dc + e : dc + e + 1, t * gr : (t + 1) * gr] for e in range(2)]
        lines = jnp.concatenate(lines + [jnp.zeros((1, width - 2 * gr), F32)] * (width > 2 * gr), axis=1)
        scratch[s ^ t, dc:] = jnp.concatenate([lines, jnp.zeros((15, width), F32)], axis=0).astype(BF16)
    hand_out(scratch, outs)


def tail_unpack_body(gr, *refs):
    ins, (out, kept_ref, sent_ref, scratch) = refs[:4], refs[4:]
    place(scratch, ins, lax.axis_index("seq"))
    dc = D // 4
    lines = None
    for k in range(4):
        out[:, k * dc : (k + 1) * dc] = scratch[k, :dc].astype(F32).T
        line = scratch[k, dc:].astype(F32)[:1]
        lines = line if k == 0 else lines + line
    halves = lines[:, :gr], lines[:, gr : 2 * gr]
    first = lax.axis_index("batch") % 2 == 0
    kept_ref[...] = jnp.where(first, halves[0], halves[1])
    sent_ref[...] = jnp.where(first, halves[1], halves[0])


def feed_pack_body(total_ref, *refs):
    outs, outer_ref, scratch = refs[:3], refs[3], refs[4]
    s, (rows, fc), orow = lax.axis_index("seq"), scratch.shape[1:], outer_ref.shape[0]
    for t in range(4):
        scratch[s ^ t] = total_ref[t * rows : (t + 1) * rows, :fc].astype(BF16)
    hand_out(scratch, outs)
    for g in range(D // 128):
        r, c = g % 3 * orow, fc + g // 3 * 128
        outer_ref[:, g * 128 : (g + 1) * 128] = total_ref[r : r + orow, c : c + 128]


def feed_pack(total, ir, fc, orow):
    outs = call(
        feed_pack_body,
        plain([total]),
        sent_shapes((ir, fc), BF16) + [((orow, D), F32)],
        0,
        [pltpu.VMEM((4, ir, fc), BF16)],
        "feed_pack",
    )
    return outs[:3], outs[3]


def feed_unpack_body(*refs):
    ins, out, scratch = refs[:4], refs[4], refs[5]
    place(scratch, ins, lax.axis_index("seq"))
    for k in range(4):
        for q in range(4):
            low = (4 * q + k) * 128
            out[:, low : low + 128] = scratch[k, :, q * 128 : (q + 1) * 128].astype(F32)


def feed_unpack(got):
    ir, fc = got[0].shape
    return call(
        feed_unpack_body, plain(got), [((ir, 4 * fc), F32)], 0, [pltpu.VMEM((4, ir, fc), BF16)], "feed_unpack"
    )[0]


def spread_body(*refs):
    out_ref = refs[6]
    count, width = out_ref.shape[0], out_ref.shape[2]
    per = 6 * D // count
    line = jnp.concatenate([x[...] for x in refs[:6]], axis=1)
    for n in range(count):
        piece = line[:, n * per : (n + 1) * per]
        out_ref[n] = jnp.concatenate([piece, jnp.zeros((1, width - per), F32)], axis=1)


def spread(rows, count, width):
    return call(spread_body, plain(rows), [((count, 1, width), F32)], 0, name="spread")[0]


def tail_pack(total, ar, gr):
    if ar % 16:
        return [total, total]
    shape = (D // 4 + 16, ar)
    mine = call(
        functools.partial(tail_pack_body, gr),
        plain([total]),
        sent_shapes(shape, BF16),
        0,
        [pltpu.VMEM((4,) + shape, BF16)],
        "tail_pack",
    )
    return send_some(mine) + [mine[1]]


def tail_unpack(mine, s, ar, gr, now, *after):
    dc = D // 4
    if ar % 16:
        got = seq_exchange(mine[0][:dc].astype(BF16).reshape(dc, 4, ar).swapaxes(0, 1), s)
        lines = lax.dynamic_slice_in_dim(sum_seq(mine[0][dc : dc + 2]), s * gr, gr, axis=1)
        y = lax.axis_index("batch") % 2
        pair = [lax.dynamic_slice_in_dim(lines, i, 1, axis=0) for i in (y, 1 - y)]
        return (got.reshape(4 * dc, ar).T.astype(F32), *pair)
    got = send_rest(mine[:3], *after)
    return call(
        functools.partial(tail_unpack_body, gr),
        plain([now(got[0]), *got[1:]]),
        [((ar, 4 * dc), F32), ((1, gr), F32), ((1, gr), F32)],
        0,
        [pltpu.VMEM((4, dc + 16, ar), BF16)],
        "tail_unpack",
    )


def split_lanes(scratch, pieces):
    width = scratch.shape[2]
    for n, piece in enumerate(pieces):
        for low in range(n * D, (n + 1) * D, D // 2):
            to = low % width
            scratch[low // width, :, to : to + D // 2] = piece[:, low - n * D : low - n * D + D // 2]


def part_pack_body(positions, *refs):
    count = len(positions)
    ins = refs[4 : 4 + 2 * count]
    kept_ref, sent_ref, squares, scratch = refs[4 + 2 * count :]
    y = lax.axis_index("batch") % 2
    place(squares, refs[:4], lax.axis_index("seq"))
    for n, position in enumerate(positions):
        pieces = [x[...] for x in ins[2 * n : 2 * n + 2]]
        pieces.insert(position, jnp.concatenate([squares[k, n] for k in range(4)], axis=1))
        split_lanes(scratch, pieces)
        kept_ref[n] = scratch[y]
        sent_ref[n] = scratch[1 - y]


def attn_parts(got, parts, width, name):
    dc = D // 4
    if width % 128 or lax.axis_size("batch") != 8:
        joined = []
        matrices = None if got is None else lanes_unpack(got, name)
        for n, (others, position) in enumerate(parts):
            pieces = list(others)
            if got is not None:
                pieces.insert(position, matrices[n])
            joined.append(jnp.concatenate(pieces, axis=1))
        joined = jnp.concatenate(joined, axis=1)
        return pair_blocks(joined.reshape(dc, -1, width).swapaxes(0, 1))
    return call(
        functools.partial(part_pack_body, [position for _, position in parts]),
        plain([*got, *(x for others, _ in parts for x in others)]),
        [((len(parts), dc, width), BF16)] * 2,
        0,
        [pltpu.VMEM((4, len(parts), dc, dc), BF16), pltpu.VMEM((2, dc, width), BF16)],
        name,
    )


def self_part_body(rows, *refs):
    x = refs[0:4]
    dq, dkt, dvt, kept_ref, sent_ref, scratch = refs[4:10]
    gq = gk = gv = None
    for j in range(4):
        at = slice(j * rows, (j + 1) * rows)
        y = x[j][...]
        a, b, c = tn(dq[at, :], y), nn(dkt[:, at], y), nn(dvt[:, at], y)
        gq, gk, gv = (a, b, c) if j == 0 else (gq + a, gk + b, gv + c)
    split_lanes(scratch, [g.astype(BF16) for g in (gq, gk, gv)])
    y = lax.axis_index("batch") % 2
    kept_ref[0] = scratch[y]
    sent_ref[0] = scratch[1 - y]


def self_part(rows, grads, width, name):
    dq, dkt, dvt = grads
    per, dc = dq.shape[0] // 4, dq.shape[1]
    if width % 128 or lax.axis_size("batch") != 8:
        gq, gk, gv = (g.reshape(4, per, dc) for g in (dq, dkt.T, dvt.T))
        made = [
            sum(tn(g[j], x.reshape(4, per, D)[j]) for j, (x, _) in enumerate(rows)).astype(BF16)
            for g in (gq, gk, gv)
        ]
        return attn_parts(None, [(made, 0)], width, name)
    return call(
        functools.partial(self_part_body, per),
        list(rows) + plain([dq, dkt, dvt]),
        [((1, dc, width), BF16)] * 2,
        0,
        [pltpu.VMEM((2, dc, width), BF16)],
        name,
    )


KINDS = ((D, 0), (D, 12), (FF, 16), (D, 18))


def group_mask(count, kind):
    per_group, offset = KINDS[kind]
    axis = 1 if kind < 3 else 0
    shape = (count, 128) if kind < 3 else (128, count)
    at = lax.axis_index(("batch", "seq")) * count + lax.broadcasted_iota(jnp.int32, shape, 1 - axis)
    low = (lax.broadcasted_iota(jnp.int32, shape, axis) - offset) * per_group
    return (at >= low) & (at < low + per_group) & (low >= 0)


def diagonal():
    return lax.broadcasted_iota(jnp.int32, (128, 128), 0) == lax.broadcasted_iota(jnp.int32, (128, 128), 1)


def by_group(values, kind):
    if kind == 3:
        mask = group_mask(values.shape[1], kind)
        column = jnp.sum(jnp.where(mask, values * values, 0.0), axis=1, keepdims=True)
        return jnp.sum(jnp.where(diagonal(), column, 0.0), axis=0, keepdims=True)
    squares = jnp.sum(values * values, axis=1, keepdims=True)
    return jnp.sum(jnp.where(group_mask(values.shape[0], kind), squares, 0.0), axis=0, keepdims=True)


def of_group(row, count, kind):
    if kind == 3:
        column = jnp.sum(jnp.where(diagonal(), row, 0.0), axis=1, keepdims=True)
        return jnp.sum(jnp.where(group_mask(count, kind), column, 0.0), axis=0, keepdims=True)
    return jnp.sum(jnp.where(group_mask(count, kind), row, 0.0), axis=1, keepdims=True)


def square_sums_body(*refs):
    total = by_group(refs[0][...], 0)
    for kind in range(1, 4):
        total = total + by_group(refs[kind][...], kind)
    refs[4][...] = total


def square_sums(masters):
    return call(square_sums_body, plain(masters), [((1, 128), F32)], 0, name="square_sums")[0]


def adam_body(kind, w_ref, m_ref, v_ref, g_ref, first_ref, second_ref, update_ref, sums_ref):
    gradient = g_ref[...]
    correction = 1.0 - 0.5**STEP
    first = 0.5 * m_ref[...] + 0.5 * gradient
    second = 0.5 * v_ref[...] + 0.5 * gradient * gradient
    update = first / correction / (jnp.sqrt(second / correction) + adam_eps)
    update = update + (decay_weight if kind < 3 else 0.0) * w_ref[...]
    first_ref[...] = first
    second_ref[...] = second
    update_ref[...] = update
    sums_ref[...] = by_group(update, kind)


def adam(kind, w, m, v, g):
    return call(
        functools.partial(adam_body, kind),
        plain([w, m, v, g]),
        [(w.shape, F32)] * 3 + [((1, 128), F32)],
        0,
        name=f"adam_{kind}",
    )


def gain_body(kept_ref, got_ref, w_ref, m_ref, v_ref, weights_ref, s0, s1, s2, grad_ref, *outs):
    grad_ref[...] = kept_ref[...] + got_ref[...]
    first_ref, second_ref, update_ref, sums_ref = *outs[:3], outs[4]
    adam_body(3, w_ref, m_ref, v_ref, grad_ref, first_ref, second_ref, update_ref, sums_ref)
    outs[3][:, :128] = weights_ref[...]
    outs[3][:, 128:] = sums_ref[...] + s0[...] + s1[...] + s2[...]


def gain_adam(kept, got, w, m, v, weight_sums, sums):
    return call(
        gain_body,
        plain([kept, got, w, m, v, weight_sums, *sums]),
        [(w.shape, F32)] * 4 + [((1, 256), F32)],
        0,
        [pltpu.VMEM((1, 128), F32)],
        "adam_3",
    )


def lamb_body(*refs):
    weight_norms, update_norms = jnp.sqrt(refs[0][:, :128]), jnp.sqrt(refs[0][:, 128:])
    ratio = weight_norms / (update_norms + 1e-06)
    masters, updates, news, copies = (refs[1 + 4 * n : 5 + 4 * n] for n in range(4))
    for kind in range(4):
        w = masters[kind]
        scale = of_group(ratio, w.shape[1] if kind == 3 else w.shape[0], kind)
        new = w[...] - lamb_rate * scale * updates[kind][...]
        if kind == 3:
            new = new[0]
        news[kind][...] = new
        copies[kind][...] = new.astype(BF16)
    refs[17][...] = weight_norms[0, :24]
    refs[18][...] = update_norms[0, :24]


def lamb(squares, masters, updates):
    shapes = [w.shape for w in masters[:3]] + [masters[3].shape[1:]]
    return call(
        lamb_body,
        plain([squares, *masters, *updates]),
        [(s, F32) for s in shapes] + [(s, BF16) for s in shapes] + [((24,), F32)] * 2,
        0,
        name="lamb",
    )


def per_device(
    encoder_layer_input,
    decoder_layer_input,
    cotangent,
    encoder_used_lengths,
    decoder_used_lengths,
    attn_master,
    inner_master,
    outer_master,
    gain_master,
    attn_first,
    inner_first,
    outer_first,
    gain_first,
    attn_second,
    inner_second,
    outer_second,
    gain_second,
):
    ns, nb = lax.axis_size("seq"), lax.axis_size("batch")
    s, b = lax.axis_index("seq"), lax.axis_index("batch")
    ar, ir, orow = attn_master.shape[0], inner_master.shape[0], outer_master.shape[0]
    dc, fc = D // ns, FF // ns
    cuts = FF // (ns * orow)

    gr = gain_master.shape[0]
    packed = nb == 8 and ar % 16 == 0 and 3 * orow == ns * ir and cuts == 4
    clock = Clock()
    now, mark = clock.now, clock.mark
    masters = [attn_master, inner_master, outer_master, gain_master[None]]
    if packed:
        attn_mine, feed_mine = head_exchange(attn_master, inner_master, outer_master, gain_master)
        feeds_mine = [feed_mine]
    else:
        width = (ar // 128 + 1) * 128
        lines = -(-gr // (width - ar))
        corner = jnp.pad(gain_master.astype(BF16), (0, lines * (width - ar) - gr)).reshape(lines, width - ar)
        corner = jnp.broadcast_to(jnp.pad(corner, ((0, dc - lines), (0, 0))), (ns, dc, width - ar))
        attn_low = attn_master.astype(BF16).T.reshape(ns, dc, ar)
        got = seq_exchange(jnp.concatenate([attn_low, corner], axis=2), s)
        attn_mine = got[:, :, :ar].swapaxes(0, 1).reshape(dc, ns * ar)
        gains_mine = got[:, :lines, ar:].reshape(ns, -1)[:, :gr].reshape(1, ns * gr)
        attn_mine = jnp.concatenate([attn_mine, jnp.pad(gains_mine, ((0, 15), (0, ns * (ar - gr))))])
        inner_low = inner_master.astype(BF16).reshape(ir, cuts, ns, orow).transpose(2, 0, 1, 3)
        inner_mine = seq_exchange(inner_low.reshape(ns, ir, fc), s).reshape(ns * ir, fc)
        feeds_mine = [inner_mine, outer_master.astype(BF16)]
    attn_got = None
    attn_ring = ring_gather(attn_mine)
    next(attn_ring)
    while not isinstance(attn_got, list):
        attn_last, attn_got = attn_got, attn_ring.send(None)
    squares = square_sums(masters)
    attn_t = gathered_lanes([attn_got[0], *(tie(x, squares) for x in attn_got[1:])], "gather_attn")
    feed_rings = [ring_gather(x) for x in feeds_mine]
    for x in feed_rings:
        next(x)
        x.send(attn_last)

    def feed_step():
        for x in feed_rings:
            clock.step(x)

    gains = attn_t[dc].reshape(nb, ns * ar)[:, : ns * gr].reshape(6, D).astype(F32)
    gain = [gains[i : i + 1] for i in range(6)]
    out_mine = turn_pack([(attn_t, part((dc, D), 0, 4 * g + 3)) for g in range(3)], "out_pack")
    out_got = send_some(out_mine)

    enc_in, dec_in = encoder_layer_input[0], decoder_layer_input[0]
    er, dr = enc_in.shape[0], dec_in.shape[0]
    enc_meta = jnp.stack([s, encoder_used_lengths[0]]).astype(jnp.int32)
    dec_meta = jnp.stack([s, decoder_used_lengths[0]]).astype(jnp.int32)
    alive = (s * dr + jnp.arange(dr, dtype=jnp.int32)) < decoder_used_lengths[0]
    seed = jnp.where(alive[:, None], cotangent[0], jnp.zeros_like(cotangent[0]))
    blocks = gather_blocks(jnp.concatenate([enc_in, dec_in, seed]))
    enc_blocks = [(x, part((er, D), 0, 0)) for x in blocks]
    dec_blocks = [(x, part((dr, D), er // dr, 0)) for x in blocks]
    seed_blocks = [(x, part((dr, D), er // dr + 1, 0)) for x in blocks]

    def quarters(rows):
        return [(rows, part((rows.shape[0] // 4, D), j, 0)) for j in range(4)]

    mark(out_mine[1])
    feed_step()
    rows_a, q0, k0, v0, logs_far0, mixed_far0 = attend_far(
        now(enc_meta), enc_blocks, None, attn_t, None, 0, False, gain[0]
    )
    mark(mixed_far0)
    logs_near0, mixed_near0 = attend_near(enc_meta, now(q0), k0, v0, None, 0, False)
    mark([mixed_near0, out_got[2]])
    feed_step()
    out_w = lanes_unpack(send_rest([now(out_got[0]), *out_got[1:]], mixed_near0), "out_unpack")
    kf, sf = project(mixed_far0, (out_w, 0), BF16, "project_far_0")
    mark(sf)
    kn_enc, sn = project(now(mixed_near0), (out_w, 0), F32, "project_near_0")
    mark(sn)
    far = mark(add_low(now(kf), seq_swap(sf, 1)))
    x_enc, c_enc = seq_swap(far, 2), seq_swap(sn, 1)
    rows_c, q1, k1, v1, logs_far1, mixed_far1, kf, sf = attend_far(
        now(dec_meta), dec_blocks, None, attn_t, (out_w, 1), 1, True, gain[3]
    )
    mark(sf)
    feed_step()
    enc_mid, norm_b = close(now(kn_enc), c_enc, x_enc, enc_in, gain[1], "close_enc_attn")
    mark(norm_b)
    rows_b = gather_blocks(norm_b)
    x_self = seq_swap(mark(far_payload(kf, now(sf))), 2)
    logs_near1, mixed_near1, kn, sn = attend_near(dec_meta, now(q1), k1, v1, (out_w, 1), 1, True)
    mark(sn)
    c_self = seq_swap(sn, 1)
    feed_got = [clock.finish(x) for x in feed_rings]
    feed_got = [[now(got[0]), *got[1:]] for got in feed_got]
    if packed:
        inner_cols, outer_rows = gathered_feeds(feed_got[0], orow, "gather_feeds")
    else:
        inner_cols = gathered_rows(feed_got[0], "gather_inner")
        outer_rows = gathered_rows(feed_got[1], "gather_outer")
    inner_cols, outer_rows = inner_cols.reshape(4 * D, fc), outer_rows.reshape(2 * fc, D)
    eg1, eu1, eh1, kf, sf = feed_forward((now(rows_b[2]), rows_b[3]), inner_cols, outer_rows, 0, BF16, "enc_feed_far")
    far = mark(far_payload(kf, sf))
    x_enc = seq_swap(far, 2)
    eg0, eu0, eh0, kn_enc, sn = feed_forward((now(rows_b[0]), rows_b[1]), inner_cols, outer_rows, 0, F32, "enc_feed_near")
    mark(sn)
    c_enc = seq_swap(sn, 1)
    dec_mid, norm_d = close(now(kn), c_self, x_self, dec_in, gain[4], "close_self")
    mark(norm_d)
    rows_d = gather_blocks(norm_d)
    enc_out, norm_e = close(now(kn_enc), c_enc, x_enc, enc_mid, gain[2], "close_enc_feed")
    mark(norm_e)
    rows_e = gather_blocks(norm_e)
    mark([norm_e, rows_d[2]])
    q0t, q1t = now(q0).T, now(q1).T
    mark(q1t)
    q2, k2, v2, logs_far2, mixed_far2, kf, sf = attend_far(
        now(enc_meta), plain(rows_d), plain(rows_e), attn_t, (out_w, 2), 2, False
    )
    far = mark(far_payload(kf, sf))
    x_dec = seq_swap(far, 2)
    logs_near2, mixed_near2, kn, sn = attend_near(enc_meta, now(q2), k2, v2, (out_w, 2), 2, False)
    mark(sn)
    dec_late, norm_f = close(now(kn), seq_swap(tie(sn, x_dec), 1), x_dec, dec_mid, gain[5], "close_cross")
    mark(norm_f)
    rows_f = gather_blocks(norm_f)
    dh0, kn_out, sn_out, a0, b0, kn_dec, sn_dec = feed_both(
        (now(rows_f[0]), rows_f[1]), seed_blocks[:2], inner_cols, outer_rows, 1, F32, "dec_feed_near"
    )
    mark(sn_dec)
    c_dec = seq_swap(sn_dec, 1)
    dh1, kf_out, sf_out, a1, b1, kf, sf = feed_both(
        (now(rows_f[2]), rows_f[3]), seed_blocks[2:], inner_cols, outer_rows, 1, BF16, "dec_feed_far"
    )

    far = mark(far_payload(kf, sf))
    x_dec = seq_swap(far, 2)
    dec_feed = feed_weight(
        rows_f, seed_blocks, (now(a0), a1), (b0, b1), (dh0, dh1), packed, "dec_feed_weight"
    )
    mark(dec_feed[-1])
    up_five, low, gain_five = close_back(now(kn_dec), c_dec, x_dec, dec_late, gain[5], seed, "back_dec_feed")
    mark(low)
    dz_cross = plain(gather_blocks(low))
    half = nb // 2
    feed_shapes = [(ns * ir, fc), (orow, D)]

    def pair_send(kept, sent):
        return kept, batch_swap(mark(sent), 1)

    def feed_parts(grads):
        if packed:
            return [pair_send(*grads)]
        blocks = [now(x).reshape((half,) + shape) for x, shape in zip(grads, feed_shapes)]
        return [pair_send(*pair_blocks(x)) for x in blocks]

    dec_parts = feed_parts(dec_feed)
    far_out = mark(far_payload(kf_out, sf_out))

    q2t = mark(now(q2).T)
    out_sent = out_weight([(dz_cross, now(mixed_near2), mixed_far2)], "cross_out_weight")
    mark(out_sent[1])
    out_got = send_blocks(out_sent)
    x_out = seq_swap(tie(far_out, out_sent[1]), 2)
    c_out = seq_swap(tie(sn_out, out_sent[1]), 1)
    decoder_layer_output = (dec_late + kn_out + c_out.astype(F32) + x_out.astype(F32)).astype(BF16)
    cross_d, outs = attend_back(
        now(enc_meta), dz_cross, q2t, attn_t, (out_w, 2), 2, (q2, k2, v2, logs_near2, logs_far2), dr, er, False, True
    )
    far = mark(far_payload(outs[6], tie(outs[7], x_out, c_out, out_got[2])))
    x_enc, c_enc = seq_swap(far, 2), seq_swap(now(outs[5]), 1)
    c_far, c_dec = seq_swap(now(outs[3]), 1), seq_swap(now(outs[1]), 1)
    kf_dec, kn_dec = outs[2], outs[0]
    cross_w = attend_weights(plain(rows_d), plain(rows_e), (now(cross_d[0]), *cross_d[1:]), "cross_weights")
    mark(cross_w[0])
    three = attn_parts([now(out_got[0]), *out_got[1:]], [(cross_w[1:], 2)], ns * ar, "part_three")
    mark(three[1])
    up_two, low, gain_two = close_back(now(outs[4]), c_enc, x_enc, enc_out, gain[2], None, "back_encoded")
    mark(low)
    dz = gather_blocks(low)
    far_dec = mark(add_low(kf_dec, now(c_far)))
    part_three = (three[0], batch_swap(three[1], 1))
    mark([far_dec] + [got for _, got in dec_parts])
    a0, b0, kn_enc, sn = feed_back(plain(dz[:2]), now(eg0), eu0, inner_cols, outer_rows, 0, F32, "enc_feed_back_near")
    mark(sn)
    c_enc = seq_swap(sn, 1)
    x_dec = seq_swap(tie(far_dec, dz[2], sn), 2)
    mark([sn, part_three[1]])
    dz = plain(dz)
    a1, b1, kf, sf = feed_back(dz[2:], now(eg1), eu1, inner_cols, outer_rows, 0, BF16, "enc_feed_back_far")
    far = mark(far_payload(kf, tie(sf, x_dec)))
    x_enc = seq_swap(far, 2)
    enc_feed = feed_weight(
        rows_b, dz, (now(a0), a1), (b0, b1), (eh0, eh1), packed, "enc_feed_weight"
    )
    mark(enc_feed[-1])
    enc_parts = feed_parts(enc_feed)
    up_four, low_self, gain_four = close_back(now(kn_dec), c_dec, x_dec, dec_mid, gain[4], up_five, "back_cross")
    mark(low_self)
    dz_self = plain(gather_blocks(low_self))
    up_one, low, gain_one = close_back(now(kn_enc), c_enc, x_enc, enc_mid, gain[1], up_two, "back_enc_feed")
    mark(low)
    dz_enc = gather_blocks(low)
    self_d, outs = attend_back(
        now(dec_meta), dz_self, q1t, attn_t, (out_w, 1), 1, (q1, k1, v1, logs_near1, logs_far1), dr, dr, True, False
    )
    mark(outs[3])
    self_w = attend_weights(quarters(rows_c), None, (now(self_d[0]), *self_d[1:]), "self_weights")
    mark(self_w[0])
    flight = []
    feeds = [ring_reduce([e, d], "feed_hop", None, flight) for e, d in zip(enc_parts, dec_parts)]
    for x in feeds:
        next(x)
    kn_self, c_self = outs[0], seq_swap(tie(outs[1], dz_enc[2]), 1)
    sf_self = seq_swap(tie(outs[3], dz_enc[2]), 1)
    dz_enc = plain(dz_enc)
    out_late = out_weight(
        [(dz_enc, now(mixed_near0), mixed_far0), (dz_self, mixed_near1, mixed_far1)], "late_out_weight"
    )
    mark(out_late[1])
    got_late = send_blocks(out_late)
    x_self = seq_swap(mark(add_low(outs[2], now(sf_self))), 2)
    for x in feeds:
        clock.step(x)
    enc_d, outs = attend_back(
        now(enc_meta), dz_enc, q0t, attn_t, (out_w, 0), 0, (q0, k0, v0, logs_near0, logs_far0), er, er, False, False
    )
    mark([outs[3], x_self, got_late[2], *flight])
    c_far, c_enc = seq_swap(outs[3], 1), seq_swap(now(outs[1]), 1)
    part_zero = pair_send(
        *self_part(quarters(rows_a), (now(enc_d[0]), *enc_d[1:]), ns * ar, "part_zero")
    )
    for x in feeds:
        clock.step(x)
    part_middle = pair_send(
        *attn_parts(
            [now(got_late[0]), *got_late[1:]],
            [(self_w[:2], 0), ((self_w[2], cross_w[0]), 1)],
            ns * ar,
            "part_middle",
        )
    )
    far = mark(add_low(now(outs[2]), c_far))
    x_enc = seq_swap(far, 2)
    decoder_input_gradient, _, gain_three = close_back(
        now(kn_self), c_self, x_self, dec_in, gain[3], up_four, "back_self"
    )
    mark(gain_three)
    for x in feeds:
        clock.step(x)
    encoder_input_gradient, _, gain_zero = close_back(
        now(outs[0]), c_enc, x_enc, enc_in, gain[0], up_one, "back_enc_attn"
    )
    mark(gain_zero)

    gain_lines = spread(
        [now(gain_zero), gain_one, gain_two, gain_three, gain_four, gain_five], nb, ns * ar
    )
    mark(gain_lines)
    last_ring = ring_reduce([part_zero, part_middle, part_three], "attn_hop", gain_lines)
    next(last_ring)
    clock.step(last_ring)
    feeds_done = [clock.finish(x)[0] for x in feeds]
    if packed:
        feed_sent, outer_grad = feed_pack(mark(feeds_done[0]), ir, fc, orow)
        mark(feed_sent[1])
        feed_got = send_some(feed_sent)
    else:
        inner_part, outer_grad = feeds_done
        inner_part = mark(now(inner_part).astype(BF16).reshape(ns, ir, fc))
        inner_part = seq_exchange(inner_part, s)
    clock.step(last_ring)
    outer_new = adam(2, outer_master, outer_first, outer_second, now(outer_grad))
    mark(outer_new[3])
    clock.step(last_ring)
    if not packed:
        inner_grad = inner_part.reshape(ns, ir, cuts, orow).transpose(1, 2, 0, 3).reshape(ir, FF).astype(F32)
    (attn_sum,) = clock.finish(last_ring)
    mine = tail_pack(mark(attn_sum), ar, gr)
    mark(mine[-1])
    if packed:
        inner_grad = feed_unpack(send_rest([now(feed_got[0]), *feed_got[1:]]))
    inner_new = adam(1, inner_master, inner_first, inner_second, now(inner_grad))
    mark(inner_new[3])
    attn_grad, gain_kept, gain_sent = tail_unpack(mine, s, ar, gr, now, clock.last)
    gain_got = batch_swap(gain_sent, 1)
    attn_new = adam(0, attn_master, attn_first, attn_second, attn_grad)
    others = (attn_new, inner_new, outer_new)
    gain_grad, *gain_new, own_squares = gain_adam(
        gain_kept, tie(gain_got, attn_new[3]), masters[3], gain_first[None], gain_second[None], squares, [x[3] for x in others]
    )
    results = (*others, gain_new)
    all_squares = sum_all(own_squares)
    last = lamb(all_squares, masters, [x[2] for x in results])
    grads = (attn_grad, inner_grad, outer_grad, gain_grad)

    def flat(four):
        return (*four[:3], four[3][0])

    return (
        decoder_layer_output[None],
        encoder_input_gradient[None],
        decoder_input_gradient[None],
        *flat(grads),
        *flat([x[0] for x in results]),
        *flat([x[1] for x in results]),
        *last,
    )


def solution(mesh):
    rows = P("batch", "seq", None)
    matrix = P(("batch", "seq"), None)
    vector = P(("batch", "seq"))
    kinds = (matrix, matrix, matrix, vector)
    return jax.shard_map(
        per_device,
        mesh=mesh,
        in_specs=(rows, rows, rows, P("batch"), P("batch")) + kinds * 3,
        out_specs=(rows, rows, rows) + kinds * 5 + (P(), P()),
        check_vma=False,
    )
```
